32 devices in a mesh: expert: 16 (over z, y, x), seq: 2 (over core).
Axes of the slice: x: 2, y: 2, z: 4, core: 2. Of those that a mesh axis runs over, the one named last changes fastest.
Arguments:
- out_grad: bfloat16 [4096, 7168], P(('expert', 'seq')), may hold values from -6 to 6
- route_ids: int32 [4096, 8], P('expert'), may hold values from 0 to 255, all different within a row
- route_weights: float32 [4096, 8], P('expert'), may hold values from 0.2 to 1
- gate_pre: bfloat16 [16, 192, 1024], P('expert', None, 'seq'), may hold values from -5 to 5
- up_pre: bfloat16 [16, 192, 1024], P('expert', None, 'seq'), may hold values from -5 to 5
- w_gate: bfloat16 [16, 7168, 1024], P('expert', None, 'seq'), may hold values from -0.75 to 0.75
- w_up: bfloat16 [16, 7168, 1024], P('expert', None, 'seq'), may hold values from -0.75 to 0.75
- w_down: bfloat16 [16, 1024, 7168], P('expert', 'seq'), may hold values from -0.0078125 to 0.0078125
Outputs:
- in_grad: bfloat16 [4096, 7168], P(('expert', 'seq'))
- weight_grad: bfloat16 [4096, 8], P(('expert', 'seq'))
The draws below stay inside these ranges and needn't reach their ends.
Inputs may be any that keep to these rules, and one draw needn't show every extreme that they name: `route_ids`: each row names 8 different experts; only experts below 16 are held in this window, the others are left to other windows.
All inputs are finite; a program needn't handle non-finite values.
Results may differ from the reference program's by a relative error of at most 0.0065.
Values may be sent and summed in bfloat16 or wider, within the bound.
A program may use at most 192 MiB of HBM per device.

```python
import jax
import jax.numpy as jnp
from jax import lax

D = 7168
ROUTED = 256
TOPK = 8
FF = 1024
TOK_DEV = 128
EXPERTS = 16
TOKENS = 4096
CAP = 12
SLOTS = 192
N_EXPERT = 16
N_SEQ = 2


def block_scale(rng, shape, split, low, top_value):
    def one(dim, shards_of):
        steps = jax.random.uniform(jax.random.fold_in(jax.random.fold_in(rng, 6), dim), (shards_of,), jnp.float32, low / len(split), top_value / len(split))
        return jnp.repeat(jnp.exp(steps), shape[dim] // shards_of).reshape((-1,) + (1,) * (len(shape) - dim - 1))

    factor_of = one(*split[0])
    for cut in split[1:]:
        factor_of = factor_of * one(*cut)
    return factor_of


def choose_distinct(rng, rows, amount, top, lift):
    order = jax.random.permutation(jax.random.fold_in(rng, 1), amount)
    pull = order
    for power in range(3):
        pull = pull * pull // amount
    pull = pull * lift // amount
    lots = jax.random.randint(jax.random.fold_in(rng, 2), (rows, amount), 0, 4096) + pull
    sure = jax.random.permutation(jax.random.fold_in(rng, 3), rows)[jnp.arange(amount) % rows]
    lots = jnp.where(jnp.arange(rows)[:, None] == sure[None, :], 1 << 14, lots)
    priority = lots * amount + jnp.arange(amount)
    return lax.top_k(priority.astype(jnp.int32), top)[1].astype(jnp.int32)


def centred(key, dims, spread, reach, shards=(), kind=jnp.bfloat16):
    result = jax.random.normal(key, dims, jnp.float32) * spread
    if len(shards) > 0:
        result = block_scale(key, dims, shards, -0.22, 0.18) * result
    return jnp.clip(result, min=-reach, max=reach).astype(kind)


def setup_inputs(seed: int = 0) -> dict:
    splits = jax.random.split(jax.random.key(seed), 9)
    return {
        "out_grad": centred(splits[0], (TOKENS, D), 1.0, 6.0, ((0, 32),)),
        "route_ids": choose_distinct(splits[1], TOKENS, ROUTED, TOPK, 512),
        "route_weights": jnp.clip(0.2 + 0.8 * jax.random.uniform(splits[2], (TOKENS, TOPK), jnp.float32) ** block_scale(splits[2], (TOKENS, TOPK), ((0, 16),), -0.2, 0.2), 0.2, 1.0),
        "gate_pre": centred(splits[3], (EXPERTS, SLOTS, FF), 1.0, 5.0, ((0, 16), (2, 2))),
        "up_pre": centred(splits[4], (EXPERTS, SLOTS, FF), 1.0, 5.0, ((0, 16), (2, 2))),
        "w_gate": centred(splits[5], (EXPERTS, D, FF), (FF // 16) ** -0.5, 0.75, ((0, 16), (2, 2))),
        "w_up": centred(splits[6], (EXPERTS, D, FF), (FF // 16) ** -0.5, 0.75, ((0, 16), (2, 2))),
        "w_down": centred(splits[7], (EXPERTS, FF, D), (D * 64) ** -0.5, 0.0078125, ((0, 16), (1, 2))),
    }


def silu_parts(value):
    sigma = jax.nn.sigmoid(value)
    return value * sigma, sigma * (1.0 + value * (1.0 - sigma))


def pair_tables(group_ids):
    pair_count = group_ids.shape[0]
    fanout = group_ids.shape[1]
    assigned = group_ids.reshape(-1).astype(jnp.int32)
    one_hot = (assigned[:, None] == jnp.arange(EXPERTS, dtype=jnp.int32)[None, :]).astype(jnp.int32)
    earlier = jnp.cumsum(one_hot, axis=0) - one_hot
    position = jnp.sum(earlier * one_hot, axis=1).astype(jnp.int32)
    retained = (assigned < EXPERTS) & (position < CAP)
    slot_index = jnp.where(retained, assigned * CAP + position, EXPERTS * CAP).astype(jnp.int32)
    owner_row = (jnp.arange(assigned.shape[0], dtype=jnp.int32) // fanout).astype(jnp.int32)
    slot_rows = jnp.full((EXPERTS * CAP + 1,), pair_count, jnp.int32).at[slot_index].set(owner_row)
    return slot_index.reshape(pair_count, fanout), slot_rows[:EXPERTS * CAP].reshape(EXPERTS, CAP)


def reference(out_grad, route_ids, route_weights, gate_pre, up_pre, w_gate, w_up, w_down):
    pair_count = TOK_DEV * N_SEQ
    half_width = FF // N_SEQ
    grouped = route_ids.reshape(N_EXPERT, pair_count, TOPK)
    slot_index, slot_rows = jax.vmap(pair_tables)(grouped)
    offsets = (jnp.arange(N_EXPERT, dtype=jnp.int32) * pair_count)[:, None, None]
    global_rows = jnp.where(slot_rows == pair_count, TOKENS, slot_rows + offsets).astype(jnp.int32)
    expert_rows = jnp.transpose(global_rows, (1, 0, 2)).reshape(EXPERTS, SLOTS)
    padded_grad = jnp.concatenate([out_grad, jnp.zeros((1, D), jnp.bfloat16)], axis=0)

    def expert_work(inputs):
        rows, gate_val, up_val, gate_w, up_w, down_w = inputs
        slot_grad = padded_grad[rows]
        input_sum = jnp.zeros((SLOTS, D), jnp.float32)
        score_sum = jnp.zeros((SLOTS,), jnp.float32)
        for half_at in range(N_SEQ):
            lower = half_at * half_width
            upper = lower + half_width
            hidden_grad = jnp.dot(slot_grad, down_w[lower:upper].T, preferred_element_type=jnp.float32)
            active, slope_val = silu_parts(gate_val[:, lower:upper].astype(jnp.float32))
            up_part = up_val[:, lower:upper].astype(jnp.float32)
            score_part = jnp.sum(hidden_grad * active * up_part, axis=1)
            gate_diff = (hidden_grad * up_part * slope_val).astype(jnp.bfloat16)
            up_diff = (hidden_grad * active).astype(jnp.bfloat16)
            input_part = jnp.dot(gate_diff, gate_w[:, lower:upper].T, preferred_element_type=jnp.float32)
            input_part = input_part + jnp.dot(up_diff, up_w[:, lower:upper].T, preferred_element_type=jnp.float32)
            input_round = lax.optimization_barrier(input_part.astype(jnp.bfloat16))
            score_round = lax.optimization_barrier(score_part.astype(jnp.bfloat16))
            input_sum = input_sum + input_round.astype(jnp.float32)
            score_sum = score_sum + score_round.astype(jnp.float32)
        return input_sum.astype(jnp.bfloat16), score_sum.astype(jnp.bfloat16)

    slot_input, slot_score = lax.map(expert_work, (expert_rows, gate_pre, up_pre, w_gate, w_up, w_down))
    expert_of = slot_index // CAP
    place = slot_index % CAP
    group_of = jnp.arange(N_EXPERT, dtype=jnp.int32)[:, None, None]
    global_slot = jnp.where(slot_index == EXPERTS * CAP, EXPERTS * SLOTS, expert_of * SLOTS + group_of * CAP + place)
    global_slot = global_slot.astype(jnp.int32).reshape(TOKENS, TOPK)
    flat_input = jnp.concatenate([slot_input.reshape(EXPERTS * SLOTS, D), jnp.zeros((1, D), jnp.bfloat16)], axis=0)
    flat_score = jnp.concatenate([slot_score.reshape(EXPERTS * SLOTS), jnp.zeros((1,), jnp.bfloat16)], axis=0)
    in_grad = jnp.zeros((TOKENS, D), jnp.float32)
    for column in range(TOPK):
        in_grad = in_grad + route_weights[:, column:column + 1] * flat_input[global_slot[:, column]].astype(jnp.float32)
    return in_grad.astype(jnp.bfloat16), flat_score[global_slot]
```

```python
import functools

import jax
import jax.numpy as jnp
from jax import lax
from jax.experimental import pallas as pl
from jax.experimental.pallas import tpu as pltpu
from jax.sharding import PartitionSpec as P

BF = jnp.bfloat16
F32 = jnp.float32
NT = (((1,), (1,)), ((), ()))
NN = (((1,), (0,)), ((), ()))
TN = (((0,), (0,)), ((), ()))


def silu_parts(value):
    sigma = jax.nn.sigmoid(value)
    return (value * sigma, sigma * (1.0 + value * (1.0 - sigma)))


def dot(a, b, dims):
    return lax.dot_general(a, b, dims, preferred_element_type=F32)


def swap(value):
    return lax.ppermute(value, "seq", [(0, 1), (1, 0)])


def ordered(mine, theirs, seq_at, axis):
    low = jnp.where(seq_at == 0, mine, theirs)
    high = jnp.where(seq_at == 0, theirs, mine)
    return jnp.concatenate([low, high], axis=axis)


def routing(ids, weights, experts, capacity):
    tokens = ids.shape[0]
    same = ids[:, :, None] == jnp.arange(experts, dtype=jnp.int32)
    hit = jnp.any(same, axis=1)
    weight = jnp.sum(jnp.where(same, weights[:, :, None], 0.0), axis=1)
    row = jnp.arange(tokens, dtype=jnp.int32)
    earlier = (row[None, :] < row[:, None]).astype(BF)
    position = dot(earlier, hit.astype(BF), NN)
    slot = jnp.where(hit, position, float(capacity))
    return slot, weight


def on_device_xla(out_grad, route_ids, route_weights, gate_pre, up_pre, w_gate, w_up, w_down):
    n_expert = lax.axis_size("expert")
    seq_at = lax.axis_index("seq")
    own, width = out_grad.shape
    half = width // 2
    experts = n_expert
    slots = gate_pre.shape[1]
    capacity = slots // n_expert
    slot, weight = routing(route_ids, route_weights, experts, capacity)
    table = (slot[:, :, None] == jnp.arange(capacity, dtype=F32)).reshape(2 * own, slots)
    w_all = jnp.broadcast_to(weight[:, :, None], (2 * own, experts, capacity)).reshape(2 * own, slots)
    w_all = jnp.where(table, w_all, 0.0)
    w_hi = w_all.astype(BF)
    w_lo = (w_all - w_hi.astype(F32)).astype(BF)
    mine = lax.dynamic_slice_in_dim(out_grad, seq_at * half, half, 1)
    other = lax.dynamic_slice_in_dim(out_grad, (1 - seq_at) * half, half, 1)
    tokens = ordered(mine, swap(other), seq_at, 0)
    outgoing = dot(table.astype(BF), tokens, TN).astype(BF).reshape(experts, capacity, half)
    received = lax.all_to_all(outgoing, "expert", split_axis=0, concat_axis=0, tiled=True)
    received = received.reshape(slots, half)
    slot_grad = ordered(received, swap(received), seq_at, 1)
    hidden_grad = dot(slot_grad, w_down[0], NT)
    active, slope = silu_parts(gate_pre[0].astype(F32))
    up_part = up_pre[0].astype(F32)
    score = jnp.sum(hidden_grad * active * up_part, axis=1).astype(BF)
    gate_diff = (hidden_grad * up_part * slope).astype(BF)
    up_diff = (hidden_grad * active).astype(BF)
    part = (dot(gate_diff, w_gate[0], NT) + dot(up_diff, w_up[0], NT)).astype(BF)
    score = lax.optimization_barrier(score)
    part = lax.optimization_barrier(part)
    keep = lax.dynamic_slice_in_dim(part, seq_at * half, half, 1)
    give = lax.dynamic_slice_in_dim(part, (1 - seq_at) * half, half, 1)
    total = (keep.astype(F32) + swap(give).astype(F32)).astype(BF)
    total_score = (score.astype(F32) + swap(score).astype(F32)).astype(BF)
    back = lax.all_to_all(
        total.reshape(n_expert, capacity, half), "expert", split_axis=0, concat_axis=0, tiled=True
    ).reshape(slots, half)
    back_score = lax.all_to_all(
        total_score.reshape(n_expert, capacity), "expert", split_axis=0, concat_axis=0, tiled=True
    ).reshape(slots)
    rows = (dot(w_hi, back, NN) + dot(w_lo, back, NN)).astype(BF)
    keep = lax.dynamic_slice_in_dim(rows, seq_at * own, own, 0)
    give = lax.dynamic_slice_in_dim(rows, (1 - seq_at) * own, own, 0)
    in_grad = ordered(keep, swap(give), seq_at, 1)
    own_table = lax.dynamic_slice_in_dim(table, seq_at * own, own, 0)
    own_ids = lax.dynamic_slice_in_dim(route_ids, seq_at * own, own, 0)
    of_expert = jnp.sum(
        jnp.where(own_table, back_score.astype(F32)[None, :], 0.0).reshape(own, experts, capacity),
        axis=2,
    )
    same = own_ids[:, :, None] == jnp.arange(experts, dtype=jnp.int32)
    weight_grad = jnp.sum(jnp.where(same, of_expert[:, None, :], 0.0), axis=2)
    return in_grad, weight_grad.astype(BF)


MESH = pl.DeviceIdType.MESH
PARTS = 4


def lanes(shape, axis):
    return lax.broadcasted_iota(jnp.int32, shape, axis).astype(F32)


def fdiv(value, by):
    return jnp.floor((value + 0.5) * (1.0 / by))


def ones(mask):
    return jnp.where(mask, 1.0, 0.0).astype(BF)

def xor2(a, b):
    a1, a0, b1, b0 = a // 2, lax.rem(a, 2), b // 2, lax.rem(b, 2)
    return 2 * (a1 + b1 - 2 * a1 * b1) + (a0 + b0 - 2 * a0 * b0)


def pick4(table, i):
    i1, i0 = i // 2, lax.rem(i, 2)
    c0, c1, c2, c3 = table
    return c0 + (c1 - c0) * i0 + (c2 - c0) * i1 + (c3 - c2 - c1 + c0) * i1 * i0


VMEM1 = 50
VMEM2 = 16
SEND = (3, 2, 1, 0)
WORK = (0, 1, 3, 2)


def packed_rows(shape, axis, blk, cap):
    r = lanes(shape, axis)
    block = fdiv(r, blk)
    part = fdiv(r - block * blk, cap)
    return block, part, r - block * blk - part * cap


def permutation(grp, blk, cap):
    a0, b0, p0 = packed_rows((grp, grp), 0, blk, cap)
    return ones(lanes((grp, grp), 1) == b0 * blk + a0 * cap + p0)


def step_kernel(
    n, cap, og, ids_ref, wt_ref, gp_ref, up_ref, wg_hbm, wu_hbm, wd_hbm,
    zo, zp, wmat, wgrad,
    wg, wu, wd, tok, sel, snd, rxo, rxp, pout, pin, snd2,
    vbuf, wbuf, gbuf, scs, sci, sco, scr, perm_ref,
    l_tok, s_tok, r_tok, l_w, s_d, r_d, s_f, r_f, s_p, r_p, s_s, r_s, s_b, r_b, s_c, r_c,
    s_g, r_g, l_z, l_o,
):
    me = lax.axis_index("expert")
    s = lax.axis_index("seq")
    o = 1 - s
    own, width = og.shape
    half = width // 2
    slots = n * cap
    blk = PARTS * cap
    grp = PARTS * blk
    rows = PARTS * cap
    qw = half // PARTS
    quads = n // PARTS
    zat = me // PARTS
    tokens = 2 * own

    barrier = pltpu.get_barrier_semaphore()
    pl.semaphore_signal(barrier, inc=1, device_id=(me, o), device_id_type=MESH)

    def greet(i, c):
        pl.semaphore_signal(
            barrier, inc=1, device_id=(lax.rem(me + i, n), s), device_id_type=MESH
        )
        return c

    lax.fori_loop(1, n, greet, 0)

    base = pl.multiple_of(s * half, 128)
    obase = pl.multiple_of(o * half, 128)
    mine = pl.multiple_of(s * own, 128)

    def remote(src, dst, ss, rs, dev):
        return pltpu.make_async_remote_copy(
            src_ref=src, dst_ref=dst, send_sem=ss, recv_sem=rs, device_id=dev, device_id_type=MESH
        )

    def tok_at(q):
        return tok.at[pl.ds(pl.multiple_of(q * tokens + mine, 16), own), :]

    def tok_local(q):
        cols = pl.ds(pl.multiple_of(base + q * qw, 128), qw)
        return pltpu.make_async_copy(og.at[:, cols], tok_at(q), l_tok.at[q])

    def tok_copy(q):
        cols = pl.ds(pl.multiple_of(obase + q * qw, 128), qw)
        return remote(og.at[:, cols], tok_at(q), s_tok.at[q], r_tok.at[q], (me, o))

    for q in range(PARTS):
        tok_local(q).start()

    ids = jnp.transpose(ids_ref[...])
    e_lane = lax.broadcasted_iota(jnp.int32, (tokens, n), 1)
    hit = jnp.zeros((tokens, n), F32)
    for k in range(ids_ref.shape[0]):
        hit = jnp.where(ids[:, k : k + 1] == e_lane, 1.0, hit)
    tri = ones(lanes((tokens, tokens), 1) < lanes((tokens, tokens), 0))
    pos = dot(tri, hit.astype(BF), NN)
    v = jnp.where((hit > 0.5) & (pos < cap - 0.5), pos, 255.0)
    vbuf[...] = v
    vb = v.astype(BF)

    pl.semaphore_wait(barrier, n)
    for q in range(PARTS):
        tok_copy(q).start()

    perm_ref[...] = permutation(grp, blk, cap)
    r_block, r_part, r_place = packed_rows((grp, tokens), 0, blk, cap)
    pick_block = packed_rows((grp, n), 0, blk, cap)[0]

    def build(quad, carry):
        pick = ones(pick_block + (quad * PARTS).astype(F32) == lanes((grp, n), 1))
        found = dot(pick, vb, NT) == r_place
        at = pl.ds(pl.multiple_of(quad * grp, 16), grp)
        for q in range(PARTS):
            sel[at, q * tokens : (q + 1) * tokens] = ones(found & (r_part == float(q)))
        return carry

    lax.fori_loop(0, quads, build, 0)

    def d_copy(dest):
        at = pl.multiple_of(dest * blk, 16)
        to = pl.multiple_of(me * blk, 16)
        return remote(
            snd.at[pl.ds(at, blk), :], rxo.at[pl.ds(to, blk), :], s_d.at[dest], r_d.at[me], (dest, s)
        )

    def d_wait(src):
        at = pl.multiple_of(src * blk, 16)
        return remote(
            snd.at[pl.ds(at, blk), :], rxo.at[pl.ds(at, blk), :], s_d.at[src], r_d.at[src], (src, s)
        )

    def f_copy(src):
        at = pl.multiple_of(src * blk, 16)
        return remote(
            rxo.at[pl.ds(at, blk), :], rxp.at[pl.ds(at, blk), :], s_f.at[src], r_f.at[src], (me, o)
        )

    def own_copy():
        at = pl.multiple_of(me * blk, 16)
        return remote(
            snd.at[pl.ds(at, blk), :], rxp.at[pl.ds(at, blk), :], s_f.at[me], r_f.at[me], (me, o)
        )

    for q in range(PARTS):
        tok_local(q).wait()
        tok_copy(q).wait_recv()

    def dispatch(i, carry):
        quad = xor2(zat, pick4(SEND, i))
        at = pl.ds(pl.multiple_of(quad * grp, 16), grp)
        snd[at, :] = dot(sel[at, :], tok[...], NN).astype(BF)
        for j in range(PARTS):
            dest = quad * PARTS + j

            @pl.when(dest != me)
            def _():
                d_copy(dest).start()

            @pl.when(dest == me)
            def _():
                here = pl.ds(pl.multiple_of(me * blk, 16), blk)
                rxo[here, :] = snd[here, :]
                own_copy().start()

        return carry

    lax.fori_loop(0, quads, dispatch, 0)
    loads = [
        pltpu.make_async_copy(wd_hbm, wd, l_w.at[0]),
        pltpu.make_async_copy(wg_hbm, wg, l_w.at[1]),
        pltpu.make_async_copy(wu_hbm, wu, l_w.at[2]),
    ]
    for load in loads:
        load.start()

    my_ids = jnp.transpose(ids_ref[:, pl.ds(mine, own)].astype(F32))
    my_wts = jnp.transpose(wt_ref[:, pl.ds(mine, own)])
    my_v = vbuf[pl.ds(mine, own), :].astype(BF)
    my_lane = lanes((own, n), 1)
    wte = jnp.zeros((own, n), F32)
    for k in range(ids_ref.shape[0]):
        wte = jnp.where(my_ids[:, k : k + 1] == my_lane, my_wts[:, k : k + 1], wte)
    c = lanes((own, slots), 1)
    place = c - cap * fdiv(c, cap)
    expand = ones(fdiv(lanes((n, slots), 1), cap) == lanes((n, slots), 0))
    taken = dot(my_v, expand, NN) == place
    hi = wte.astype(BF)
    lo = (wte - hi.astype(F32)).astype(BF)
    wbuf[:own, :] = jnp.where(taken, dot(hi, expand, NN), 0.0).astype(BF)
    wbuf[own:, :] = jnp.where(taken, dot(lo, expand, NN), 0.0).astype(BF)
    w_out = pltpu.make_async_copy(wbuf, wmat, l_o.at[0])
    w_out.start()

    def p_copy(i, q):
        return remote(
            pout.at[i, q], pin.at[i, q], s_p.at[i * PARTS + q], r_p.at[i * PARTS + q], (me, o)
        )

    def sc_copy(i):
        return remote(scs.at[i], sci.at[i], s_s.at[i], r_s.at[i], (me, o))

    def b_copy(dest):
        at = pl.multiple_of(dest * blk, 16)
        to = pl.multiple_of(me * blk, 16)
        return remote(
            snd2.at[pl.ds(at, blk), :], zo.at[pl.ds(to, blk), :], s_b.at[dest], r_b.at[me], (dest, s)
        )

    def b_wait(src):
        at = pl.multiple_of(src * blk, 16)
        return remote(
            snd2.at[pl.ds(at, blk), :], zo.at[pl.ds(at, blk), :], s_b.at[src], r_b.at[src], (src, s)
        )

    def g_copy(src):
        at = pl.multiple_of(src * blk, 16)
        return remote(
            zo.at[pl.ds(at, blk), :], zp.at[pl.ds(at, blk), :], s_g.at[src], r_g.at[src], (me, o)
        )

    def own_back():
        at = pl.multiple_of(me * blk, 16)
        return remote(
            snd2.at[pl.ds(at, blk), :], zp.at[pl.ds(at, blk), :], s_g.at[me], r_g.at[me], (me, o)
        )

    def own_local():
        at = pl.multiple_of(me * blk, 16)
        return pltpu.make_async_copy(snd2.at[pl.ds(at, blk), :], zo.at[pl.ds(at, blk), :], l_z)

    def c_copy(dest):
        at = pl.multiple_of(dest * 16, 16)
        to = pl.multiple_of(me * 16, 16)
        return remote(
            sco.at[pl.ds(at, 16), :], scr.at[pl.ds(to, 16), :], s_c.at[dest], r_c.at[me], (dest, s)
        )

    def c_wait(src):
        at = pl.multiple_of(src * 16, 16)
        return remote(
            sco.at[pl.ds(at, 16), :], scr.at[pl.ds(at, 16), :], s_c.at[src], r_c.at[src], (src, s)
        )

    def work(i, carry):
        quad = xor2(zat, pick4(WORK, i))
        packed = pl.ds(pl.multiple_of(quad * grp, 16), grp)
        slot_at = pl.ds(pl.multiple_of(quad * rows, 16), rows)
        for j in range(PARTS):
            src = quad * PARTS + j

            @pl.when(src != me)
            def _():
                d_wait(src).wait_recv()
                f_copy(src).start()

        @pl.when(i == 0)
        def _():
            loads[0].wait()

        perm = perm_ref[...]
        got = dot(perm, rxo[packed, :], NN).astype(BF)
        grad = jnp.zeros((rows, gp_ref.shape[1]), F32)
        for q in range(PARTS):
            cols = pl.ds(pl.multiple_of(base + q * qw, 128), qw)
            grad = grad + dot(got[q * rows : (q + 1) * rows], wd[:, cols], NT)
        for j in range(PARTS):
            f_copy(quad * PARTS + j).wait_recv()
        got = dot(perm, rxp[packed, :], NN).astype(BF)
        for q in range(PARTS):
            cols = pl.ds(pl.multiple_of(obase + q * qw, 128), qw)
            grad = grad + dot(got[q * rows : (q + 1) * rows], wd[:, cols], NT)
        active, slope = silu_parts(gp_ref[slot_at, :].astype(F32))
        up = up_ref[slot_at, :].astype(F32)
        ud_v = grad * active
        gd = (grad * up * slope).astype(BF)
        ud = ud_v.astype(BF)
        score = jnp.sum(ud_v * up, axis=1, keepdims=True)
        scs[i] = jnp.broadcast_to(score, (rows, 128)).astype(BF)
        sc_copy(i).start()

        @pl.when(i == 0)
        def _():
            loads[1].wait()
            loads[2].wait()

        def part(start):
            at = pl.ds(pl.multiple_of(start, 128), qw)
            return (dot(gd, wg[at, :], NT) + dot(ud, wu[at, :], NT)).astype(BF)

        for q in range(PARTS):
            pout[i, q] = part(obase + q * qw)
            p_copy(i, q).start()
        kept = []
        for q in range(PARTS):
            value = part(base + q * qw).astype(F32)
            p_copy(i, q).wait_recv()
            kept.append((value + pin[i, q].astype(F32)).astype(BF))
        snd2[packed, :] = dot(perm, jnp.concatenate(kept, axis=0), NN).astype(BF)
        sc_copy(i).wait_recv()
        total = (scs[i].astype(F32) + sci[i].astype(F32)).astype(BF)
        sr = lanes((PARTS * 16, rows), 0)
        se = fdiv(sr, 16)
        sp = sr - 16 * se
        spread = ones((lanes((PARTS * 16, rows), 1) == se * cap + sp) & (sp < cap - 0.5))
        sco[pl.ds(pl.multiple_of(quad * PARTS * 16, 16), PARTS * 16), :] = dot(spread, total, NN).astype(BF)
        for j in range(PARTS):
            dest = quad * PARTS + j

            @pl.when(dest != me)
            def _():
                c_copy(dest).start()
                b_copy(dest).start()

            @pl.when(dest == me)
            def _():
                own_back().start()
                own_local().start()
                there = pl.ds(pl.multiple_of(me * 16, 16), 16)
                scr[there, :] = sco[there, :]

        return carry

    lax.fori_loop(0, quads, work, 0)

    def collect(i, carry):
        quad = xor2(zat, pick4(WORK, i))
        for j in range(PARTS):
            src = quad * PARTS + j

            @pl.when(src != me)
            def _():
                b_wait(src).wait_recv()
                g_copy(src).start()

        return carry

    lax.fori_loop(0, quads - 1, collect, 0)

    def scores(i, carry):
        c_wait(lax.rem(me + i, n)).wait_recv()
        return carry

    lax.fori_loop(1, n, scores, 0)
    wide = n * 16
    wc = lanes((own, wide), 1)
    we = fdiv(wc, 16)
    spot = dot(my_v, ones(fdiv(lanes((n, wide), 1), 16) == lanes((n, wide), 0)), NN) == wc - 16 * we
    acc = jnp.zeros((own, 128), F32)
    for k in range(ids_ref.shape[0]):
        mask = ones(spot & (we == my_ids[:, k : k + 1]))
        acc = jnp.where(lanes((own, 128), 1) == k, dot(mask, scr[...], NN), acc)
    gbuf[...] = jnp.transpose(acc)[: gbuf.shape[0]]
    g_out = pltpu.make_async_copy(gbuf, wgrad, l_o.at[1])
    g_out.start()

    for q in range(PARTS):
        tok_copy(q).wait_send()

    def drain(i, carry):
        dest = lax.rem(me + i, n)
        d_copy(dest).wait_send()
        f_copy(dest).wait_send()
        c_copy(dest).wait_send()
        return carry

    lax.fori_loop(1, n, drain, 0)
    own_copy().wait_send()

    def drain2(i, carry):
        sc_copy(i).wait_send()
        for q in range(PARTS):
            p_copy(i, q).wait_send()
        return carry

    lax.fori_loop(0, quads, drain2, 0)
    w_out.wait()
    own_local().wait()

    collect(quads - 1, 0)

    g_out.wait()
    own_back().wait_send()
    g_copy(me).wait_recv()

    def drain3(i, carry):
        src = lax.rem(me + i, n)
        b_copy(src).wait_send()
        g_copy(src).wait_send()
        g_copy(src).wait_recv()
        return carry

    lax.fori_loop(1, n, drain3, 0)


def finish_kernel(n, cap, zo, zp, w_ref, g_ref, out, gout, zb, zu, ob, s_in, s_out):
    s = lax.axis_index("seq")
    own = out.shape[0]
    half = out.shape[1] // 2
    qw = half // PARTS
    blk = PARTS * cap
    grp = PARTS * blk
    rows = PARTS * cap
    quads = n // PARTS
    loads = []
    for h, z in enumerate((zo, zp)):
        for quad in range(quads):
            copy = pltpu.make_async_copy(
                z.at[pl.ds(quad * grp, grp), :], zb.at[h, quad], s_in.at[h * quads + quad]
            )
            copy.start()
            loads.append(copy)
    perm = permutation(grp, blk, cap)
    gout[...] = g_ref[...].astype(BF)
    stores = []
    for h in range(2):
        for quad in range(quads):
            loads[h * quads + quad].wait()
            got = dot(perm, zb[h, quad], NN).astype(BF)
            for q in range(PARTS):
                zu[h, q, quad * rows : (quad + 1) * rows, :] = got[q * rows : (q + 1) * rows]
        start = s * half if h == 0 else (1 - s) * half
        for q in range(PARTS):
            both = dot(w_ref[...], zu[h, q], NN)
            ob[h, q] = (both[:own] + both[own:]).astype(BF)
            copy = pltpu.make_async_copy(
                ob.at[h, q], out.at[:, pl.ds(pl.multiple_of(start + q * qw, 128), qw)],
                s_out.at[h * PARTS + q],
            )
            copy.start()
            stores.append(copy)
    for copy in stores:
        copy.wait()


def scratch(n, cap, own, width, hidden, topk):
    half = width // 2
    slots = n * cap
    big = PARTS * slots
    qw = half // PARTS
    quads = n // PARTS
    rows = PARTS * cap
    grp = PARTS * rows
    vm, dma = pltpu.VMEM, pltpu.SemaphoreType.DMA
    return [
        vm((width, hidden), BF), vm((width, hidden), BF), vm((hidden, width), BF),
        vm((PARTS * 2 * own, qw), BF), vm((big, PARTS * 2 * own), BF), vm((big, qw), BF),
        vm((big, qw), BF), vm((big, qw), BF),
        vm((quads, PARTS, rows, qw), BF), vm((quads, PARTS, rows, qw), BF), vm((big, qw), BF),
        vm((2 * own, n), F32), vm((2 * own, slots), BF), vm((topk, own), F32),
        vm((quads, rows, 128), BF), vm((quads, rows, 128), BF), vm((n * 16, 128), BF),
        vm((n * 16, 128), BF), vm((grp, grp), BF),
        dma((PARTS,)), dma((PARTS,)), dma((PARTS,)), dma((3,)),
        dma((n,)), dma((n,)), dma((n,)), dma((n,)), dma((n,)), dma((n,)), dma((quads,)), dma((quads,)),
        dma((n,)), dma((n,)), dma((n,)), dma((n,)), dma((n,)), dma((n,)), dma, dma((2,)),
    ]


def kernel_fits(n, cap, own, width, hidden):
    half = width // 2
    slots = n * cap
    size = 2 * (3 * width * hidden + 10 * slots * half + 4 * own * half)
    aligned = (PARTS * cap) % 16 == 0 and half % (PARTS * 128) == 0 and half % 512 == 0
    return n == PARTS * 4 and cap <= 16 and aligned and own == 128 and size < 48 * 2**20


def on_device(out_grad, route_ids, route_weights, gate_pre, up_pre, w_gate, w_up, w_down):
    n = lax.axis_size("expert")
    own, width = out_grad.shape
    slots, hidden = gate_pre.shape[1:]
    cap = slots // n
    topk = route_ids.shape[1]
    args = (out_grad, route_ids, route_weights, gate_pre, up_pre, w_gate, w_up, w_down)
    if not kernel_fits(n, cap, own, width, hidden):
        return on_device_xla(*args)
    qw = width // 2 // PARTS
    big = PARTS * slots
    grp = PARTS * PARTS * cap
    quads = n // PARTS
    anywhere = pl.BlockSpec(memory_space=pl.ANY)
    vmem = pl.BlockSpec(memory_space=pltpu.VMEM)
    zo, zp, wmat, wgrad = pl.pallas_call(
        functools.partial(step_kernel, n, cap),
        out_shape=(
            jax.ShapeDtypeStruct((big, qw), BF),
            jax.ShapeDtypeStruct((big, qw), BF),
            jax.ShapeDtypeStruct((2 * own, slots), BF),
            jax.ShapeDtypeStruct((topk, own), F32),
        ),
        in_specs=[anywhere, vmem, vmem, vmem, vmem, anywhere, anywhere, anywhere],
        out_specs=(anywhere, anywhere, anywhere, anywhere),
        scratch_shapes=scratch(n, cap, own, width, hidden, topk),
        compiler_params=pltpu.CompilerParams(
            collective_id=0, has_side_effects=True, vmem_limit_bytes=VMEM1 * 2**20
        ),
        name="expert_step",
    )(
        out_grad, route_ids.T, route_weights.T, gate_pre[0], up_pre[0], w_gate[0], w_up[0], w_down[0]
    )
    in_grad, weight_grad = pl.pallas_call(
        functools.partial(finish_kernel, n, cap),
        out_shape=(
            jax.ShapeDtypeStruct((own, width), BF),
            jax.ShapeDtypeStruct((topk, own), BF),
        ),
        in_specs=[anywhere, anywhere, vmem, vmem],
        out_specs=(anywhere, vmem),
        scratch_shapes=[
            pltpu.VMEM((2, quads, grp, qw), BF), pltpu.VMEM((2, PARTS, slots, qw), BF),
            pltpu.VMEM((2, PARTS, own, qw), BF),
            pltpu.SemaphoreType.DMA((2 * quads,)), pltpu.SemaphoreType.DMA((2 * PARTS,)),
        ],
        compiler_params=pltpu.CompilerParams(vmem_limit_bytes=VMEM2 * 2**20),
        name="combine",
    )(zo, zp, wmat, wgrad)
    return in_grad, weight_grad.T


def solution(mesh):
    in_specs = (
        P(("expert", "seq"), None),
        P("expert", None),
        P("expert", None),
        P("expert", None, "seq"),
        P("expert", None, "seq"),
        P("expert", None, "seq"),
        P("expert", None, "seq"),
        P("expert", "seq", None),
    )
    out_specs = (P(("expert", "seq"), None), P(("expert", "seq"), None))
    return jax.shard_map(
        on_device, mesh=mesh, in_specs=in_specs, out_specs=out_specs, check_vma=False
    )
```

```python
import functools

import jax
import jax.numpy as jnp
from jax import lax
from jax.experimental import pallas as pl
from jax.experimental.pallas import tpu as pltpu
from jax.sharding import PartitionSpec as P

BF = jnp.bfloat16
F32 = jnp.float32
NT = (((1,), (1,)), ((), ()))
NN = (((1,), (0,)), ((), ()))
TN = (((0,), (0,)), ((), ()))


def silu_parts(value):
    sigma = jax.nn.sigmoid(value)
    return (value * sigma, sigma * (1.0 + value * (1.0 - sigma)))


def dot(a, b, dims):
    return lax.dot_general(a, b, dims, preferred_element_type=F32)


def swap(value):
    return lax.ppermute(value, "seq", [(0, 1), (1, 0)])


def ordered(mine, theirs, seq_at, axis):
    low = jnp.where(seq_at == 0, mine, theirs)
    high = jnp.where(seq_at == 0, theirs, mine)
    return jnp.concatenate([low, high], axis=axis)


def routing(ids, weights, experts, capacity):
    tokens = ids.shape[0]
    same = ids[:, :, None] == jnp.arange(experts, dtype=jnp.int32)
    hit = jnp.any(same, axis=1)
    weight = jnp.sum(jnp.where(same, weights[:, :, None], 0.0), axis=1)
    row = jnp.arange(tokens, dtype=jnp.int32)
    earlier = (row[None, :] < row[:, None]).astype(BF)
    position = dot(earlier, hit.astype(BF), NN)
    slot = jnp.where(hit, position, float(capacity))
    return slot, weight


def on_device_xla(out_grad, route_ids, route_weights, gate_pre, up_pre, w_gate, w_up, w_down):
    n_expert = lax.axis_size("expert")
    seq_at = lax.axis_index("seq")
    own, width = out_grad.shape
    half = width // 2
    experts = n_expert
    slots = gate_pre.shape[1]
    capacity = slots // n_expert
    slot, weight = routing(route_ids, route_weights, experts, capacity)
    table = (slot[:, :, None] == jnp.arange(capacity, dtype=F32)).reshape(2 * own, slots)
    w_all = jnp.broadcast_to(weight[:, :, None], (2 * own, experts, capacity)).reshape(2 * own, slots)
    w_all = jnp.where(table, w_all, 0.0)
    w_hi = w_all.astype(BF)
    w_lo = (w_all - w_hi.astype(F32)).astype(BF)
    mine = lax.dynamic_slice_in_dim(out_grad, seq_at * half, half, 1)
    other = lax.dynamic_slice_in_dim(out_grad, (1 - seq_at) * half, half, 1)
    tokens = ordered(mine, swap(other), seq_at, 0)
    outgoing = dot(table.astype(BF), tokens, TN).astype(BF).reshape(experts, capacity, half)
    received = lax.all_to_all(outgoing, "expert", split_axis=0, concat_axis=0, tiled=True)
    received = received.reshape(slots, half)
    slot_grad = ordered(received, swap(received), seq_at, 1)
    hidden_grad = dot(slot_grad, w_down[0], NT)
    active, slope = silu_parts(gate_pre[0].astype(F32))
    up_part = up_pre[0].astype(F32)
    score = jnp.sum(hidden_grad * active * up_part, axis=1).astype(BF)
    gate_diff = (hidden_grad * up_part * slope).astype(BF)
    up_diff = (hidden_grad * active).astype(BF)
    part = (dot(gate_diff, w_gate[0], NT) + dot(up_diff, w_up[0], NT)).astype(BF)
    score = lax.optimization_barrier(score)
    part = lax.optimization_barrier(part)
    keep = lax.dynamic_slice_in_dim(part, seq_at * half, half, 1)
    give = lax.dynamic_slice_in_dim(part, (1 - seq_at) * half, half, 1)
    total = (keep.astype(F32) + swap(give).astype(F32)).astype(BF)
    total_score = (score.astype(F32) + swap(score).astype(F32)).astype(BF)
    back = lax.all_to_all(
        total.reshape(n_expert, capacity, half), "expert", split_axis=0, concat_axis=0, tiled=True
    ).reshape(slots, half)
    back_score = lax.all_to_all(
        total_score.reshape(n_expert, capacity), "expert", split_axis=0, concat_axis=0, tiled=True
    ).reshape(slots)
    rows = (dot(w_hi, back, NN) + dot(w_lo, back, NN)).astype(BF)
    keep = lax.dynamic_slice_in_dim(rows, seq_at * own, own, 0)
    give = lax.dynamic_slice_in_dim(rows, (1 - seq_at) * own, own, 0)
    in_grad = ordered(keep, swap(give), seq_at, 1)
    own_table = lax.dynamic_slice_in_dim(table, seq_at * own, own, 0)
    own_ids = lax.dynamic_slice_in_dim(route_ids, seq_at * own, own, 0)
    of_expert = jnp.sum(
        jnp.where(own_table, back_score.astype(F32)[None, :], 0.0).reshape(own, experts, capacity),
        axis=2,
    )
    same = own_ids[:, :, None] == jnp.arange(experts, dtype=jnp.int32)
    weight_grad = jnp.sum(jnp.where(same, of_expert[:, None, :], 0.0), axis=2)
    return in_grad, weight_grad.astype(BF)


MESH = pl.DeviceIdType.MESH
PARTS = 4


def lanes(shape, axis):
    return lax.broadcasted_iota(jnp.int32, shape, axis).astype(F32)


def fdiv(value, by):
    return jnp.floor((value + 0.5) * (1.0 / by))


def ones(mask):
    return jnp.where(mask, 1.0, 0.0).astype(BF)

def pick4(table, i):
    i1, i0 = i // 2, lax.rem(i, 2)
    c0, c1, c2, c3 = table
    return c0 + (c1 - c0) * i0 + (c2 - c0) * i1 + (c3 - c2 - c1 + c0) * i1 * i0


VMEM1 = 50
VMEM2 = 16
SEND = ((2, 0, 3, 1), (1, 0, 3, 2), (2, 3, 0, 1), (1, 3, 0, 2))
WORK = ((0, 3, 1, 2), (1, 3, 0, 2), (2, 0, 3, 1), (3, 0, 2, 1))
COLLECT = ((0, 1, 2, 3), (1, 0, 2, 3), (2, 3, 1, 0), (3, 2, 1, 0))


def quad_in(order, z, i):
    return pick4([pick4(row, i) for row in order], z)


def packed_rows(shape, axis, blk, cap):
    r = lanes(shape, axis)
    block = fdiv(r, blk)
    part = fdiv(r - block * blk, cap)
    return block, part, r - block * blk - part * cap


def permutation(grp, blk, cap):
    a0, b0, p0 = packed_rows((grp, grp), 0, blk, cap)
    return ones(lanes((grp, grp), 1) == b0 * blk + a0 * cap + p0)


def step_kernel(
    n, cap, og, ids_hbm, wt_hbm, gp_hbm, up_hbm, wg_hbm, wu_hbm, wd_hbm,
    zl, accp_out, own_out, wlast_out, wgrad,
    ids_ref, wt_ref, gp_ref, up_ref, wg, wu, wd, tok, sel, snd, rxo, rxp, pout, pin, snd2, zo, zp,
    vbuf, wk, wlast, acco, accp, ohalf, gbuf, scs, sci, sco, scr, perm_ref,
    l_in, l_tok, s_tok, r_tok, l_w, s_d, r_d, s_f, r_f, s_p, r_p, s_s, r_s, s_b, r_b, s_c, r_c,
    s_g, r_g, l_o, l_h,
):
    me = lax.axis_index("expert")
    s = lax.axis_index("seq")
    o = 1 - s
    own, width = og.shape
    half = width // 2
    slots = n * cap
    blk = PARTS * cap
    grp = PARTS * blk
    rows = PARTS * cap
    qw = half // PARTS
    quads = n // PARTS
    zat = me // PARTS
    tokens = 2 * own

    inputs = [
        pltpu.make_async_copy(ids_hbm, ids_ref, l_in.at[0]),
        pltpu.make_async_copy(wt_hbm, wt_ref, l_in.at[1]),
        pltpu.make_async_copy(gp_hbm, gp_ref, l_in.at[2]),
        pltpu.make_async_copy(up_hbm, up_ref, l_in.at[3]),
    ]
    inputs[0].start()
    barrier = pltpu.get_barrier_semaphore()
    pl.semaphore_signal(barrier, inc=1, device_id=(me, o), device_id_type=MESH)

    def greet(i, c):
        pl.semaphore_signal(
            barrier, inc=1, device_id=(lax.rem(me + i, n), s), device_id_type=MESH
        )
        return c

    lax.fori_loop(1, n, greet, 0)

    base = pl.multiple_of(s * half, 128)
    obase = pl.multiple_of(o * half, 128)
    mine = pl.multiple_of(s * own, 128)

    def remote(src, dst, ss, rs, dev):
        return pltpu.make_async_remote_copy(
            src_ref=src, dst_ref=dst, send_sem=ss, recv_sem=rs, device_id=dev, device_id_type=MESH
        )

    def tok_at(q):
        return tok.at[pl.ds(pl.multiple_of(q * tokens + mine, 16), own), :]

    def tok_local(q):
        cols = pl.ds(pl.multiple_of(base + q * qw, 128), qw)
        return pltpu.make_async_copy(og.at[:, cols], tok_at(q), l_tok.at[q])

    def tok_copy(q):
        cols = pl.ds(pl.multiple_of(obase + q * qw, 128), qw)
        return remote(og.at[:, cols], tok_at(q), s_tok.at[q], r_tok.at[q], (me, o))

    for q in range(PARTS):
        tok_local(q).start()
    for load in inputs[1:]:
        load.start()

    inputs[0].wait()
    ids = jnp.transpose(ids_ref[...])
    e_lane = lax.broadcasted_iota(jnp.int32, (tokens, n), 1)
    hit = jnp.zeros((tokens, n), F32)
    for k in range(ids_ref.shape[0]):
        hit = jnp.where(ids[:, k : k + 1] == e_lane, 1.0, hit)
    tri = ones(lanes((tokens, tokens), 1) < lanes((tokens, tokens), 0))
    pos = dot(tri, hit.astype(BF), NN)
    v = jnp.where((hit > 0.5) & (pos < cap - 0.5), pos, 255.0)
    vbuf[...] = v
    vb = v.astype(BF)

    pl.semaphore_wait(barrier, n)
    for q in range(PARTS):
        tok_copy(q).start()

    perm_ref[...] = permutation(grp, blk, cap)
    r_block, r_part, r_place = packed_rows((grp, tokens), 0, blk, cap)
    pick_block = packed_rows((grp, n), 0, blk, cap)[0]

    def build(quad, carry):
        pick = ones(pick_block + (quad * PARTS).astype(F32) == lanes((grp, n), 1))
        found = dot(pick, vb, NT) == r_place
        at = pl.ds(pl.multiple_of(quad * grp, 16), grp)
        for q in range(PARTS):
            sel[at, q * tokens : (q + 1) * tokens] = ones(found & (r_part == float(q)))
        return carry

    lax.fori_loop(0, quads, build, 0)

    def d_copy(dest):
        at = pl.multiple_of(dest * blk, 16)
        to = pl.multiple_of(me * blk, 16)
        return remote(
            snd.at[pl.ds(at, blk), :], rxo.at[pl.ds(to, blk), :], s_d.at[dest], r_d.at[me], (dest, s)
        )

    def d_wait(src):
        at = pl.multiple_of(src * blk, 16)
        return remote(
            snd.at[pl.ds(at, blk), :], rxo.at[pl.ds(at, blk), :], s_d.at[src], r_d.at[src], (src, s)
        )

    def f_copy(src):
        at = pl.multiple_of(src * blk, 16)
        return remote(
            rxo.at[pl.ds(at, blk), :], rxp.at[pl.ds(at, blk), :], s_f.at[src], r_f.at[src], (me, o)
        )

    def own_copy():
        at = pl.multiple_of(me * blk, 16)
        return remote(
            snd.at[pl.ds(at, blk), :], rxp.at[pl.ds(at, blk), :], s_f.at[me], r_f.at[me], (me, o)
        )

    for q in range(PARTS):
        tok_local(q).wait()
        tok_copy(q).wait_recv()

    def dispatch(i, carry):
        quad = quad_in(SEND, zat, i)
        at = pl.ds(pl.multiple_of(quad * grp, 16), grp)
        snd[at, :] = dot(sel[at, :], tok[...], NN).astype(BF)
        for j in range(PARTS):
            dest = quad * PARTS + j

            @pl.when(dest != me)
            def _():
                d_copy(dest).start()

            @pl.when(dest == me)
            def _():
                here = pl.ds(pl.multiple_of(me * blk, 16), blk)
                rxo[here, :] = snd[here, :]
                own_copy().start()

        return carry

    lax.fori_loop(0, quads, dispatch, 0)
    loads = [
        pltpu.make_async_copy(wd_hbm, wd, l_w.at[0]),
        pltpu.make_async_copy(wg_hbm, wg, l_w.at[1]),
        pltpu.make_async_copy(wu_hbm, wu, l_w.at[2]),
    ]
    for load in loads:
        load.start()

    for load in inputs[1:]:
        load.wait()
    my_ids = jnp.transpose(ids_ref[:, pl.ds(mine, own)].astype(F32))
    my_wts = jnp.transpose(wt_ref[:, pl.ds(mine, own)])
    my_v = vbuf[pl.ds(mine, own), :].astype(BF)
    my_lane = lanes((own, n), 1)
    wte = jnp.zeros((own, n), F32)
    for k in range(ids_ref.shape[0]):
        wte = jnp.where(my_ids[:, k : k + 1] == my_lane, my_wts[:, k : k + 1], wte)
    hi = wte.astype(BF)
    lo = (wte - hi.astype(F32)).astype(BF)

    def weights(order):
        c = lanes((own, len(order) * rows), 1)
        place = c - cap * fdiv(c, cap)
        ce = fdiv(lanes((n, len(order) * rows), 1), cap)
        expert = ce + (order[0] * PARTS).astype(F32)
        if len(order) > 1:
            expert = jnp.where(ce < PARTS - 0.5, expert, ce + ((order[1] - 1) * PARTS).astype(F32))
        expand = ones(expert == lanes((n, len(order) * rows), 0))
        taken = dot(my_v, expand, NN) == place
        return [jnp.where(taken, dot(x, expand, NN), 0.0).astype(BF) for x in (hi, lo)]

    for i in range(2):
        wk[i, :own, :], wk[i, own:, :] = weights([quad_in(COLLECT, zat, i)])
    wlast[:own, :], wlast[own:, :] = weights([quad_in(COLLECT, zat, i) for i in (2, 3)])
    w_out = pltpu.make_async_copy(wlast, wlast_out, l_o.at[0])
    w_out.start()

    def p_copy(i, q):
        return remote(
            pout.at[i, q], pin.at[i, q], s_p.at[i * PARTS + q], r_p.at[i * PARTS + q], (me, o)
        )

    def sc_copy(i):
        return remote(scs.at[i], sci.at[i], s_s.at[i], r_s.at[i], (me, o))

    def b_copy(dest):
        at = pl.multiple_of(dest * blk, 16)
        to = pl.multiple_of(me * blk, 16)
        return remote(
            snd2.at[pl.ds(at, blk), :], zo.at[pl.ds(to, blk), :], s_b.at[dest], r_b.at[me], (dest, s)
        )

    def b_wait(src):
        at = pl.multiple_of(src * blk, 16)
        return remote(
            snd2.at[pl.ds(at, blk), :], zo.at[pl.ds(at, blk), :], s_b.at[src], r_b.at[src], (src, s)
        )

    def g_copy(src):
        at = pl.multiple_of(src * blk, 16)
        return remote(
            zo.at[pl.ds(at, blk), :], zp.at[pl.ds(at, blk), :], s_g.at[src], r_g.at[src], (me, o)
        )

    def h_copy(src, place):
        at = pl.multiple_of(src * blk, 16)
        to = pl.multiple_of(place * blk, 16)
        return remote(
            zo.at[pl.ds(at, blk), :], zl.at[pl.ds(to, blk), :], s_g.at[src], r_g.at[src], (me, o)
        )

    def own_back():
        at = pl.multiple_of(me * blk, 16)
        return remote(
            snd2.at[pl.ds(at, blk), :], zp.at[pl.ds(at, blk), :], s_g.at[me], r_g.at[me], (me, o)
        )

    def c_copy(dest):
        at = pl.multiple_of(dest * 16, 16)
        to = pl.multiple_of(me * 16, 16)
        return remote(
            sco.at[pl.ds(at, 16), :], scr.at[pl.ds(to, 16), :], s_c.at[dest], r_c.at[me], (dest, s)
        )

    def c_wait(src):
        at = pl.multiple_of(src * 16, 16)
        return remote(
            sco.at[pl.ds(at, 16), :], scr.at[pl.ds(at, 16), :], s_c.at[src], r_c.at[src], (src, s)
        )

    def work(i, carry):
        quad = quad_in(WORK, zat, i)
        packed = pl.ds(pl.multiple_of(quad * grp, 16), grp)
        slot_at = pl.ds(pl.multiple_of(quad * rows, 16), rows)
        for j in range(PARTS):
            src = quad * PARTS + j

            @pl.when(src != me)
            def _():
                d_wait(src).wait_recv()
                f_copy(src).start()

        @pl.when(i == 0)
        def _():
            loads[0].wait()

        perm = perm_ref[...]
        got = dot(perm, rxo[packed, :], NN).astype(BF)
        grad = jnp.zeros((rows, gp_ref.shape[1]), F32)
        for q in range(PARTS):
            cols = pl.ds(pl.multiple_of(base + q * qw, 128), qw)
            grad = grad + dot(got[q * rows : (q + 1) * rows], wd[:, cols], NT)
        for j in range(PARTS):
            f_copy(quad * PARTS + j).wait_recv()
        got = dot(perm, rxp[packed, :], NN).astype(BF)
        for q in range(PARTS):
            cols = pl.ds(pl.multiple_of(obase + q * qw, 128), qw)
            grad = grad + dot(got[q * rows : (q + 1) * rows], wd[:, cols], NT)
        active, slope = silu_parts(gp_ref[slot_at, :].astype(F32))
        up = up_ref[slot_at, :].astype(F32)
        ud_v = grad * active
        gd = (grad * up * slope).astype(BF)
        ud = ud_v.astype(BF)
        score = jnp.sum(ud_v * up, axis=1, keepdims=True)
        scs[i] = jnp.broadcast_to(score, (rows, 128)).astype(BF)
        sc_copy(i).start()

        @pl.when(i == 0)
        def _():
            loads[1].wait()
            loads[2].wait()

        def part(start):
            at = pl.ds(pl.multiple_of(start, 128), qw)
            return (dot(gd, wg[at, :], NT) + dot(ud, wu[at, :], NT)).astype(BF)

        for q in range(PARTS):
            pout[i, q] = part(obase + q * qw)
            p_copy(i, q).start()
        kept = []
        for q in range(PARTS):
            value = part(base + q * qw).astype(F32)
            p_copy(i, q).wait_recv()
            kept.append((value + pin[i, q].astype(F32)).astype(BF))
        snd2[packed, :] = dot(perm, jnp.concatenate(kept, axis=0), NN).astype(BF)
        sc_copy(i).wait_recv()
        total = (scs[i].astype(F32) + sci[i].astype(F32)).astype(BF)
        sr = lanes((PARTS * 16, rows), 0)
        se = fdiv(sr, 16)
        sp = sr - 16 * se
        spread = ones((lanes((PARTS * 16, rows), 1) == se * cap + sp) & (sp < cap - 0.5))
        sco[pl.ds(pl.multiple_of(quad * PARTS * 16, 16), PARTS * 16), :] = dot(spread, total, NN).astype(BF)
        for j in range(PARTS):
            dest = quad * PARTS + j

            @pl.when(dest != me)
            def _():
                c_copy(dest).start()
                b_copy(dest).start()

            @pl.when(dest == me)
            def _():
                here = pl.ds(pl.multiple_of(me * blk, 16), blk)
                zo[here, :] = snd2[here, :]
                own_back().start()
                there = pl.ds(pl.multiple_of(me * 16, 16), 16)
                scr[there, :] = sco[there, :]

        return carry

    lax.fori_loop(0, quads, work, 0)

    def add(acc, i, z, packed):
        got = dot(perm_ref[...], z[packed, :], NN).astype(BF)
        for q in range(PARTS):
            both = dot(wk[i], got[q * rows : (q + 1) * rows], NN)
            acc[:, q * qw : (q + 1) * qw] += both[:own] + both[own:]

    acco[...] = jnp.zeros_like(acco)
    accp[...] = jnp.zeros_like(accp)

    def collect(i, carry):
        quad = quad_in(COLLECT, zat, i)
        packed = pl.ds(pl.multiple_of(quad * grp, 16), grp)
        for j in range(PARTS):
            src = quad * PARTS + j

            @pl.when(src != me)
            def _():
                b_wait(src).wait_recv()
                g_copy(src).start()

        add(acco, i, zo, packed)
        for j in range(PARTS):
            g_copy(quad * PARTS + j).wait_recv()
        add(accp, i, zp, packed)
        return carry

    lax.fori_loop(0, 2, collect, 0)
    a_out = pltpu.make_async_copy(accp, accp_out, l_o.at[2])
    a_out.start()

    def scores(i, carry):
        c_wait(lax.rem(me + i, n)).wait_recv()
        return carry

    lax.fori_loop(1, n, scores, 0)
    wide = n * 16
    wc = lanes((own, wide), 1)
    we = fdiv(wc, 16)
    spot = dot(my_v, ones(fdiv(lanes((n, wide), 1), 16) == lanes((n, wide), 0)), NN) == wc - 16 * we
    acc = jnp.zeros((own, 128), F32)
    for k in range(ids_ref.shape[0]):
        mask = ones(spot & (we == my_ids[:, k : k + 1]))
        acc = jnp.where(lanes((own, 128), 1) == k, dot(mask, scr[...], NN), acc)
    gbuf[...] = jnp.transpose(acc)[: gbuf.shape[0]]
    g_out = pltpu.make_async_copy(gbuf, wgrad, l_o.at[1])
    g_out.start()

    for q in range(PARTS):
        tok_copy(q).wait_send()

    def drain(i, carry):
        dest = lax.rem(me + i, n)
        d_copy(dest).wait_send()
        f_copy(dest).wait_send()
        return carry

    lax.fori_loop(1, n, drain, 0)
    own_copy().wait_send()

    def drain2(i, carry):
        sc_copy(i).wait_send()
        for q in range(PARTS):
            p_copy(i, q).wait_send()
        return carry

    lax.fori_loop(0, quads, drain2, 0)
    w_out.wait()
    a_out.wait()
    own_back().wait_send()

    for i in range(2):
        quad = quad_in(COLLECT, zat, i)
        for j in range(PARTS):
            src = quad * PARTS + j

            @pl.when(src != me)
            def _():
                g_copy(src).wait_send()

    ends = [quad_in(COLLECT, zat, i) for i in (2, 3)]

    def last(j, carry):
        for i, quad in enumerate(ends):
            src = quad * PARTS + j
            b_wait(src).wait_recv()
            h_copy(src, i * PARTS + j).start()
        return carry

    lax.fori_loop(0, PARTS, last, 0)
    got = [
        dot(perm_ref[...], zo[pl.ds(pl.multiple_of(quad * grp, 16), grp), :], NN).astype(BF)
        for quad in ends
    ]
    half_out = []
    for q in range(PARTS):
        z = jnp.concatenate([g[q * rows : (q + 1) * rows] for g in got], axis=0)
        both = dot(wlast[...], z, NN)
        ohalf[q] = (acco[:, q * qw : (q + 1) * qw] + both[:own] + both[own:]).astype(BF)
        half_out.append(pltpu.make_async_copy(ohalf.at[q], own_out.at[q], l_h.at[q]))
        half_out[q].start()

    def drain3(i, carry):
        dest = lax.rem(me + i, n)
        b_copy(dest).wait_send()
        c_copy(dest).wait_send()
        return carry

    lax.fori_loop(1, n, drain3, 0)

    def drain4(j, carry):
        for i, quad in enumerate(ends):
            src = quad * PARTS + j
            h_copy(src, i * PARTS + j).wait_send()
            h_copy(src, i * PARTS + j).wait_recv()
        return carry

    lax.fori_loop(0, PARTS, drain4, 0)
    g_out.wait()
    for copy in half_out:
        copy.wait()


def finish_kernel(cap, own_half, zl, accp, w_ref, g_ref, out, gout, ob, s_out):
    s = lax.axis_index("seq")
    own = out.shape[0]
    half = out.shape[1] // 2
    qw = half // PARTS
    blk = PARTS * cap
    grp = PARTS * blk
    rows = PARTS * cap
    stores = []

    def store(src, start, q):
        copy = pltpu.make_async_copy(
            src, out.at[:, pl.ds(pl.multiple_of(start + q * qw, 128), qw)], s_out.at[len(stores)]
        )
        copy.start()
        stores.append(copy)

    for q in range(PARTS):
        store(own_half.at[q], s * half, q)
    gout[...] = g_ref[...].astype(BF)
    perm = permutation(grp, blk, cap)
    got = [dot(perm, zl[i * grp : (i + 1) * grp, :], NN).astype(BF) for i in range(2)]
    for q in range(PARTS):
        z = jnp.concatenate([g[q * rows : (q + 1) * rows] for g in got], axis=0)
        both = dot(w_ref[...], z, NN)
        ob[q] = (accp[:, q * qw : (q + 1) * qw] + both[:own] + both[own:]).astype(BF)
        store(ob.at[q], (1 - s) * half, q)
    for copy in stores:
        copy.wait()


def scratch(n, cap, own, width, hidden, topk):
    half = width // 2
    slots = n * cap
    big = PARTS * slots
    qw = half // PARTS
    quads = n // PARTS
    rows = PARTS * cap
    grp = PARTS * rows
    vm, dma = pltpu.VMEM, pltpu.SemaphoreType.DMA
    return [
        vm((topk, 2 * own), jnp.int32), vm((topk, 2 * own), F32), vm((slots, hidden), BF), vm((slots, hidden), BF),
        vm((width, hidden), BF), vm((width, hidden), BF), vm((hidden, width), BF),
        vm((PARTS * 2 * own, qw), BF), vm((big, PARTS * 2 * own), BF), vm((big, qw), BF),
        vm((big, qw), BF), vm((big, qw), BF),
        vm((quads, PARTS, rows, qw), BF), vm((quads, PARTS, rows, qw), BF), vm((big, qw), BF),
        vm((big, qw), BF), vm((big, qw), BF),
        vm((2 * own, n), F32), vm((2, 2 * own, rows), BF), vm((2 * own, 2 * rows), BF),
        vm((own, half), F32), vm((own, half), F32), vm((PARTS, own, qw), BF), vm((topk, own), F32),
        vm((quads, rows, 128), BF), vm((quads, rows, 128), BF), vm((n * 16, 128), BF),
        vm((n * 16, 128), BF), vm((grp, grp), BF),
        dma((4,)), dma((PARTS,)), dma((PARTS,)), dma((PARTS,)), dma((3,)),
        dma((n,)), dma((n,)), dma((n,)), dma((n,)), dma((n,)), dma((n,)), dma((quads,)), dma((quads,)),
        dma((n,)), dma((n,)), dma((n,)), dma((n,)), dma((n,)), dma((n,)), dma((3,)), dma((PARTS,)),
    ]


def kernel_fits(n, cap, own, width, hidden):
    half = width // 2
    slots = n * cap
    size = 2 * (3 * width * hidden + 10 * slots * half + 4 * own * half)
    aligned = (PARTS * cap) % 16 == 0 and half % (PARTS * 128) == 0 and half % 512 == 0
    return n == PARTS * 4 and cap <= 16 and aligned and own == 128 and size < 48 * 2**20


def on_device(out_grad, route_ids, route_weights, gate_pre, up_pre, w_gate, w_up, w_down):
    n = lax.axis_size("expert")
    own, width = out_grad.shape
    slots, hidden = gate_pre.shape[1:]
    cap = slots // n
    topk = route_ids.shape[1]
    args = (out_grad, route_ids, route_weights, gate_pre, up_pre, w_gate, w_up, w_down)
    if not kernel_fits(n, cap, own, width, hidden):
        return on_device_xla(*args)
    half = width // 2
    qw = half // PARTS
    rows = PARTS * cap
    grp = PARTS * rows
    anywhere = pl.BlockSpec(memory_space=pl.ANY)
    hbm = pl.BlockSpec(memory_space=pltpu.HBM)
    vmem = pl.BlockSpec(memory_space=pltpu.VMEM)
    operands = [
        pltpu.with_memory_space_constraint(x, pltpu.HBM)
        for x in (
            out_grad, route_ids.T, route_weights.T, gate_pre[0], up_pre[0], w_gate[0], w_up[0], w_down[0]
        )
    ]
    zl, accp, own_half, wlast, wgrad = pl.pallas_call(
        functools.partial(step_kernel, n, cap),
        out_shape=(
            jax.ShapeDtypeStruct((2 * grp, qw), BF),
            jax.ShapeDtypeStruct((own, half), F32),
            jax.ShapeDtypeStruct((PARTS, own, qw), BF),
            jax.ShapeDtypeStruct((2 * own, 2 * rows), BF),
            jax.ShapeDtypeStruct((topk, own), F32),
        ),
        in_specs=[hbm] * 8,
        out_specs=(anywhere,) * 5,
        scratch_shapes=scratch(n, cap, own, width, hidden, topk),
        compiler_params=pltpu.CompilerParams(
            collective_id=0, has_side_effects=True, vmem_limit_bytes=VMEM1 * 2**20
        ),
        name="expert_step",
    )(
        *operands
    )
    in_grad, weight_grad = pl.pallas_call(
        functools.partial(finish_kernel, cap),
        out_shape=(
            jax.ShapeDtypeStruct((own, width), BF),
            jax.ShapeDtypeStruct((topk, own), BF),
        ),
        in_specs=[anywhere, vmem, vmem, vmem, vmem],
        out_specs=(anywhere, vmem),
        scratch_shapes=[pltpu.VMEM((PARTS, own, qw), BF), pltpu.SemaphoreType.DMA((2 * PARTS,))],
        compiler_params=pltpu.CompilerParams(vmem_limit_bytes=VMEM2 * 2**20),
        name="combine",
    )(own_half, zl, accp, wlast, wgrad)
    return in_grad, weight_grad.T


def solution(mesh):
    in_specs = (
        P(("expert", "seq"), None),
        P("expert", None),
        P("expert", None),
        P("expert", None, "seq"),
        P("expert", None, "seq"),
        P("expert", None, "seq"),
        P("expert", None, "seq"),
        P("expert", "seq", None),
    )
    out_specs = (P(("expert", "seq"), None), P(("expert", "seq"), None))
    return jax.shard_map(
        on_device, mesh=mesh, in_specs=in_specs, out_specs=out_specs, check_vma=False
    )
```

```python
import functools

import jax
import jax.numpy as jnp
from jax import lax
from jax.experimental import pallas as pl
from jax.experimental.pallas import tpu as pltpu
from jax.sharding import PartitionSpec as P

BF = jnp.bfloat16
F32 = jnp.float32
NT = (((1,), (1,)), ((), ()))
NN = (((1,), (0,)), ((), ()))
TN = (((0,), (0,)), ((), ()))


def silu_parts(value):
    sigma = jax.nn.sigmoid(value)
    return (value * sigma, sigma * (1.0 + value * (1.0 - sigma)))


def dot(a, b, dims):
    return lax.dot_general(a, b, dims, preferred_element_type=F32)


def swap(value):
    return lax.ppermute(value, "seq", [(0, 1), (1, 0)])


def ordered(mine, theirs, seq_at, axis):
    low = jnp.where(seq_at == 0, mine, theirs)
    high = jnp.where(seq_at == 0, theirs, mine)
    return jnp.concatenate([low, high], axis=axis)


def routing(ids, weights, experts, capacity):
    tokens = ids.shape[0]
    same = ids[:, :, None] == jnp.arange(experts, dtype=jnp.int32)
    hit = jnp.any(same, axis=1)
    weight = jnp.sum(jnp.where(same, weights[:, :, None], 0.0), axis=1)
    row = jnp.arange(tokens, dtype=jnp.int32)
    earlier = (row[None, :] < row[:, None]).astype(BF)
    position = dot(earlier, hit.astype(BF), NN)
    slot = jnp.where(hit, position, float(capacity))
    return slot, weight


def on_device_xla(out_grad, route_ids, route_weights, gate_pre, up_pre, w_gate, w_up, w_down):
    n_expert = lax.axis_size("expert")
    seq_at = lax.axis_index("seq")
    own, width = out_grad.shape
    half = width // 2
    experts = n_expert
    slots = gate_pre.shape[1]
    capacity = slots // n_expert
    slot, weight = routing(route_ids, route_weights, experts, capacity)
    table = (slot[:, :, None] == jnp.arange(capacity, dtype=F32)).reshape(2 * own, slots)
    w_all = jnp.broadcast_to(weight[:, :, None], (2 * own, experts, capacity)).reshape(2 * own, slots)
    w_all = jnp.where(table, w_all, 0.0)
    w_hi = w_all.astype(BF)
    w_lo = (w_all - w_hi.astype(F32)).astype(BF)
    mine = lax.dynamic_slice_in_dim(out_grad, seq_at * half, half, 1)
    other = lax.dynamic_slice_in_dim(out_grad, (1 - seq_at) * half, half, 1)
    tokens = ordered(mine, swap(other), seq_at, 0)
    outgoing = dot(table.astype(BF), tokens, TN).astype(BF).reshape(experts, capacity, half)
    received = lax.all_to_all(outgoing, "expert", split_axis=0, concat_axis=0, tiled=True)
    received = received.reshape(slots, half)
    slot_grad = ordered(received, swap(received), seq_at, 1)
    hidden_grad = dot(slot_grad, w_down[0], NT)
    active, slope = silu_parts(gate_pre[0].astype(F32))
    up_part = up_pre[0].astype(F32)
    score = jnp.sum(hidden_grad * active * up_part, axis=1).astype(BF)
    gate_diff = (hidden_grad * up_part * slope).astype(BF)
    up_diff = (hidden_grad * active).astype(BF)
    part = (dot(gate_diff, w_gate[0], NT) + dot(up_diff, w_up[0], NT)).astype(BF)
    score = lax.optimization_barrier(score)
    part = lax.optimization_barrier(part)
    keep = lax.dynamic_slice_in_dim(part, seq_at * half, half, 1)
    give = lax.dynamic_slice_in_dim(part, (1 - seq_at) * half, half, 1)
    total = (keep.astype(F32) + swap(give).astype(F32)).astype(BF)
    total_score = (score.astype(F32) + swap(score).astype(F32)).astype(BF)
    back = lax.all_to_all(
        total.reshape(n_expert, capacity, half), "expert", split_axis=0, concat_axis=0, tiled=True
    ).reshape(slots, half)
    back_score = lax.all_to_all(
        total_score.reshape(n_expert, capacity), "expert", split_axis=0, concat_axis=0, tiled=True
    ).reshape(slots)
    rows = (dot(w_hi, back, NN) + dot(w_lo, back, NN)).astype(BF)
    keep = lax.dynamic_slice_in_dim(rows, seq_at * own, own, 0)
    give = lax.dynamic_slice_in_dim(rows, (1 - seq_at) * own, own, 0)
    in_grad = ordered(keep, swap(give), seq_at, 1)
    own_table = lax.dynamic_slice_in_dim(table, seq_at * own, own, 0)
    own_ids = lax.dynamic_slice_in_dim(route_ids, seq_at * own, own, 0)
    of_expert = jnp.sum(
        jnp.where(own_table, back_score.astype(F32)[None, :], 0.0).reshape(own, experts, capacity),
        axis=2,
    )
    same = own_ids[:, :, None] == jnp.arange(experts, dtype=jnp.int32)
    weight_grad = jnp.sum(jnp.where(same, of_expert[:, None, :], 0.0), axis=2)
    return in_grad, weight_grad.astype(BF)


MESH = pl.DeviceIdType.MESH
PARTS = 4
PIECES = 2


def lanes(shape, axis):
    return lax.broadcasted_iota(jnp.int32, shape, axis).astype(F32)


def fdiv(value, by):
    return jnp.floor((value + 0.5) * (1.0 / by))


def ones(mask):
    return jnp.where(mask, 1.0, 0.0).astype(BF)

def pick4(table, i):
    i1, i0 = i // 2, lax.rem(i, 2)
    c0, c1, c2, c3 = table
    return c0 + (c1 - c0) * i0 + (c2 - c0) * i1 + (c3 - c2 - c1 + c0) * i1 * i0


VMEM1 = 50
VMEM2 = 16
SEND = ((2, 0, 3, 1), (1, 3, 2, 0), (2, 0, 1, 3), (1, 3, 0, 2))
COLLECT = ((3, 2, 1), (1, 2, 3), (1, 2, 3), (3, 2, 1))
WORK = ((0, 3, 1, 2), (1, 3, 0, 2), (2, 0, 3, 1), (3, 0, 2, 1))


def quad_in(order, z, i):
    return pick4([pick4(row, i) for row in order], z)


def xor2(a, b):
    a1, a0, b1, b0 = a // 2, lax.rem(a, 2), b // 2, lax.rem(b, 2)
    return 2 * (a1 + b1 - 2 * a1 * b1) + (a0 + b0 - 2 * a0 * b0)


def packed_rows(shape, axis, blk, cap):
    r = lanes(shape, axis)
    block = fdiv(r, blk)
    part = fdiv(r - block * blk, cap)
    return block, part, r - block * blk - part * cap


def permutation(grp, blk, cap):
    a0, b0, p0 = packed_rows((grp, grp), 0, blk, cap)
    return ones(lanes((grp, grp), 1) == b0 * blk + a0 * cap + p0)


def step_kernel(
    n, cap, og, ids_hbm, wt_hbm, gp_hbm, up_hbm, wg_hbm, wu_hbm, wd_hbm,
    zol, zpl, home_out, wmat, wgrad,
    ids_ref, wt_ref, gp_ref, up_ref, wgu, wd, tok, sel, snd, rxo, rxp, pout, pin, snd2, zo, zp,
    vbuf, wbuf, home, gbuf, scs, sci, sco, scr, perm_ref,
    l_in, l_tok, s_tok, r_tok, l_w, s_d, r_d, s_f, r_f, s_p, r_p, s_s, r_s, s_b, r_b, s_c, r_c,
    s_g, r_g, l_o, l_n,
):
    me = lax.axis_index("expert")
    s = lax.axis_index("seq")
    o = 1 - s
    own, width = og.shape
    half = width // 2
    slots = n * cap
    blk = PARTS * cap
    grp = PARTS * blk
    rows = PARTS * cap
    qw = half // PARTS
    pw = half // PIECES
    hidden = wd_hbm.shape[0]
    quads = n // PARTS
    zat = me // PARTS
    tokens = 2 * own
    jat = lax.rem(me, PARTS)
    peers = [xor2(jat, r) for r in range(PARTS)]

    inputs = [
        pltpu.make_async_copy(ids_hbm, ids_ref, l_in.at[0]),
        pltpu.make_async_copy(wt_hbm, wt_ref, l_in.at[1]),
        pltpu.make_async_copy(gp_hbm, gp_ref, l_in.at[2]),
        pltpu.make_async_copy(up_hbm, up_ref, l_in.at[3]),
    ]
    inputs[0].start()
    barrier = pltpu.get_barrier_semaphore()
    pl.semaphore_signal(barrier, inc=1, device_id=(me, o), device_id_type=MESH)

    def greet(i, c):
        pl.semaphore_signal(
            barrier, inc=1, device_id=(lax.rem(me + i, n), s), device_id_type=MESH
        )
        return c

    lax.fori_loop(1, n, greet, 0)

    base = pl.multiple_of(s * half, 128)
    obase = pl.multiple_of(o * half, 128)
    mine = pl.multiple_of(s * own, 128)

    def remote(src, dst, ss, rs, dev):
        return pltpu.make_async_remote_copy(
            src_ref=src, dst_ref=dst, send_sem=ss, recv_sem=rs, device_id=dev, device_id_type=MESH
        )

    def tok_at(q):
        return tok.at[pl.ds(pl.multiple_of(q * tokens + mine, 16), own), :]

    def tok_local(q):
        cols = pl.ds(pl.multiple_of(base + q * qw, 128), qw)
        return pltpu.make_async_copy(og.at[:, cols], tok_at(q), l_tok)

    def tok_copy(q):
        cols = pl.ds(pl.multiple_of(obase + q * qw, 128), qw)
        return remote(og.at[:, cols], tok_at(q), s_tok, r_tok, (me, o))

    all_own = og.at[:, pl.ds(0, half)]
    all_tok = tok.at[pl.ds(0, PARTS * own), :]
    tok_all = remote(all_own, all_tok, s_tok, r_tok, (me, o))

    for q in range(PARTS):
        tok_local(q).start()
    for load in inputs[1:]:
        load.start()

    pl.semaphore_wait(barrier, n)
    for q in range(PARTS):
        tok_copy(q).start()

    inputs[0].wait()
    ids = jnp.transpose(ids_ref[...])
    e_lane = lax.broadcasted_iota(jnp.int32, (tokens, n), 1)
    hit = jnp.zeros((tokens, n), F32)
    for k in range(ids_ref.shape[0]):
        hit = jnp.where(ids[:, k : k + 1] == e_lane, 1.0, hit)
    tri = ones(lanes((tokens, tokens), 1) < lanes((tokens, tokens), 0))
    pos = dot(tri, hit.astype(BF), NN)
    v = jnp.where((hit > 0.5) & (pos < cap - 0.5), pos, 255.0)
    vbuf[...] = v
    vb = v.astype(BF)

    perm_ref[...] = permutation(grp, blk, cap)
    r_block, r_part, r_place = packed_rows((grp, tokens), 0, blk, cap)
    pick_block = packed_rows((grp, n), 0, blk, cap)[0]

    def build(quad, carry):
        pick = ones(pick_block + (quad * PARTS).astype(F32) == lanes((grp, n), 1))
        found = dot(pick, vb, NT) == r_place
        at = pl.ds(pl.multiple_of(quad * grp, 16), grp)
        for q in range(PARTS):
            sel[at, q * tokens : (q + 1) * tokens] = ones(found & (r_part == float(q)))
        return carry

    lax.fori_loop(0, quads, build, 0)

    def d_copy(dest):
        at = pl.multiple_of(dest * blk, 16)
        to = pl.multiple_of(me * blk, 16)
        return remote(
            snd.at[pl.ds(at, blk), :], rxo.at[pl.ds(to, blk), :], s_d, r_d.at[me], (dest, s)
        )

    def d_wait(src):
        at = pl.multiple_of(src * blk, 16)
        return remote(
            snd.at[pl.ds(at, blk), :], rxo.at[pl.ds(at, blk), :], s_d, r_d.at[src], (src, s)
        )

    def f_copy(src):
        at = pl.multiple_of(src * blk, 16)
        return remote(
            rxo.at[pl.ds(at, blk), :], rxp.at[pl.ds(at, blk), :], s_f, r_f.at[src // PARTS], (me, o)
        )

    def f_all(quad):
        at = pl.ds(pl.multiple_of(quad * grp, 16), grp)
        return remote(rxo.at[at, :], rxp.at[at, :], s_f, r_f.at[quad], (me, o))

    def own_copy():
        at = pl.multiple_of(me * blk, 16)
        return remote(
            snd.at[pl.ds(at, blk), :], rxp.at[pl.ds(at, blk), :], s_f, r_f.at[zat], (me, o)
        )

    pltpu.make_async_copy(all_own, all_tok, l_tok).wait()
    tok_all.wait_recv()

    def dispatch(i, carry):
        quad = quad_in(SEND, zat, i)
        at = pl.ds(pl.multiple_of(quad * grp, 16), grp)
        snd[at, :] = dot(sel[at, :], tok[...], NN).astype(BF)
        for j in peers:
            dest = quad * PARTS + j

            @pl.when(dest != me)
            def _():
                d_copy(dest).start()

            @pl.when(dest == me)
            def _():
                here = pl.ds(pl.multiple_of(me * blk, 16), blk)
                rxo[here, :] = snd[here, :]
                own_copy().start()

        return carry

    lax.fori_loop(0, quads, dispatch, 0)
    loads = [
        pltpu.make_async_copy(wd_hbm, wd, l_w.at[0]),
        pltpu.make_async_copy(wg_hbm, wgu.at[:, :hidden], l_w.at[1]),
        pltpu.make_async_copy(wu_hbm, wgu.at[:, hidden:], l_w.at[2]),
    ]
    for load in loads:
        load.start()

    for load in inputs[1:]:
        load.wait()
    my_ids = jnp.transpose(ids_ref[:, pl.ds(mine, own)].astype(F32))
    my_wts = jnp.transpose(wt_ref[:, pl.ds(mine, own)])
    my_v = vbuf[pl.ds(mine, own), :].astype(BF)
    my_lane = lanes((own, n), 1)
    wte = jnp.zeros((own, n), F32)
    for k in range(ids_ref.shape[0]):
        wte = jnp.where(my_ids[:, k : k + 1] == my_lane, my_wts[:, k : k + 1], wte)
    hi = wte.astype(BF)
    lo = (wte - hi.astype(F32)).astype(BF)

    c = lanes((own, slots), 1)
    place = c - cap * fdiv(c, cap)
    ce = fdiv(lanes((n, slots), 1), cap)
    group = fdiv(ce, PARTS)
    expert = ce - PARTS * group
    for g, quad in enumerate([xor2(zat, k) for k in range(quads)]):
        expert = jnp.where(group == float(g), expert + (quad * PARTS).astype(F32), expert)
    expand = ones(expert == lanes((n, slots), 0))
    taken = dot(my_v, expand, NN) == place
    wbuf[:own, :] = jnp.where(taken, dot(hi, expand, NN), 0.0).astype(BF)
    wbuf[own:, :] = jnp.where(taken, dot(lo, expand, NN), 0.0).astype(BF)
    w_out = pltpu.make_async_copy(wbuf, wmat, l_o.at[0])
    w_out.start()

    def p_copy(i, h):
        return remote(
            pout.at[i, h], pin.at[i, h], s_p, r_p.at[i * PIECES + h], (me, o)
        )

    def sc_copy(i):
        return remote(scs.at[i], sci.at[i], s_s, r_s.at[i], (me, o))

    def back_at(quad, j):
        return pl.multiple_of((xor2(zat, quad) - 1) * grp + j * blk, 16)

    def far_copy(quad, j):
        dest = quad * PARTS + j
        at = pl.multiple_of(dest * blk, 16)
        return remote(
            snd2.at[pl.ds(at, blk), :], zol.at[pl.ds(back_at(quad, jat), blk), :],
            s_b, r_b.at[me], (dest, s),
        )

    def far_wait(quad, j):
        src = quad * PARTS + j
        at = pl.multiple_of(src * blk, 16)
        return remote(
            snd2.at[pl.ds(at, blk), :], zol.at[pl.ds(back_at(quad, j), blk), :],
            s_b, r_b.at[src], (src, s),
        )

    def h_copy(quad, j):
        src = quad * PARTS + j
        at = back_at(quad, j)
        return remote(
            zol.at[pl.ds(at, blk), :], zpl.at[pl.ds(at, blk), :], s_g, r_g.at[src // PARTS], (me, o)
        )

    def b_copy(dest):
        at = pl.multiple_of(dest * blk, 16)
        to = pl.multiple_of(jat * blk, 16)
        return remote(
            snd2.at[pl.ds(at, blk), :], zo.at[pl.ds(to, blk), :], s_b, r_b.at[me], (dest, s)
        )

    def b_wait(j):
        src = zat * PARTS + j
        at = pl.multiple_of(src * blk, 16)
        to = pl.multiple_of(j * blk, 16)
        return remote(
            snd2.at[pl.ds(at, blk), :], zo.at[pl.ds(to, blk), :], s_b, r_b.at[src], (src, s)
        )

    def g_copy(j):
        src = zat * PARTS + j
        at = pl.multiple_of(j * blk, 16)
        return remote(
            zo.at[pl.ds(at, blk), :], zp.at[pl.ds(at, blk), :], s_g, r_g.at[src // PARTS], (me, o)
        )

    def own_back():
        at = pl.multiple_of(me * blk, 16)
        to = pl.multiple_of(jat * blk, 16)
        return remote(
            snd2.at[pl.ds(at, blk), :], zp.at[pl.ds(to, blk), :], s_g, r_g.at[zat], (me, o)
        )

    def c_copy(dest):
        at = pl.multiple_of(dest * 16, 16)
        to = pl.multiple_of(me * 16, 16)
        return remote(
            sco.at[pl.ds(at, 16), :], scr.at[pl.ds(to, 16), :], s_c, r_c, (dest, s)
        )

    c_rows = pl.ds(0, (n - 1) * 16)
    c_all = remote(sco.at[c_rows, :], scr.at[c_rows, :], s_c, r_c, (me, o))

    def work(i, carry):
        quad = quad_in(WORK, zat, i)
        packed = pl.ds(pl.multiple_of(quad * grp, 16), grp)
        slot_at = pl.ds(pl.multiple_of(quad * rows, 16), rows)
        for j in peers:
            src = quad * PARTS + j

            @pl.when(src != me)
            def _():
                d_wait(src).wait_recv()
                f_copy(src).start()

        @pl.when(i == 0)
        def _():
            loads[0].wait()

        perm = perm_ref[...]

        def contract(got, start):
            total = jnp.zeros((rows, hidden), F32)
            for q in range(0, PARTS, 2):
                x = jnp.concatenate([got[p * rows : (p + 1) * rows] for p in (q, q + 1)], axis=1)
                cols = pl.ds(pl.multiple_of(start + q * qw, 128), 2 * qw)
                total = total + dot(x, wd[:, cols], NT)
            return total

        grad = contract(dot(perm, rxo[packed, :], NN).astype(BF), base)
        f_all(quad).wait_recv()
        grad = grad + contract(dot(perm, rxp[packed, :], NN).astype(BF), obase)
        active, slope = silu_parts(gp_ref[slot_at, :].astype(F32))
        up = up_ref[slot_at, :].astype(F32)
        ud_v = grad * active
        diffs = jnp.concatenate([(grad * up * slope).astype(BF), ud_v.astype(BF)], axis=1)
        score = jnp.sum(ud_v * up, axis=1, keepdims=True)
        scs[i] = jnp.broadcast_to(score, (rows, 128)).astype(BF)
        sc_copy(i).start()

        @pl.when(i == 0)
        def _():
            loads[1].wait()
            loads[2].wait()

        def part(start):
            at = pl.ds(pl.multiple_of(start, 128), pw)
            return dot(diffs, wgu[at, :], NT).astype(BF)

        for h in range(PIECES):
            pout[i, h] = part(obase + h * pw)
            p_copy(i, h).start()
        kept = []
        for h in range(PIECES):
            value = part(base + h * pw).astype(F32)
            p_copy(i, h).wait_recv()
            value = (value + pin[i, h].astype(F32)).astype(BF)
            kept += [value[:, at : at + qw] for at in range(0, pw, qw)]
        snd2[packed, :] = dot(perm, jnp.concatenate(kept, axis=0), NN).astype(BF)
        sc_copy(i).wait_recv()
        total = (scs[i].astype(F32) + sci[i].astype(F32)).astype(BF)
        sr = lanes((PARTS * 16, rows), 0)
        se = fdiv(sr, 16)
        sp = sr - 16 * se
        spread = ones((lanes((PARTS * 16, rows), 1) == se * cap + sp) & (sp < cap - 0.5))
        sco[pl.ds(pl.multiple_of(quad * PARTS * 16, 16), PARTS * 16), :] = dot(spread, total, NN).astype(BF)
        for j in peers:
            dest = quad * PARTS + j

            @pl.when(dest != me)
            def _():
                c_copy(dest).start()

                @pl.when(quad == zat)
                def _():
                    b_copy(dest).start()

                @pl.when(quad != zat)
                def _():
                    far_copy(quad, j).start()

            @pl.when(dest == me)
            def _():
                here = pl.ds(pl.multiple_of(me * blk, 16), blk)
                zo[pl.ds(pl.multiple_of(jat * blk, 16), blk), :] = snd2[here, :]
                own_back().start()
                there = pl.ds(pl.multiple_of(me * 16, 16), 16)
                scr[there, :] = sco[there, :]

        return carry

    lax.fori_loop(0, quads, work, 0)

    def home_copy(h):
        return pltpu.make_async_copy(home.at[h], home_out.at[h], l_n.at[h])

    def unpack(h, z):
        got = dot(perm_ref[...], z[...], NN).astype(BF)
        for q in range(PARTS):
            home[h, q] = got[q * rows : (q + 1) * rows]
        home_copy(h).start()

    for j in peers[1:]:
        b_wait(j).wait_recv()
        g_copy(j).start()
    unpack(0, zo)
    remote(zo, zp, s_g, r_g.at[zat], (me, o)).wait_recv()
    unpack(1, zp)

    most = pl.ds(0, (n - 1) * blk)
    remote(snd.at[most, :], rxo.at[most, :], s_d, r_d.at[me], (me, o)).wait_send()
    remote(rxo, rxp, s_f, r_f.at[zat], (me, o)).wait_send()
    tok_all.wait_send()
    remote(scs, sci, s_s, r_s.at[0], (me, o)).wait_send()
    remote(pout, pin, s_p, r_p.at[0], (me, o)).wait_send()
    w_out.wait()

    others = [xor2(zat, pick4([row[i] for row in COLLECT], zat)) for i in range(quads - 1)]
    for quad in others:
        for j in peers:
            far_wait(quad, j).wait_recv()
            h_copy(quad, j).start()

    c_all.wait_recv()
    wide = n * 16
    wc = lanes((own, wide), 1)
    we = fdiv(wc, 16)
    spot = dot(my_v, ones(fdiv(lanes((n, wide), 1), 16) == lanes((n, wide), 0)), NN) == wc - 16 * we
    acc = jnp.zeros((own, 128), F32)
    for k in range(ids_ref.shape[0]):
        mask = ones(spot & (we == my_ids[:, k : k + 1]))
        acc = jnp.where(lanes((own, 128), 1) == k, dot(mask, scr[...], NN), acc)
    gbuf[...] = jnp.transpose(acc)[: gbuf.shape[0]]
    g_out = pltpu.make_async_copy(gbuf, wgrad, l_o.at[1])
    g_out.start()

    remote(snd2.at[most, :], rxo.at[most, :], s_b, r_b.at[me], (me, o)).wait_send()
    c_all.wait_send()
    for h in range(2):
        home_copy(h).wait()
    g_out.wait()
    for k in range(1, quads):
        at = pl.ds((k - 1) * grp, grp)
        remote(zol.at[at, :], zpl.at[at, :], s_g, r_g.at[xor2(zat, k)], (me, o)).wait_recv()
    remote(rxo, rxp, s_g, r_g.at[zat], (me, o)).wait_send()


def finish_kernel(cap, zol, zpl, home, w_ref, g_ref, out, gout, ob, s_out):
    s = lax.axis_index("seq")
    own = out.shape[0]
    half = out.shape[1] // 2
    qw = half // PARTS
    blk = PARTS * cap
    grp = PARTS * blk
    rows = PARTS * cap
    gout[...] = g_ref[...].astype(BF)
    perm = permutation(grp, blk, cap)
    stores = []
    for h, far in enumerate((zol, zpl)):
        start = s * half if h == 0 else (1 - s) * half
        got = [
            dot(perm, far[at : at + grp, :], NN).astype(BF) for at in range(0, far.shape[0], grp)
        ]
        for q in range(PARTS):
            z = jnp.concatenate([home[h, q]] + [g[q * rows : (q + 1) * rows] for g in got], axis=0)
            both = dot(w_ref[...], z, NN)
            ob[h, q] = (both[:own] + both[own:]).astype(BF)
            copy = pltpu.make_async_copy(
                ob.at[h, q], out.at[:, pl.ds(pl.multiple_of(start + q * qw, 128), qw)],
                s_out.at[h * PARTS + q],
            )
            copy.start()
            stores.append(copy)
    for copy in stores:
        copy.wait()


def scratch(n, cap, own, width, hidden, topk):
    half = width // 2
    slots = n * cap
    big = PARTS * slots
    qw = half // PARTS
    quads = n // PARTS
    rows = PARTS * cap
    grp = PARTS * rows
    vm, dma = pltpu.VMEM, pltpu.SemaphoreType.DMA
    pw = half // PIECES
    return [
        vm((topk, 2 * own), jnp.int32), vm((topk, 2 * own), F32), vm((slots, hidden), BF), vm((slots, hidden), BF),
        vm((width, 2 * hidden), BF), vm((hidden, width), BF),
        vm((PARTS * 2 * own, qw), BF), vm((big, PARTS * 2 * own), BF), vm((big, qw), BF),
        vm((big, qw), BF), vm((big, qw), BF),
        vm((quads, PIECES, rows, pw), BF), vm((quads, PIECES, rows, pw), BF), vm((big, qw), BF),
        vm((grp, qw), BF), vm((grp, qw), BF),
        vm((2 * own, n), F32), vm((2 * own, slots), BF), vm((2, PARTS, rows, qw), BF), vm((topk, own), F32),
        vm((quads, rows, 128), BF), vm((quads, rows, 128), BF), vm((n * 16, 128), BF),
        vm((n * 16, 128), BF), vm((grp, grp), BF),
        dma((4,)), dma, dma, dma, dma((3,)),
        dma, dma((n,)), dma, dma((quads,)), dma, dma((quads * PIECES,)), dma, dma((quads,)),
        dma, dma((n,)), dma, dma, dma, dma((quads,)), dma((2,)), dma((2,)),
    ]


def kernel_fits(n, cap, own, width, hidden):
    half = width // 2
    slots = n * cap
    size = 2 * (3 * width * hidden + 10 * slots * half + 4 * own * half)
    aligned = (PARTS * cap) % 16 == 0 and half % (PARTS * 128) == 0 and half % 512 == 0
    return n == PARTS * 4 and cap <= 16 and aligned and own == 128 and size < 48 * 2**20


def on_device(out_grad, route_ids, route_weights, gate_pre, up_pre, w_gate, w_up, w_down):
    n = lax.axis_size("expert")
    own, width = out_grad.shape
    slots, hidden = gate_pre.shape[1:]
    cap = slots // n
    topk = route_ids.shape[1]
    args = (out_grad, route_ids, route_weights, gate_pre, up_pre, w_gate, w_up, w_down)
    if not kernel_fits(n, cap, own, width, hidden):
        return on_device_xla(*args)
    half = width // 2
    qw = half // PARTS
    rows = PARTS * cap
    grp = PARTS * rows
    quads = n // PARTS
    anywhere = pl.BlockSpec(memory_space=pl.ANY)
    hbm = pl.BlockSpec(memory_space=pltpu.HBM)
    vmem = pl.BlockSpec(memory_space=pltpu.VMEM)
    operands = [
        pltpu.with_memory_space_constraint(x, pltpu.HBM)
        for x in (
            out_grad, route_ids.T, route_weights.T, gate_pre[0], up_pre[0], w_gate[0], w_up[0], w_down[0]
        )
    ]
    zol, zpl, home, wmat, wgrad = pl.pallas_call(
        functools.partial(step_kernel, n, cap),
        out_shape=(
            jax.ShapeDtypeStruct(((quads - 1) * grp, qw), BF),
            jax.ShapeDtypeStruct(((quads - 1) * grp, qw), BF),
            jax.ShapeDtypeStruct((2, PARTS, rows, qw), BF),
            jax.ShapeDtypeStruct((2 * own, slots), BF),
            jax.ShapeDtypeStruct((topk, own), F32),
        ),
        in_specs=[hbm] * 8,
        out_specs=(anywhere,) * 5,
        scratch_shapes=scratch(n, cap, own, width, hidden, topk),
        compiler_params=pltpu.CompilerParams(
            collective_id=0, has_side_effects=True, vmem_limit_bytes=VMEM1 * 2**20
        ),
        name="expert_step",
    )(
        *operands
    )
    in_grad, weight_grad = pl.pallas_call(
        functools.partial(finish_kernel, cap),
        out_shape=(
            jax.ShapeDtypeStruct((own, width), BF),
            jax.ShapeDtypeStruct((topk, own), BF),
        ),
        in_specs=[vmem] * 5,
        out_specs=(anywhere, vmem),
        scratch_shapes=[pltpu.VMEM((2, PARTS, own, qw), BF), pltpu.SemaphoreType.DMA((2 * PARTS,))],
        compiler_params=pltpu.CompilerParams(vmem_limit_bytes=VMEM2 * 2**20),
        name="combine",
    )(zol, zpl, home, wmat, wgrad)
    return in_grad, weight_grad.T


def solution(mesh):
    in_specs = (
        P(("expert", "seq"), None),
        P("expert", None),
        P("expert", None),
        P("expert", None, "seq"),
        P("expert", None, "seq"),
        P("expert", None, "seq"),
        P("expert", None, "seq"),
        P("expert", "seq", None),
    )
    out_specs = (P(("expert", "seq"), None), P(("expert", "seq"), None))
    return jax.shard_map(
        on_device, mesh=mesh, in_specs=in_specs, out_specs=out_specs, check_vma=False
    )
```

```python
import functools

import jax
import jax.numpy as jnp
from jax import lax
from jax.experimental import pallas as pl
from jax.experimental.pallas import tpu as pltpu
from jax.sharding import PartitionSpec as P

BF = jnp.bfloat16
F32 = jnp.float32
NT = (((1,), (1,)), ((), ()))
NN = (((1,), (0,)), ((), ()))
TN = (((0,), (0,)), ((), ()))


def silu_parts(value):
    sigma = jax.nn.sigmoid(value)
    return (value * sigma, sigma * (1.0 + value * (1.0 - sigma)))


def dot(a, b, dims):
    return lax.dot_general(a, b, dims, preferred_element_type=F32)


def swap(value):
    return lax.ppermute(value, "seq", [(0, 1), (1, 0)])


def ordered(mine, theirs, seq_at, axis):
    low = jnp.where(seq_at == 0, mine, theirs)
    high = jnp.where(seq_at == 0, theirs, mine)
    return jnp.concatenate([low, high], axis=axis)


def routing(ids, weights, experts, capacity):
    tokens = ids.shape[0]
    same = ids[:, :, None] == jnp.arange(experts, dtype=jnp.int32)
    hit = jnp.any(same, axis=1)
    weight = jnp.sum(jnp.where(same, weights[:, :, None], 0.0), axis=1)
    row = jnp.arange(tokens, dtype=jnp.int32)
    earlier = (row[None, :] < row[:, None]).astype(BF)
    position = dot(earlier, hit.astype(BF), NN)
    slot = jnp.where(hit, position, float(capacity))
    return slot, weight


def on_device_xla(out_grad, route_ids, route_weights, gate_pre, up_pre, w_gate, w_up, w_down):
    n_expert = lax.axis_size("expert")
    seq_at = lax.axis_index("seq")
    own, width = out_grad.shape
    half = width // 2
    experts = n_expert
    slots = gate_pre.shape[1]
    capacity = slots // n_expert
    slot, weight = routing(route_ids, route_weights, experts, capacity)
    table = (slot[:, :, None] == jnp.arange(capacity, dtype=F32)).reshape(2 * own, slots)
    w_all = jnp.broadcast_to(weight[:, :, None], (2 * own, experts, capacity)).reshape(2 * own, slots)
    w_all = jnp.where(table, w_all, 0.0)
    w_hi = w_all.astype(BF)
    w_lo = (w_all - w_hi.astype(F32)).astype(BF)
    mine = lax.dynamic_slice_in_dim(out_grad, seq_at * half, half, 1)
    other = lax.dynamic_slice_in_dim(out_grad, (1 - seq_at) * half, half, 1)
    tokens = ordered(mine, swap(other), seq_at, 0)
    outgoing = dot(table.astype(BF), tokens, TN).astype(BF).reshape(experts, capacity, half)
    received = lax.all_to_all(outgoing, "expert", split_axis=0, concat_axis=0, tiled=True)
    received = received.reshape(slots, half)
    slot_grad = ordered(received, swap(received), seq_at, 1)
    hidden_grad = dot(slot_grad, w_down[0], NT)
    active, slope = silu_parts(gate_pre[0].astype(F32))
    up_part = up_pre[0].astype(F32)
    score = jnp.sum(hidden_grad * active * up_part, axis=1).astype(BF)
    gate_diff = (hidden_grad * up_part * slope).astype(BF)
    up_diff = (hidden_grad * active).astype(BF)
    part = (dot(gate_diff, w_gate[0], NT) + dot(up_diff, w_up[0], NT)).astype(BF)
    score = lax.optimization_barrier(score)
    part = lax.optimization_barrier(part)
    keep = lax.dynamic_slice_in_dim(part, seq_at * half, half, 1)
    give = lax.dynamic_slice_in_dim(part, (1 - seq_at) * half, half, 1)
    total = (keep.astype(F32) + swap(give).astype(F32)).astype(BF)
    total_score = (score.astype(F32) + swap(score).astype(F32)).astype(BF)
    back = lax.all_to_all(
        total.reshape(n_expert, capacity, half), "expert", split_axis=0, concat_axis=0, tiled=True
    ).reshape(slots, half)
    back_score = lax.all_to_all(
        total_score.reshape(n_expert, capacity), "expert", split_axis=0, concat_axis=0, tiled=True
    ).reshape(slots)
    rows = (dot(w_hi, back, NN) + dot(w_lo, back, NN)).astype(BF)
    keep = lax.dynamic_slice_in_dim(rows, seq_at * own, own, 0)
    give = lax.dynamic_slice_in_dim(rows, (1 - seq_at) * own, own, 0)
    in_grad = ordered(keep, swap(give), seq_at, 1)
    own_table = lax.dynamic_slice_in_dim(table, seq_at * own, own, 0)
    own_ids = lax.dynamic_slice_in_dim(route_ids, seq_at * own, own, 0)
    of_expert = jnp.sum(
        jnp.where(own_table, back_score.astype(F32)[None, :], 0.0).reshape(own, experts, capacity),
        axis=2,
    )
    same = own_ids[:, :, None] == jnp.arange(experts, dtype=jnp.int32)
    weight_grad = jnp.sum(jnp.where(same, of_expert[:, None, :], 0.0), axis=2)
    return in_grad, weight_grad.astype(BF)


MESH = pl.DeviceIdType.MESH
PARTS = 4
PIECES = 2


def lanes(shape, axis):
    return lax.broadcasted_iota(jnp.int32, shape, axis).astype(F32)


def fdiv(value, by):
    return jnp.floor((value + 0.5) * (1.0 / by))


def ones(mask):
    return jnp.where(mask, 1.0, 0.0).astype(BF)

def pick4(table, i):
    i1, i0 = i // 2, lax.rem(i, 2)
    c0, c1, c2, c3 = table
    return c0 + (c1 - c0) * i0 + (c2 - c0) * i1 + (c3 - c2 - c1 + c0) * i1 * i0


VMEM1 = 46
VMEM2 = 16
SEND = ((2, 0, 3, 1), (1, 3, 2, 0), (2, 0, 1, 3), (1, 3, 0, 2))
COLLECT = ((3, 2, 1), (1, 2, 3), (1, 2, 3), (3, 2, 1))
WORK = ((0, 3, 1, 2), (1, 3, 0, 2), (2, 0, 3, 1), (3, 0, 2, 1))


def quad_in(order, z, i):
    return pick4([pick4(row, i) for row in order], z)


def xor2(a, b):
    a1, a0, b1, b0 = a // 2, lax.rem(a, 2), b // 2, lax.rem(b, 2)
    return 2 * (a1 + b1 - 2 * a1 * b1) + (a0 + b0 - 2 * a0 * b0)


def packed_rows(shape, axis, blk, cap):
    r = lanes(shape, axis)
    block = fdiv(r, blk)
    part = fdiv(r - block * blk, cap)
    return block, part, r - block * blk - part * cap


def permutation(grp, blk, cap):
    a0, b0, p0 = packed_rows((grp, grp), 0, blk, cap)
    return ones(lanes((grp, grp), 1) == b0 * blk + a0 * cap + p0)


def step_kernel(
    n, cap, og, ids_hbm, wt_hbm, gp_hbm, up_hbm, wg_hbm, wu_hbm, wd_hbm,
    zlo, zlp, acc_out, wlast, wgrad,
    ids_ref, wt_ref, gp_ref, up_ref, wgu, wd, tok, sel, snd, rxo, rxp, pout, pin, snd2, zo, zp, zol, zpl,
    vbuf, wk, acc, gbuf, scs, sci, sco, scr, perm_ref,
    l_in, l_tok, s_tok, r_tok, l_w, s_d, r_d, s_f, r_f, s_p, r_p, s_s, r_s, s_b, r_b, s_c, r_c,
    s_g, r_g, l_o, l_a,
):
    me = lax.axis_index("expert")
    s = lax.axis_index("seq")
    o = 1 - s
    own, width = og.shape
    half = width // 2
    slots = n * cap
    blk = PARTS * cap
    grp = PARTS * blk
    rows = PARTS * cap
    qw = half // PARTS
    pw = half // PIECES
    hidden = wd_hbm.shape[0]
    quads = n // PARTS
    zat = me // PARTS
    tokens = 2 * own
    jat = lax.rem(me, PARTS)
    peers = [xor2(jat, r) for r in range(PARTS)]

    inputs = [
        pltpu.make_async_copy(ids_hbm, ids_ref, l_in.at[0]),
        pltpu.make_async_copy(wt_hbm, wt_ref, l_in.at[1]),
        pltpu.make_async_copy(gp_hbm, gp_ref, l_in.at[2]),
        pltpu.make_async_copy(up_hbm, up_ref, l_in.at[3]),
    ]
    inputs[0].start()
    barrier = pltpu.get_barrier_semaphore()
    pl.semaphore_signal(barrier, inc=1, device_id=(me, o), device_id_type=MESH)

    def greet(i, c):
        pl.semaphore_signal(
            barrier, inc=1, device_id=(lax.rem(me + i, n), s), device_id_type=MESH
        )
        return c

    lax.fori_loop(1, n, greet, 0)

    base = pl.multiple_of(s * half, 128)
    obase = pl.multiple_of(o * half, 128)
    mine = pl.multiple_of(s * own, 128)

    def remote(src, dst, ss, rs, dev):
        return pltpu.make_async_remote_copy(
            src_ref=src, dst_ref=dst, send_sem=ss, recv_sem=rs, device_id=dev, device_id_type=MESH
        )

    def tok_at(q):
        return tok.at[pl.ds(pl.multiple_of(q * tokens + mine, 16), own), :]

    def tok_local(q):
        cols = pl.ds(pl.multiple_of(base + q * qw, 128), qw)
        return pltpu.make_async_copy(og.at[:, cols], tok_at(q), l_tok)

    def tok_copy(q):
        cols = pl.ds(pl.multiple_of(obase + q * qw, 128), qw)
        return remote(og.at[:, cols], tok_at(q), s_tok, r_tok, (me, o))

    all_own = og.at[:, pl.ds(0, half)]
    all_tok = tok.at[pl.ds(0, PARTS * own), :]
    tok_all = remote(all_own, all_tok, s_tok, r_tok, (me, o))

    for q in range(PARTS):
        tok_local(q).start()
    for load in inputs[1:]:
        load.start()

    pl.semaphore_wait(barrier, n)
    for q in range(PARTS):
        tok_copy(q).start()

    inputs[0].wait()
    ids = jnp.transpose(ids_ref[...])
    e_lane = lax.broadcasted_iota(jnp.int32, (tokens, n), 1)
    hit = jnp.zeros((tokens, n), F32)
    for k in range(ids_ref.shape[0]):
        hit = jnp.where(ids[:, k : k + 1] == e_lane, 1.0, hit)
    tri = ones(lanes((tokens, tokens), 1) < lanes((tokens, tokens), 0))
    pos = dot(tri, hit.astype(BF), NN)
    v = jnp.where((hit > 0.5) & (pos < cap - 0.5), pos, 255.0)
    vbuf[...] = v
    vb = v.astype(BF)

    perm_ref[...] = permutation(grp, blk, cap)
    r_block, r_part, r_place = packed_rows((grp, tokens), 0, blk, cap)
    pick_block = packed_rows((grp, n), 0, blk, cap)[0]

    def build(quad, carry):
        pick = ones(pick_block + (quad * PARTS).astype(F32) == lanes((grp, n), 1))
        found = dot(pick, vb, NT) == r_place
        at = pl.ds(pl.multiple_of(quad * grp, 16), grp)
        for q in range(PARTS):
            sel[at, q * tokens : (q + 1) * tokens] = ones(found & (r_part == float(q)))
        return carry

    lax.fori_loop(0, quads, build, 0)

    def d_copy(dest):
        at = pl.multiple_of(dest * blk, 16)
        to = pl.multiple_of(me * blk, 16)
        return remote(
            snd.at[pl.ds(at, blk), :], rxo.at[pl.ds(to, blk), :], s_d, r_d.at[me], (dest, s)
        )

    def d_wait(src):
        at = pl.multiple_of(src * blk, 16)
        return remote(
            snd.at[pl.ds(at, blk), :], rxo.at[pl.ds(at, blk), :], s_d, r_d.at[src], (src, s)
        )

    def f_copy(src):
        at = pl.multiple_of(src * blk, 16)
        return remote(
            rxo.at[pl.ds(at, blk), :], rxp.at[pl.ds(at, blk), :], s_f, r_f.at[src // PARTS], (me, o)
        )

    def f_all(quad):
        at = pl.ds(pl.multiple_of(quad * grp, 16), grp)
        return remote(rxo.at[at, :], rxp.at[at, :], s_f, r_f.at[quad], (me, o))

    def own_copy():
        at = pl.multiple_of(me * blk, 16)
        return remote(
            snd.at[pl.ds(at, blk), :], rxp.at[pl.ds(at, blk), :], s_f, r_f.at[zat], (me, o)
        )

    pltpu.make_async_copy(all_own, all_tok, l_tok).wait()
    tok_all.wait_recv()

    def dispatch(i, carry):
        quad = quad_in(SEND, zat, i)
        at = pl.ds(pl.multiple_of(quad * grp, 16), grp)
        snd[at, :] = dot(sel[at, :], tok[...], NN).astype(BF)
        for j in peers:
            dest = quad * PARTS + j

            @pl.when(dest != me)
            def _():
                d_copy(dest).start()

            @pl.when(dest == me)
            def _():
                here = pl.ds(pl.multiple_of(me * blk, 16), blk)
                rxo[here, :] = snd[here, :]
                own_copy().start()

        return carry

    lax.fori_loop(0, quads, dispatch, 0)
    loads = [
        pltpu.make_async_copy(wd_hbm, wd, l_w.at[0]),
        pltpu.make_async_copy(wg_hbm, wgu.at[:, :hidden], l_w.at[1]),
        pltpu.make_async_copy(wu_hbm, wgu.at[:, hidden:], l_w.at[2]),
    ]
    for load in loads:
        load.start()

    for load in inputs[1:]:
        load.wait()
    my_ids = jnp.transpose(ids_ref[:, pl.ds(mine, own)].astype(F32))
    my_wts = jnp.transpose(wt_ref[:, pl.ds(mine, own)])
    my_v = vbuf[pl.ds(mine, own), :].astype(BF)
    my_lane = lanes((own, n), 1)
    wte = jnp.zeros((own, n), F32)
    for k in range(ids_ref.shape[0]):
        wte = jnp.where(my_ids[:, k : k + 1] == my_lane, my_wts[:, k : k + 1], wte)
    hi = wte.astype(BF)
    lo = (wte - hi.astype(F32)).astype(BF)

    others = [xor2(zat, pick4([row[i] for row in COLLECT], zat)) for i in range(quads - 1)]
    order = [zat] + others
    place = packed_rows((own, 2 * rows), 1, rows, cap)[2]
    upper = lanes((own, 2 * rows), 1) < rows - 0.5
    e_half, e_block, _ = packed_rows((n, 2 * rows), 1, rows, cap)
    for i, quad in enumerate(order):
        expert = e_block + (quad * PARTS).astype(F32)
        expand = ones(expert == lanes((n, 2 * rows), 0))
        taken = dot(my_v, expand, NN) == place
        both = jnp.where(upper, dot(hi, expand, NN), dot(lo, expand, NN))
        wk[i] = jnp.where(taken, both, 0.0).astype(BF)
    w_out = pltpu.make_async_copy(wk.at[quads - 1], wlast, l_o.at[0])
    w_out.start()

    def p_copy(i, h):
        return remote(
            pout.at[i, h], pin.at[i, h], s_p, r_p.at[i * PIECES + h], (me, o)
        )

    def sc_copy(i):
        return remote(scs.at[i], sci.at[i], s_s, r_s.at[i], (me, o))

    def back_at(quad, j):
        return pl.multiple_of((xor2(zat, quad) - 1) * grp + j * blk, 16)

    def far_copy(quad, j):
        dest = quad * PARTS + j
        at = pl.multiple_of(dest * blk, 16)
        return remote(
            snd2.at[pl.ds(at, blk), :], zol.at[pl.ds(back_at(quad, jat), blk), :],
            s_b, r_b.at[me], (dest, s),
        )

    def last_copy(quad, j):
        dest = quad * PARTS + j
        at = pl.multiple_of(dest * blk, 16)
        to = pl.multiple_of(jat * blk, 16)
        return remote(
            snd2.at[pl.ds(at, blk), :], zlo.at[pl.ds(to, blk), :], s_b, r_b.at[me], (dest, s)
        )

    def last_wait(quad, j):
        src = quad * PARTS + j
        at = pl.multiple_of(src * blk, 16)
        to = pl.multiple_of(j * blk, 16)
        return remote(
            snd2.at[pl.ds(at, blk), :], zlo.at[pl.ds(to, blk), :], s_b, r_b.at[src], (src, s)
        )

    def last_share(quad, j):
        src = quad * PARTS + j
        at = pl.multiple_of(j * blk, 16)
        return remote(
            zlo.at[pl.ds(at, blk), :], zlp.at[pl.ds(at, blk), :], s_g, r_g.at[src // PARTS], (me, o)
        )

    def far_wait(quad, j):
        src = quad * PARTS + j
        at = pl.multiple_of(src * blk, 16)
        return remote(
            snd2.at[pl.ds(at, blk), :], zol.at[pl.ds(back_at(quad, j), blk), :],
            s_b, r_b.at[src], (src, s),
        )

    def h_copy(quad, j):
        src = quad * PARTS + j
        at = back_at(quad, j)
        return remote(
            zol.at[pl.ds(at, blk), :], zpl.at[pl.ds(at, blk), :], s_g, r_g.at[src // PARTS], (me, o)
        )

    def b_copy(dest):
        at = pl.multiple_of(dest * blk, 16)
        to = pl.multiple_of(jat * blk, 16)
        return remote(
            snd2.at[pl.ds(at, blk), :], zo.at[pl.ds(to, blk), :], s_b, r_b.at[me], (dest, s)
        )

    def b_wait(j):
        src = zat * PARTS + j
        at = pl.multiple_of(src * blk, 16)
        to = pl.multiple_of(j * blk, 16)
        return remote(
            snd2.at[pl.ds(at, blk), :], zo.at[pl.ds(to, blk), :], s_b, r_b.at[src], (src, s)
        )

    def g_copy(j):
        src = zat * PARTS + j
        at = pl.multiple_of(j * blk, 16)
        return remote(
            zo.at[pl.ds(at, blk), :], zp.at[pl.ds(at, blk), :], s_g, r_g.at[src // PARTS], (me, o)
        )

    def own_back():
        at = pl.multiple_of(me * blk, 16)
        to = pl.multiple_of(jat * blk, 16)
        return remote(
            snd2.at[pl.ds(at, blk), :], zp.at[pl.ds(to, blk), :], s_g, r_g.at[zat], (me, o)
        )

    def c_copy(dest):
        at = pl.multiple_of(dest * 16, 16)
        to = pl.multiple_of(me * 16, 16)
        return remote(
            sco.at[pl.ds(at, 16), :], scr.at[pl.ds(to, 16), :], s_c, r_c, (dest, s)
        )

    c_rows = pl.ds(0, (n - 1) * 16)
    c_all = remote(sco.at[c_rows, :], scr.at[c_rows, :], s_c, r_c, (me, o))

    def work(i, carry):
        quad = quad_in(WORK, zat, i)
        packed = pl.ds(pl.multiple_of(quad * grp, 16), grp)
        slot_at = pl.ds(pl.multiple_of(quad * rows, 16), rows)
        for j in peers:
            src = quad * PARTS + j

            @pl.when(src != me)
            def _():
                d_wait(src).wait_recv()
                f_copy(src).start()

        @pl.when(i == 0)
        def _():
            loads[0].wait()

        perm = perm_ref[...]

        def contract(got, start):
            total = jnp.zeros((rows, hidden), F32)
            for q in range(0, PARTS, 2):
                x = jnp.concatenate([got[p * rows : (p + 1) * rows] for p in (q, q + 1)], axis=1)
                cols = pl.ds(pl.multiple_of(start + q * qw, 128), 2 * qw)
                total = total + dot(x, wd[:, cols], NT)
            return total

        grad = contract(dot(perm, rxo[packed, :], NN).astype(BF), base)
        f_all(quad).wait_recv()
        grad = grad + contract(dot(perm, rxp[packed, :], NN).astype(BF), obase)
        active, slope = silu_parts(gp_ref[slot_at, :].astype(F32))
        up = up_ref[slot_at, :].astype(F32)
        ud_v = grad * active
        diffs = jnp.concatenate([(grad * up * slope).astype(BF), ud_v.astype(BF)], axis=1)
        score = jnp.sum(ud_v * up, axis=1, keepdims=True)
        scs[i] = jnp.broadcast_to(score, (rows, 128)).astype(BF)
        sc_copy(i).start()

        @pl.when(i == 0)
        def _():
            loads[1].wait()
            loads[2].wait()

        def part(start):
            at = pl.ds(pl.multiple_of(start, 128), pw)
            return dot(diffs, wgu[at, :], NT).astype(BF)

        for h in range(PIECES):
            pout[i, h] = part(obase + h * pw)
            p_copy(i, h).start()
        kept = []
        for h in range(PIECES):
            value = part(base + h * pw).astype(F32)
            p_copy(i, h).wait_recv()
            value = (value + pin[i, h].astype(F32)).astype(BF)
            kept += [value[:, at : at + qw] for at in range(0, pw, qw)]
        snd2[packed, :] = dot(perm, jnp.concatenate(kept, axis=0), NN).astype(BF)
        sc_copy(i).wait_recv()
        total = (scs[i].astype(F32) + sci[i].astype(F32)).astype(BF)
        sr = lanes((PARTS * 16, rows), 0)
        se = fdiv(sr, 16)
        sp = sr - 16 * se
        spread = ones((lanes((PARTS * 16, rows), 1) == se * cap + sp) & (sp < cap - 0.5))
        sco[pl.ds(pl.multiple_of(quad * PARTS * 16, 16), PARTS * 16), :] = dot(spread, total, NN).astype(BF)
        for j in peers:
            dest = quad * PARTS + j

            @pl.when(dest != me)
            def _():
                c_copy(dest).start()

                @pl.when(quad == zat)
                def _():
                    b_copy(dest).start()

                to_last = xor2(zat, quad) == pick4([row[-1] for row in COLLECT], quad)

                @pl.when((quad != zat) & to_last)
                def _():
                    last_copy(quad, j).start()

                @pl.when((quad != zat) & jnp.logical_not(to_last))
                def _():
                    far_copy(quad, j).start()

            @pl.when(dest == me)
            def _():
                here = pl.ds(pl.multiple_of(me * blk, 16), blk)
                zo[pl.ds(pl.multiple_of(jat * blk, 16), blk), :] = snd2[here, :]
                own_back().start()
                there = pl.ds(pl.multiple_of(me * 16, 16), 16)
                scr[there, :] = sco[there, :]

        return carry

    lax.fori_loop(0, quads, work, 0)

    def add(i, h, z, at):
        got = dot(perm_ref[...], z[at, :], NN).astype(BF)
        for q in range(PARTS):
            part = got[q * rows : (q + 1) * rows]
            value = dot(wk[i], jnp.concatenate([part, part], axis=0), NN)
            cols = slice(q * qw, (q + 1) * qw)
            acc[h, :, cols] = value if i == 0 else acc[h, :, cols] + value

    whole = pl.ds(0, grp)
    for j in peers[1:]:
        b_wait(j).wait_recv()
        g_copy(j).start()
    add(0, 0, zo, whole)
    remote(zo, zp, s_g, r_g.at[zat], (me, o)).wait_recv()
    add(0, 1, zp, whole)
    for i, quad in enumerate(others[:-1]):
        at = pl.ds(back_at(quad, 0), grp)
        for j in peers:
            far_wait(quad, j).wait_recv()
            h_copy(quad, j).start()
        add(i + 1, 0, zol, at)
        remote(zol.at[at, :], zpl.at[at, :], s_g, r_g.at[quad], (me, o)).wait_recv()
        add(i + 1, 1, zpl, at)
    a_out = pltpu.make_async_copy(acc, acc_out, l_a)
    a_out.start()

    most = pl.ds(0, (n - 1) * blk)
    remote(snd.at[most, :], rxo.at[most, :], s_d, r_d.at[me], (me, o)).wait_send()
    remote(rxo, rxp, s_f, r_f.at[zat], (me, o)).wait_send()
    tok_all.wait_send()
    remote(scs, sci, s_s, r_s.at[0], (me, o)).wait_send()
    remote(pout, pin, s_p, r_p.at[0], (me, o)).wait_send()
    w_out.wait()

    for j in peers:
        last_wait(others[-1], j).wait_recv()
        last_share(others[-1], j).start()
    c_all.wait_recv()
    wide = n * 16
    wc = lanes((own, wide), 1)
    we = fdiv(wc, 16)
    spot = dot(my_v, ones(fdiv(lanes((n, wide), 1), 16) == lanes((n, wide), 0)), NN) == wc - 16 * we
    found = jnp.zeros((own, 128), F32)
    for k in range(ids_ref.shape[0]):
        mask = ones(spot & (we == my_ids[:, k : k + 1]))
        found = jnp.where(lanes((own, 128), 1) == k, dot(mask, scr[...], NN), found)
    gbuf[...] = jnp.transpose(found)[: gbuf.shape[0]]
    g_out = pltpu.make_async_copy(gbuf, wgrad, l_o.at[1])
    g_out.start()

    remote(snd2.at[most, :], rxo.at[most, :], s_b, r_b.at[me], (me, o)).wait_send()
    c_all.wait_send()
    a_out.wait()
    g_out.wait()
    remote(zlo, zlp, s_g, r_g.at[others[-1]], (me, o)).wait_recv()
    remote(rxo, rxp, s_g, r_g.at[zat], (me, o)).wait_send()


def finish_kernel(cap, zlo, zlp, acc, w_ref, g_ref, out, gout, ob, gb, s_out, s_g):
    s = lax.axis_index("seq")
    own = out.shape[0]
    half = out.shape[1] // 2
    qw = half // PARTS
    blk = PARTS * cap
    grp = PARTS * blk
    rows = PARTS * cap
    gb[...] = g_ref[...].astype(BF)
    g_copy = pltpu.make_async_copy(gb, gout, s_g)
    g_copy.start()
    perm = permutation(grp, blk, cap)
    stores = []
    for h, far in enumerate((zlo, zlp)):
        start = s * half if h == 0 else (1 - s) * half
        got = dot(perm, far[...], NN).astype(BF)
        for q in range(PARTS):
            part = got[q * rows : (q + 1) * rows]
            value = dot(w_ref[...], jnp.concatenate([part, part], axis=0), NN)
            ob[h, q] = (acc[h, :, q * qw : (q + 1) * qw] + value).astype(BF)
            copy = pltpu.make_async_copy(
                ob.at[h, q], out.at[:, pl.ds(pl.multiple_of(start + q * qw, 128), qw)],
                s_out.at[h * PARTS + q],
            )
            copy.start()
            stores.append(copy)
    g_copy.wait()
    for copy in stores:
        copy.wait()


def scratch(n, cap, own, width, hidden, topk):
    half = width // 2
    slots = n * cap
    big = PARTS * slots
    qw = half // PARTS
    quads = n // PARTS
    rows = PARTS * cap
    grp = PARTS * rows
    vm, dma = pltpu.VMEM, pltpu.SemaphoreType.DMA
    pw = half // PIECES
    return [
        vm((topk, 2 * own), jnp.int32), vm((topk, 2 * own), F32), vm((slots, hidden), BF), vm((slots, hidden), BF),
        vm((width, 2 * hidden), BF), vm((hidden, width), BF),
        vm((PARTS * 2 * own, qw), BF), vm((big, PARTS * 2 * own), BF), vm((big, qw), BF),
        vm((big, qw), BF), vm((big, qw), BF),
        vm((quads, PIECES, rows, pw), BF), vm((quads, PIECES, rows, pw), BF), vm((big, qw), BF),
        vm((grp, qw), BF), vm((grp, qw), BF), vm(((quads - 1) * grp, qw), BF), vm(((quads - 1) * grp, qw), BF),
        vm((2 * own, n), F32), vm((quads, own, 2 * rows), BF), vm((2, own, half), F32), vm((topk, own), F32),
        vm((quads, rows, 128), BF), vm((quads, rows, 128), BF), vm((n * 16, 128), BF),
        vm((n * 16, 128), BF), vm((grp, grp), BF),
        dma((4,)), dma, dma, dma, dma((3,)),
        dma, dma((n,)), dma, dma((quads,)), dma, dma((quads * PIECES,)), dma, dma((quads,)),
        dma, dma((n,)), dma, dma, dma, dma((quads,)), dma((2,)), dma,
    ]


def kernel_fits(n, cap, own, width, hidden):
    half = width // 2
    slots = n * cap
    size = 2 * (3 * width * hidden + 10 * slots * half + 4 * own * half)
    aligned = (PARTS * cap) % 16 == 0 and half % (PARTS * 128) == 0 and half % 512 == 0
    return n == PARTS * 4 and cap <= 16 and aligned and own == 128 and size < 48 * 2**20


def on_device(out_grad, route_ids, route_weights, gate_pre, up_pre, w_gate, w_up, w_down):
    n = lax.axis_size("expert")
    own, width = out_grad.shape
    slots, hidden = gate_pre.shape[1:]
    cap = slots // n
    topk = route_ids.shape[1]
    args = (out_grad, route_ids, route_weights, gate_pre, up_pre, w_gate, w_up, w_down)
    if not kernel_fits(n, cap, own, width, hidden):
        return on_device_xla(*args)
    half = width // 2
    qw = half // PARTS
    rows = PARTS * cap
    grp = PARTS * rows
    quads = n // PARTS
    anywhere = pl.BlockSpec(memory_space=pl.ANY)
    hbm = pl.BlockSpec(memory_space=pltpu.HBM)
    vmem = pl.BlockSpec(memory_space=pltpu.VMEM)
    operands = [
        pltpu.with_memory_space_constraint(x, pltpu.HBM)
        for x in (
            out_grad, route_ids.T, route_weights.T, gate_pre[0], up_pre[0], w_gate[0], w_up[0], w_down[0]
        )
    ]
    zlo, zlp, acc, wlast, wgrad = pl.pallas_call(
        functools.partial(step_kernel, n, cap),
        out_shape=(
            jax.ShapeDtypeStruct((grp, qw), BF),
            jax.ShapeDtypeStruct((grp, qw), BF),
            jax.ShapeDtypeStruct((2, own, half), F32),
            jax.ShapeDtypeStruct((own, 2 * rows), BF),
            jax.ShapeDtypeStruct((topk, own), F32),
        ),
        in_specs=[hbm] * 8,
        out_specs=(anywhere,) * 5,
        scratch_shapes=scratch(n, cap, own, width, hidden, topk),
        compiler_params=pltpu.CompilerParams(
            collective_id=0, has_side_effects=True, vmem_limit_bytes=VMEM1 * 2**20
        ),
        name="expert_step",
    )(
        *operands
    )
    in_grad, weight_grad = pl.pallas_call(
        functools.partial(finish_kernel, cap),
        out_shape=(
            jax.ShapeDtypeStruct((own, width), BF),
            jax.ShapeDtypeStruct((topk, own), BF),
        ),
        in_specs=[vmem] * 5,
        out_specs=(anywhere, anywhere),
        scratch_shapes=[
            pltpu.VMEM((2, PARTS, own, qw), BF), pltpu.VMEM((topk, own), BF),
            pltpu.SemaphoreType.DMA((2 * PARTS,)), pltpu.SemaphoreType.DMA,
        ],
        compiler_params=pltpu.CompilerParams(vmem_limit_bytes=VMEM2 * 2**20),
        name="combine",
    )(zlo, zlp, acc, wlast, wgrad)
    return in_grad, weight_grad.T


def solution(mesh):
    in_specs = (
        P(("expert", "seq"), None),
        P("expert", None),
        P("expert", None),
        P("expert", None, "seq"),
        P("expert", None, "seq"),
        P("expert", None, "seq"),
        P("expert", None, "seq"),
        P("expert", "seq", None),
    )
    out_specs = (P(("expert", "seq"), None), P(("expert", "seq"), None))
    return jax.shard_map(
        on_device, mesh=mesh, in_specs=in_specs, out_specs=out_specs, check_vma=False
    )
```

```python
import functools

import jax
import jax.numpy as jnp
from jax import lax
from jax.experimental import pallas as pl
from jax.experimental.pallas import tpu as pltpu
from jax.sharding import PartitionSpec as P

BF = jnp.bfloat16
F32 = jnp.float32
NT = (((1,), (1,)), ((), ()))
NN = (((1,), (0,)), ((), ()))
TN = (((0,), (0,)), ((), ()))


def silu_parts(value):
    sigma = jax.nn.sigmoid(value)
    return (value * sigma, sigma * (1.0 + value * (1.0 - sigma)))


def dot(a, b, dims):
    return lax.dot_general(a, b, dims, preferred_element_type=F32)


def swap(value):
    return lax.ppermute(value, "seq", [(0, 1), (1, 0)])


def ordered(mine, theirs, seq_at, axis):
    low = jnp.where(seq_at == 0, mine, theirs)
    high = jnp.where(seq_at == 0, theirs, mine)
    return jnp.concatenate([low, high], axis=axis)


def routing(ids, weights, experts, capacity):
    tokens = ids.shape[0]
    same = ids[:, :, None] == jnp.arange(experts, dtype=jnp.int32)
    hit = jnp.any(same, axis=1)
    weight = jnp.sum(jnp.where(same, weights[:, :, None], 0.0), axis=1)
    row = jnp.arange(tokens, dtype=jnp.int32)
    earlier = (row[None, :] < row[:, None]).astype(BF)
    position = dot(earlier, hit.astype(BF), NN)
    slot = jnp.where(hit, position, float(capacity))
    return slot, weight


def on_device_xla(out_grad, route_ids, route_weights, gate_pre, up_pre, w_gate, w_up, w_down):
    n_expert = lax.axis_size("expert")
    seq_at = lax.axis_index("seq")
    own, width = out_grad.shape
    half = width // 2
    experts = n_expert
    slots = gate_pre.shape[1]
    capacity = slots // n_expert
    slot, weight = routing(route_ids, route_weights, experts, capacity)
    table = (slot[:, :, None] == jnp.arange(capacity, dtype=F32)).reshape(2 * own, slots)
    w_all = jnp.broadcast_to(weight[:, :, None], (2 * own, experts, capacity)).reshape(2 * own, slots)
    w_all = jnp.where(table, w_all, 0.0)
    w_hi = w_all.astype(BF)
    w_lo = (w_all - w_hi.astype(F32)).astype(BF)
    mine = lax.dynamic_slice_in_dim(out_grad, seq_at * half, half, 1)
    other = lax.dynamic_slice_in_dim(out_grad, (1 - seq_at) * half, half, 1)
    tokens = ordered(mine, swap(other), seq_at, 0)
    outgoing = dot(table.astype(BF), tokens, TN).astype(BF).reshape(experts, capacity, half)
    received = lax.all_to_all(outgoing, "expert", split_axis=0, concat_axis=0, tiled=True)
    received = received.reshape(slots, half)
    slot_grad = ordered(received, swap(received), seq_at, 1)
    hidden_grad = dot(slot_grad, w_down[0], NT)
    active, slope = silu_parts(gate_pre[0].astype(F32))
    up_part = up_pre[0].astype(F32)
    score = jnp.sum(hidden_grad * active * up_part, axis=1).astype(BF)
    gate_diff = (hidden_grad * up_part * slope).astype(BF)
    up_diff = (hidden_grad * active).astype(BF)
    part = (dot(gate_diff, w_gate[0], NT) + dot(up_diff, w_up[0], NT)).astype(BF)
    score = lax.optimization_barrier(score)
    part = lax.optimization_barrier(part)
    keep = lax.dynamic_slice_in_dim(part, seq_at * half, half, 1)
    give = lax.dynamic_slice_in_dim(part, (1 - seq_at) * half, half, 1)
    total = (keep.astype(F32) + swap(give).astype(F32)).astype(BF)
    total_score = (score.astype(F32) + swap(score).astype(F32)).astype(BF)
    back = lax.all_to_all(
        total.reshape(n_expert, capacity, half), "expert", split_axis=0, concat_axis=0, tiled=True
    ).reshape(slots, half)
    back_score = lax.all_to_all(
        total_score.reshape(n_expert, capacity), "expert", split_axis=0, concat_axis=0, tiled=True
    ).reshape(slots)
    rows = (dot(w_hi, back, NN) + dot(w_lo, back, NN)).astype(BF)
    keep = lax.dynamic_slice_in_dim(rows, seq_at * own, own, 0)
    give = lax.dynamic_slice_in_dim(rows, (1 - seq_at) * own, own, 0)
    in_grad = ordered(keep, swap(give), seq_at, 1)
    own_table = lax.dynamic_slice_in_dim(table, seq_at * own, own, 0)
    own_ids = lax.dynamic_slice_in_dim(route_ids, seq_at * own, own, 0)
    of_expert = jnp.sum(
        jnp.where(own_table, back_score.astype(F32)[None, :], 0.0).reshape(own, experts, capacity),
        axis=2,
    )
    same = own_ids[:, :, None] == jnp.arange(experts, dtype=jnp.int32)
    weight_grad = jnp.sum(jnp.where(same, of_expert[:, None, :], 0.0), axis=2)
    return in_grad, weight_grad.astype(BF)


MESH = pl.DeviceIdType.MESH
PARTS = 4
PIECES = 2


def lanes(shape, axis):
    return lax.broadcasted_iota(jnp.int32, shape, axis).astype(F32)


def fdiv(value, by):
    return jnp.floor((value + 0.5) * (1.0 / by))


def ones(mask):
    return jnp.where(mask, 1.0, 0.0).astype(BF)

def pick4(table, i):
    i1, i0 = i // 2, lax.rem(i, 2)
    c0, c1, c2, c3 = table
    return c0 + (c1 - c0) * i0 + (c2 - c0) * i1 + (c3 - c2 - c1 + c0) * i1 * i0


VMEM1 = 46
VMEM2 = 16
SEND = ((2, 0, 3, 1), (1, 3, 2, 0), (2, 0, 1, 3), (1, 3, 0, 2))
COLLECT = ((3, 2, 1), (1, 2, 3), (1, 2, 3), (3, 2, 1))
WORK = ((0, 3, 1, 2), (1, 3, 0, 2), (2, 0, 3, 1), (3, 0, 2, 1))


def quad_in(order, z, i):
    return pick4([pick4(row, i) for row in order], z)


def xor2(a, b):
    a1, a0, b1, b0 = a // 2, lax.rem(a, 2), b // 2, lax.rem(b, 2)
    return 2 * (a1 + b1 - 2 * a1 * b1) + (a0 + b0 - 2 * a0 * b0)


def packed_rows(shape, axis, blk, cap):
    r = lanes(shape, axis)
    block = fdiv(r, blk)
    part = fdiv(r - block * blk, cap)
    return block, part, r - block * blk - part * cap


def permutation(grp, blk, cap):
    a0, b0, p0 = packed_rows((grp, grp), 0, blk, cap)
    return ones(lanes((grp, grp), 1) == b0 * blk + a0 * cap + p0)


def step_kernel(
    n, cap, og, ids_hbm, wt_hbm, gp_hbm, up_hbm, wg_hbm, wu_hbm, wd_hbm,
    zlo, zlp, acc_out, wlast, wgrad,
    ids_ref, wt_ref, gp_ref, up_ref, wgu, wd, tok, sel, snd, rxo, rxp, pout, pin, snd2, zo, zp, zol, zpl,
    vbuf, wk, acc, gbuf, scs, sci, sco, scr, perm_ref,
    l_in, l_tok, s_tok, r_tok, l_w, s_d, r_d, s_f, r_f, s_p, r_p, s_s, r_s, s_b, r_b, s_c, r_c,
    s_g, r_g, l_o, l_a,
):
    me = lax.axis_index("expert")
    s = lax.axis_index("seq")
    o = 1 - s
    own, width = og.shape
    half = width // 2
    slots = n * cap
    blk = PARTS * cap
    grp = PARTS * blk
    rows = PARTS * cap
    qw = half // PARTS
    pw = half // PIECES
    hidden = wd_hbm.shape[0]
    quads = n // PARTS
    zat = me // PARTS
    tokens = 2 * own
    jat = lax.rem(me, PARTS)
    peers = [xor2(jat, r) for r in range(PARTS)]

    inputs = [
        pltpu.make_async_copy(ids_hbm, ids_ref, l_in.at[0]),
        pltpu.make_async_copy(wt_hbm, wt_ref, l_in.at[1]),
        pltpu.make_async_copy(gp_hbm, gp_ref, l_in.at[2]),
        pltpu.make_async_copy(up_hbm, up_ref, l_in.at[3]),
    ]
    inputs[0].start()
    barrier = pltpu.get_barrier_semaphore()
    pl.semaphore_signal(barrier, inc=1, device_id=(me, o), device_id_type=MESH)

    def greet(i, c):
        pl.semaphore_signal(
            barrier, inc=1, device_id=(lax.rem(me + i, n), s), device_id_type=MESH
        )
        return c

    lax.fori_loop(1, n, greet, 0)

    base = pl.multiple_of(s * half, 128)
    obase = pl.multiple_of(o * half, 128)
    mine = pl.multiple_of(s * own, 128)

    def remote(src, dst, ss, rs, dev):
        return pltpu.make_async_remote_copy(
            src_ref=src, dst_ref=dst, send_sem=ss, recv_sem=rs, device_id=dev, device_id_type=MESH
        )

    def tok_at(q):
        return tok.at[pl.ds(pl.multiple_of(q * tokens + mine, 16), own), :]

    def tok_local(q):
        cols = pl.ds(pl.multiple_of(base + q * qw, 128), qw)
        return pltpu.make_async_copy(og.at[:, cols], tok_at(q), l_tok)

    def tok_copy(q):
        cols = pl.ds(pl.multiple_of(obase + q * qw, 128), qw)
        return remote(og.at[:, cols], tok_at(q), s_tok, r_tok, (me, o))

    all_own = og.at[:, pl.ds(0, half)]
    all_tok = tok.at[pl.ds(0, PARTS * own), :]
    tok_all = remote(all_own, all_tok, s_tok, r_tok, (me, o))

    for q in range(PARTS):
        tok_local(q).start()
    for load in inputs[1:]:
        load.start()

    pl.semaphore_wait(barrier, n)
    for q in range(PARTS):
        tok_copy(q).start()

    inputs[0].wait()
    ids = jnp.transpose(ids_ref[...])
    e_lane = lax.broadcasted_iota(jnp.int32, (tokens, n), 1)
    hit = jnp.zeros((tokens, n), F32)
    for k in range(ids_ref.shape[0]):
        hit = jnp.where(ids[:, k : k + 1] == e_lane, 1.0, hit)
    tri = ones(lanes((tokens, tokens), 1) < lanes((tokens, tokens), 0))
    pos = dot(tri, hit.astype(BF), NN)
    v = jnp.where((hit > 0.5) & (pos < cap - 0.5), pos, 255.0)
    vbuf[...] = v
    vb = v.astype(BF)

    perm_ref[...] = permutation(grp, blk, cap)
    r_block, r_part, r_place = packed_rows((grp, tokens), 0, blk, cap)
    pick_block = packed_rows((grp, n), 0, blk, cap)[0]

    def build(quad, carry):
        pick = ones(pick_block + (quad * PARTS).astype(F32) == lanes((grp, n), 1))
        found = dot(pick, vb, NT) == r_place
        at = pl.ds(pl.multiple_of(quad * grp, 16), grp)
        for q in range(PARTS):
            sel[at, q * tokens : (q + 1) * tokens] = ones(found & (r_part == float(q)))
        return carry

    lax.fori_loop(0, quads, build, 0)

    def d_copy(dest):
        at = pl.multiple_of(dest * blk, 16)
        to = pl.multiple_of(me * blk, 16)
        return remote(
            snd.at[pl.ds(at, blk), :], rxo.at[pl.ds(to, blk), :], s_d, r_d.at[me], (dest, s)
        )

    def d_wait(src):
        at = pl.multiple_of(src * blk, 16)
        return remote(
            snd.at[pl.ds(at, blk), :], rxo.at[pl.ds(at, blk), :], s_d, r_d.at[src], (src, s)
        )

    def f_copy(src):
        at = pl.multiple_of(src * blk, 16)
        return remote(
            rxo.at[pl.ds(at, blk), :], rxp.at[pl.ds(at, blk), :], s_f, r_f.at[src // PARTS], (me, o)
        )

    def f_all(quad):
        at = pl.ds(pl.multiple_of(quad * grp, 16), grp)
        return remote(rxo.at[at, :], rxp.at[at, :], s_f, r_f.at[quad], (me, o))

    def own_copy():
        at = pl.multiple_of(me * blk, 16)
        return remote(
            snd.at[pl.ds(at, blk), :], rxp.at[pl.ds(at, blk), :], s_f, r_f.at[zat], (me, o)
        )

    pltpu.make_async_copy(all_own, all_tok, l_tok).wait()
    tok_all.wait_recv()

    def dispatch(i, carry):
        quad = quad_in(SEND, zat, i)
        at = pl.ds(pl.multiple_of(quad * grp, 16), grp)
        snd[at, :] = dot(sel[at, :], tok[...], NN).astype(BF)
        for j in peers:
            dest = quad * PARTS + j

            @pl.when(dest != me)
            def _():
                d_copy(dest).start()

            @pl.when(dest == me)
            def _():
                here = pl.ds(pl.multiple_of(me * blk, 16), blk)
                rxo[here, :] = snd[here, :]
                own_copy().start()

        return carry

    lax.fori_loop(0, quads, dispatch, 0)
    loads = [
        pltpu.make_async_copy(wd_hbm, wd, l_w.at[0]),
        pltpu.make_async_copy(wg_hbm, wgu.at[:, :hidden], l_w.at[1]),
        pltpu.make_async_copy(wu_hbm, wgu.at[:, hidden:], l_w.at[2]),
    ]
    for load in loads:
        load.start()

    for load in inputs[1:]:
        load.wait()
    my_ids = jnp.transpose(ids_ref[:, pl.ds(mine, own)].astype(F32))
    my_wts = jnp.transpose(wt_ref[:, pl.ds(mine, own)])
    my_v = vbuf[pl.ds(mine, own), :].astype(BF)
    my_lane = lanes((own, n), 1)
    wte = jnp.zeros((own, n), F32)
    for k in range(ids_ref.shape[0]):
        wte = jnp.where(my_ids[:, k : k + 1] == my_lane, my_wts[:, k : k + 1], wte)
    hi = wte.astype(BF)
    lo = (wte - hi.astype(F32)).astype(BF)

    others = [xor2(zat, pick4([row[i] for row in COLLECT], zat)) for i in range(quads - 1)]
    order = [zat] + others
    place = packed_rows((own, 2 * rows), 1, rows, cap)[2]
    upper = lanes((own, 2 * rows), 1) < rows - 0.5
    e_half, e_block, _ = packed_rows((n, 2 * rows), 1, rows, cap)
    for i, quad in enumerate(order):
        expert = e_block + (quad * PARTS).astype(F32)
        expand = ones(expert == lanes((n, 2 * rows), 0))
        taken = dot(my_v, expand, NN) == place
        both = jnp.where(upper, dot(hi, expand, NN), dot(lo, expand, NN))
        wk[i] = jnp.where(taken, both, 0.0).astype(BF)
    w_out = pltpu.make_async_copy(wk.at[quads - 1], wlast, l_o.at[0])
    w_out.start()

    def p_copy(i, h):
        return remote(
            pout.at[i, h], pin.at[i, h], s_p, r_p.at[i * PIECES + h], (me, o)
        )

    def sc_copy(i):
        return remote(scs.at[i], sci.at[i], s_s, r_s.at[i], (me, o))

    def back_at(quad, j):
        return pl.multiple_of((xor2(zat, quad) - 1) * grp + j * blk, 16)

    def far_copy(quad, j):
        dest = quad * PARTS + j
        at = pl.multiple_of(dest * blk, 16)
        return remote(
            snd2.at[pl.ds(at, blk), :], zol.at[pl.ds(back_at(quad, jat), blk), :],
            s_b, r_b.at[me], (dest, s),
        )

    def last_copy(quad, j):
        dest = quad * PARTS + j
        at = pl.multiple_of(dest * blk, 16)
        to = pl.multiple_of(jat * blk, 16)
        return remote(
            snd2.at[pl.ds(at, blk), :], zlo.at[pl.ds(to, blk), :], s_b, r_b.at[me], (dest, s)
        )

    def last_wait(quad, j):
        src = quad * PARTS + j
        at = pl.multiple_of(src * blk, 16)
        to = pl.multiple_of(j * blk, 16)
        return remote(
            snd2.at[pl.ds(at, blk), :], zlo.at[pl.ds(to, blk), :], s_b, r_b.at[src], (src, s)
        )

    def last_share(quad, j):
        src = quad * PARTS + j
        at = pl.multiple_of(j * blk, 16)
        return remote(
            zlo.at[pl.ds(at, blk), :], zlp.at[pl.ds(at, blk), :], s_g, r_g.at[src // PARTS], (me, o)
        )

    def far_wait(quad, j):
        src = quad * PARTS + j
        at = pl.multiple_of(src * blk, 16)
        return remote(
            snd2.at[pl.ds(at, blk), :], zol.at[pl.ds(back_at(quad, j), blk), :],
            s_b, r_b.at[src], (src, s),
        )

    def h_copy(quad, j):
        src = quad * PARTS + j
        at = back_at(quad, j)
        return remote(
            zol.at[pl.ds(at, blk), :], zpl.at[pl.ds(at, blk), :], s_g, r_g.at[src // PARTS], (me, o)
        )

    def b_copy(dest):
        at = pl.multiple_of(dest * blk, 16)
        to = pl.multiple_of(jat * blk, 16)
        return remote(
            snd2.at[pl.ds(at, blk), :], zo.at[pl.ds(to, blk), :], s_b, r_b.at[me], (dest, s)
        )

    def b_wait(j):
        src = zat * PARTS + j
        at = pl.multiple_of(src * blk, 16)
        to = pl.multiple_of(j * blk, 16)
        return remote(
            snd2.at[pl.ds(at, blk), :], zo.at[pl.ds(to, blk), :], s_b, r_b.at[src], (src, s)
        )

    def g_copy(j):
        src = zat * PARTS + j
        at = pl.multiple_of(j * blk, 16)
        return remote(
            zo.at[pl.ds(at, blk), :], zp.at[pl.ds(at, blk), :], s_g, r_g.at[src // PARTS], (me, o)
        )

    def own_back():
        at = pl.multiple_of(me * blk, 16)
        to = pl.multiple_of(jat * blk, 16)
        return remote(
            snd2.at[pl.ds(at, blk), :], zp.at[pl.ds(to, blk), :], s_g, r_g.at[zat], (me, o)
        )

    def c_copy(dest):
        return remote(sco.at[dest], scr.at[me], s_c, r_c, (dest, s))

    c_rows = pl.ds(0, n - 1)
    c_all = remote(sco.at[c_rows], scr.at[c_rows], s_c, r_c, (me, o))

    def work(i, carry):
        quad = quad_in(WORK, zat, i)
        packed = pl.ds(pl.multiple_of(quad * grp, 16), grp)
        slot_at = pl.ds(pl.multiple_of(quad * rows, 16), rows)
        for j in peers:
            src = quad * PARTS + j

            @pl.when(src != me)
            def _():
                d_wait(src).wait_recv()
                f_copy(src).start()

        @pl.when(i == 0)
        def _():
            loads[0].wait()

        perm = perm_ref[...]

        def contract(got, start):
            total = jnp.zeros((rows, hidden), F32)
            for q in range(0, PARTS, 2):
                x = jnp.concatenate([got[p * rows : (p + 1) * rows] for p in (q, q + 1)], axis=1)
                cols = pl.ds(pl.multiple_of(start + q * qw, 128), 2 * qw)
                total = total + dot(x, wd[:, cols], NT)
            return total

        grad = contract(dot(perm, rxo[packed, :], NN).astype(BF), base)
        f_all(quad).wait_recv()
        grad = grad + contract(dot(perm, rxp[packed, :], NN).astype(BF), obase)
        active, slope = silu_parts(gp_ref[slot_at, :].astype(F32))
        up = up_ref[slot_at, :].astype(F32)
        ud_v = grad * active
        diffs = jnp.concatenate([(grad * up * slope).astype(BF), ud_v.astype(BF)], axis=1)
        score = jnp.sum(ud_v * up, axis=1, keepdims=True)
        scs[i] = jnp.broadcast_to(score, (rows, 128)).astype(BF)
        sc_copy(i).start()

        @pl.when(i == 0)
        def _():
            loads[1].wait()
            loads[2].wait()

        def part(start):
            at = pl.ds(pl.multiple_of(start, 128), pw)
            return dot(diffs, wgu[at, :], NT).astype(BF)

        for h in range(PIECES):
            pout[i, h] = part(obase + h * pw)
            p_copy(i, h).start()
        kept = []
        for h in range(PIECES):
            value = part(base + h * pw).astype(F32)
            p_copy(i, h).wait_recv()
            value = (value + pin[i, h].astype(F32)).astype(BF)
            kept += [value[:, at : at + qw] for at in range(0, pw, qw)]
        snd2[packed, :] = dot(perm, jnp.concatenate(kept, axis=0), NN).astype(BF)
        sc_copy(i).wait_recv()
        total = (scs[i].astype(F32) + sci[i].astype(F32)).astype(BF)
        spot = packed_rows((rows, 128), 0, rows, cap)[2]
        spread = jnp.where(spot == lanes((rows, 128), 1), total.astype(F32), 0.0).astype(BF)
        block = packed_rows((8, rows), 1, rows, cap)[1]
        table = dot(ones(block == lanes((8, rows), 0)), spread, NN)
        for j in range(PARTS):
            sco[quad * PARTS + j] = table[j : j + 1]
        for j in peers:
            dest = quad * PARTS + j

            @pl.when(dest != me)
            def _():
                c_copy(dest).start()

                @pl.when(quad == zat)
                def _():
                    b_copy(dest).start()

                to_last = xor2(zat, quad) == pick4([row[-1] for row in COLLECT], quad)

                @pl.when((quad != zat) & to_last)
                def _():
                    last_copy(quad, j).start()

                @pl.when((quad != zat) & jnp.logical_not(to_last))
                def _():
                    far_copy(quad, j).start()

            @pl.when(dest == me)
            def _():
                here = pl.ds(pl.multiple_of(me * blk, 16), blk)
                zo[pl.ds(pl.multiple_of(jat * blk, 16), blk), :] = snd2[here, :]
                own_back().start()
                scr[me] = sco[me]

        return carry

    lax.fori_loop(0, quads, work, 0)

    def add(i, h, z, at):
        got = dot(perm_ref[...], z[at, :], NN).astype(BF)
        for q in range(PARTS):
            part = got[q * rows : (q + 1) * rows]
            value = dot(wk[i], jnp.concatenate([part, part], axis=0), NN)
            cols = slice(q * qw, (q + 1) * qw)
            acc[h, :, cols] = value if i == 0 else acc[h, :, cols] + value

    whole = pl.ds(0, grp)
    for j in peers[1:]:
        b_wait(j).wait_recv()
        g_copy(j).start()
    add(0, 0, zo, whole)
    remote(zo, zp, s_g, r_g.at[zat], (me, o)).wait_recv()
    add(0, 1, zp, whole)
    for i, quad in enumerate(others[:-1]):
        at = pl.ds(back_at(quad, 0), grp)
        for j in peers:
            far_wait(quad, j).wait_recv()
            h_copy(quad, j).start()
        add(i + 1, 0, zol, at)
        remote(zol.at[at, :], zpl.at[at, :], s_g, r_g.at[quad], (me, o)).wait_recv()
        add(i + 1, 1, zpl, at)
    a_out = pltpu.make_async_copy(acc, acc_out, l_a)
    a_out.start()

    most = pl.ds(0, (n - 1) * blk)
    remote(snd.at[most, :], rxo.at[most, :], s_d, r_d.at[me], (me, o)).wait_send()
    remote(rxo, rxp, s_f, r_f.at[zat], (me, o)).wait_send()
    tok_all.wait_send()
    remote(scs, sci, s_s, r_s.at[0], (me, o)).wait_send()
    remote(pout, pin, s_p, r_p.at[0], (me, o)).wait_send()
    w_out.wait()

    for j in peers:
        last_wait(others[-1], j).wait_recv()
        last_share(others[-1], j).start()
    c_all.wait_recv()
    scores = scr[...].reshape(n, 128).astype(BF)
    slot_of = vbuf[pl.ds(mine, own), :]
    found = jnp.zeros((own, 128), F32)
    for k in range(ids_ref.shape[0]):
        mask = my_ids[:, k : k + 1] == my_lane
        at = jnp.sum(jnp.where(mask, slot_of, 0.0), axis=1, keepdims=True)
        picked = jnp.where(lanes((own, 128), 1) == at, dot(ones(mask), scores, NN), 0.0)
        found = jnp.where(lanes((own, 128), 1) == k, jnp.sum(picked, axis=1, keepdims=True), found)
    gbuf[...] = jnp.transpose(found)[: gbuf.shape[0]]
    g_out = pltpu.make_async_copy(gbuf, wgrad, l_o.at[1])
    g_out.start()

    remote(snd2.at[most, :], rxo.at[most, :], s_b, r_b.at[me], (me, o)).wait_send()
    c_all.wait_send()
    a_out.wait()
    g_out.wait()
    remote(zlo, zlp, s_g, r_g.at[others[-1]], (me, o)).wait_recv()
    remote(rxo, rxp, s_g, r_g.at[zat], (me, o)).wait_send()


def finish_kernel(cap, zlo, zlp, acc, w_ref, g_ref, out, gout, ob, gb, s_out, s_g):
    s = lax.axis_index("seq")
    own = out.shape[0]
    half = out.shape[1] // 2
    qw = half // PARTS
    blk = PARTS * cap
    grp = PARTS * blk
    rows = PARTS * cap
    gb[...] = g_ref[...].astype(BF)
    g_copy = pltpu.make_async_copy(gb, gout, s_g)
    g_copy.start()
    perm = permutation(grp, blk, cap)
    stores = []
    for h, far in enumerate((zlo, zlp)):
        start = s * half if h == 0 else (1 - s) * half
        got = dot(perm, far[...], NN).astype(BF)
        for q in range(PARTS):
            part = got[q * rows : (q + 1) * rows]
            value = dot(w_ref[...], jnp.concatenate([part, part], axis=0), NN)
            ob[h, q] = (acc[h, :, q * qw : (q + 1) * qw] + value).astype(BF)
            copy = pltpu.make_async_copy(
                ob.at[h, q], out.at[:, pl.ds(pl.multiple_of(start + q * qw, 128), qw)],
                s_out.at[h * PARTS + q],
            )
            copy.start()
            stores.append(copy)
    g_copy.wait()
    for copy in stores:
        copy.wait()


def scratch(n, cap, own, width, hidden, topk):
    half = width // 2
    slots = n * cap
    big = PARTS * slots
    qw = half // PARTS
    quads = n // PARTS
    rows = PARTS * cap
    grp = PARTS * rows
    vm, dma = pltpu.VMEM, pltpu.SemaphoreType.DMA
    pw = half // PIECES
    return [
        vm((topk, 2 * own), jnp.int32), vm((topk, 2 * own), F32), vm((slots, hidden), BF), vm((slots, hidden), BF),
        vm((width, 2 * hidden), BF), vm((hidden, width), BF),
        vm((PARTS * 2 * own, qw), BF), vm((big, PARTS * 2 * own), BF), vm((big, qw), BF),
        vm((big, qw), BF), vm((big, qw), BF),
        vm((quads, PIECES, rows, pw), BF), vm((quads, PIECES, rows, pw), BF), vm((big, qw), BF),
        vm((grp, qw), BF), vm((grp, qw), BF), vm(((quads - 1) * grp, qw), BF), vm(((quads - 1) * grp, qw), BF),
        vm((2 * own, n), F32), vm((quads, own, 2 * rows), BF), vm((2, own, half), F32), vm((topk, own), F32),
        vm((quads, rows, 128), BF), vm((quads, rows, 128), BF), vm((n, 1, 128), F32),
        vm((n, 1, 128), F32), vm((grp, grp), BF),
        dma((4,)), dma, dma, dma, dma((3,)),
        dma, dma((n,)), dma, dma((quads,)), dma, dma((quads * PIECES,)), dma, dma((quads,)),
        dma, dma((n,)), dma, dma, dma, dma((quads,)), dma((2,)), dma,
    ]


def kernel_fits(n, cap, own, width, hidden):
    half = width // 2
    slots = n * cap
    size = 2 * (3 * width * hidden + 10 * slots * half + 4 * own * half)
    aligned = (PARTS * cap) % 16 == 0 and half % (PARTS * 128) == 0 and half % 512 == 0
    return n == PARTS * 4 and cap <= 16 and aligned and own == 128 and size < 48 * 2**20


def on_device(out_grad, route_ids, route_weights, gate_pre, up_pre, w_gate, w_up, w_down):
    n = lax.axis_size("expert")
    own, width = out_grad.shape
    slots, hidden = gate_pre.shape[1:]
    cap = slots // n
    topk = route_ids.shape[1]
    args = (out_grad, route_ids, route_weights, gate_pre, up_pre, w_gate, w_up, w_down)
    if not kernel_fits(n, cap, own, width, hidden):
        return on_device_xla(*args)
    half = width // 2
    qw = half // PARTS
    rows = PARTS * cap
    grp = PARTS * rows
    quads = n // PARTS
    anywhere = pl.BlockSpec(memory_space=pl.ANY)
    hbm = pl.BlockSpec(memory_space=pltpu.HBM)
    vmem = pl.BlockSpec(memory_space=pltpu.VMEM)
    operands = [
        pltpu.with_memory_space_constraint(x, pltpu.HBM)
        for x in (
            out_grad, route_ids.T, route_weights.T, gate_pre[0], up_pre[0], w_gate[0], w_up[0], w_down[0]
        )
    ]
    zlo, zlp, acc, wlast, wgrad = pl.pallas_call(
        functools.partial(step_kernel, n, cap),
        out_shape=(
            jax.ShapeDtypeStruct((grp, qw), BF),
            jax.ShapeDtypeStruct((grp, qw), BF),
            jax.ShapeDtypeStruct((2, own, half), F32),
            jax.ShapeDtypeStruct((own, 2 * rows), BF),
            jax.ShapeDtypeStruct((topk, own), F32),
        ),
        in_specs=[hbm] * 8,
        out_specs=(anywhere,) * 5,
        scratch_shapes=scratch(n, cap, own, width, hidden, topk),
        compiler_params=pltpu.CompilerParams(
            collective_id=0, has_side_effects=True, vmem_limit_bytes=VMEM1 * 2**20
        ),
        name="expert_step",
    )(
        *operands
    )
    in_grad, weight_grad = pl.pallas_call(
        functools.partial(finish_kernel, cap),
        out_shape=(
            jax.ShapeDtypeStruct((own, width), BF),
            jax.ShapeDtypeStruct((topk, own), BF),
        ),
        in_specs=[vmem] * 5,
        out_specs=(anywhere, anywhere),
        scratch_shapes=[
            pltpu.VMEM((2, PARTS, own, qw), BF), pltpu.VMEM((topk, own), BF),
            pltpu.SemaphoreType.DMA((2 * PARTS,)), pltpu.SemaphoreType.DMA,
        ],
        compiler_params=pltpu.CompilerParams(vmem_limit_bytes=VMEM2 * 2**20),
        name="combine",
    )(zlo, zlp, acc, wlast, wgrad)
    return in_grad, weight_grad.T


def solution(mesh):
    in_specs = (
        P(("expert", "seq"), None),
        P("expert", None),
        P("expert", None),
        P("expert", None, "seq"),
        P("expert", None, "seq"),
        P("expert", None, "seq"),
        P("expert", None, "seq"),
        P("expert", "seq", None),
    )
    out_specs = (P(("expert", "seq"), None), P(("expert", "seq"), None))
    return jax.shard_map(
        on_device, mesh=mesh, in_specs=in_specs, out_specs=out_specs, check_vma=False
    )
```

```python
import functools

import jax
import jax.numpy as jnp
from jax import lax
from jax.experimental import pallas as pl
from jax.experimental.pallas import tpu as pltpu
from jax.sharding import PartitionSpec as P

BF = jnp.bfloat16
F32 = jnp.float32
NT = (((1,), (1,)), ((), ()))
NN = (((1,), (0,)), ((), ()))
TN = (((0,), (0,)), ((), ()))


def silu_parts(value):
    sigma = jax.nn.sigmoid(value)
    return (value * sigma, sigma * (1.0 + value * (1.0 - sigma)))


def dot(a, b, dims):
    return lax.dot_general(a, b, dims, preferred_element_type=F32)


def swap(value):
    return lax.ppermute(value, "seq", [(0, 1), (1, 0)])


def ordered(mine, theirs, seq_at, axis):
    low = jnp.where(seq_at == 0, mine, theirs)
    high = jnp.where(seq_at == 0, theirs, mine)
    return jnp.concatenate([low, high], axis=axis)


def routing(ids, weights, experts, capacity):
    tokens = ids.shape[0]
    same = ids[:, :, None] == jnp.arange(experts, dtype=jnp.int32)
    hit = jnp.any(same, axis=1)
    weight = jnp.sum(jnp.where(same, weights[:, :, None], 0.0), axis=1)
    row = jnp.arange(tokens, dtype=jnp.int32)
    earlier = (row[None, :] < row[:, None]).astype(BF)
    position = dot(earlier, hit.astype(BF), NN)
    slot = jnp.where(hit, position, float(capacity))
    return slot, weight


def on_device_xla(out_grad, route_ids, route_weights, gate_pre, up_pre, w_gate, w_up, w_down):
    n_expert = lax.axis_size("expert")
    seq_at = lax.axis_index("seq")
    own, width = out_grad.shape
    half = width // 2
    experts = n_expert
    slots = gate_pre.shape[1]
    capacity = slots // n_expert
    slot, weight = routing(route_ids, route_weights, experts, capacity)
    table = (slot[:, :, None] == jnp.arange(capacity, dtype=F32)).reshape(2 * own, slots)
    w_all = jnp.broadcast_to(weight[:, :, None], (2 * own, experts, capacity)).reshape(2 * own, slots)
    w_all = jnp.where(table, w_all, 0.0)
    w_hi = w_all.astype(BF)
    w_lo = (w_all - w_hi.astype(F32)).astype(BF)
    mine = lax.dynamic_slice_in_dim(out_grad, seq_at * half, half, 1)
    other = lax.dynamic_slice_in_dim(out_grad, (1 - seq_at) * half, half, 1)
    tokens = ordered(mine, swap(other), seq_at, 0)
    outgoing = dot(table.astype(BF), tokens, TN).astype(BF).reshape(experts, capacity, half)
    received = lax.all_to_all(outgoing, "expert", split_axis=0, concat_axis=0, tiled=True)
    received = received.reshape(slots, half)
    slot_grad = ordered(received, swap(received), seq_at, 1)
    hidden_grad = dot(slot_grad, w_down[0], NT)
    active, slope = silu_parts(gate_pre[0].astype(F32))
    up_part = up_pre[0].astype(F32)
    score = jnp.sum(hidden_grad * active * up_part, axis=1).astype(BF)
    gate_diff = (hidden_grad * up_part * slope).astype(BF)
    up_diff = (hidden_grad * active).astype(BF)
    part = (dot(gate_diff, w_gate[0], NT) + dot(up_diff, w_up[0], NT)).astype(BF)
    score = lax.optimization_barrier(score)
    part = lax.optimization_barrier(part)
    keep = lax.dynamic_slice_in_dim(part, seq_at * half, half, 1)
    give = lax.dynamic_slice_in_dim(part, (1 - seq_at) * half, half, 1)
    total = (keep.astype(F32) + swap(give).astype(F32)).astype(BF)
    total_score = (score.astype(F32) + swap(score).astype(F32)).astype(BF)
    back = lax.all_to_all(
        total.reshape(n_expert, capacity, half), "expert", split_axis=0, concat_axis=0, tiled=True
    ).reshape(slots, half)
    back_score = lax.all_to_all(
        total_score.reshape(n_expert, capacity), "expert", split_axis=0, concat_axis=0, tiled=True
    ).reshape(slots)
    rows = (dot(w_hi, back, NN) + dot(w_lo, back, NN)).astype(BF)
    keep = lax.dynamic_slice_in_dim(rows, seq_at * own, own, 0)
    give = lax.dynamic_slice_in_dim(rows, (1 - seq_at) * own, own, 0)
    in_grad = ordered(keep, swap(give), seq_at, 1)
    own_table = lax.dynamic_slice_in_dim(table, seq_at * own, own, 0)
    own_ids = lax.dynamic_slice_in_dim(route_ids, seq_at * own, own, 0)
    of_expert = jnp.sum(
        jnp.where(own_table, back_score.astype(F32)[None, :], 0.0).reshape(own, experts, capacity),
        axis=2,
    )
    same = own_ids[:, :, None] == jnp.arange(experts, dtype=jnp.int32)
    weight_grad = jnp.sum(jnp.where(same, of_expert[:, None, :], 0.0), axis=2)
    return in_grad, weight_grad.astype(BF)


MESH = pl.DeviceIdType.MESH
PARTS = 4
PIECES = 2


def lanes(shape, axis):
    return lax.broadcasted_iota(jnp.int32, shape, axis).astype(F32)


def fdiv(value, by):
    return jnp.floor((value + 0.5) * (1.0 / by))


def ones(mask):
    return jnp.where(mask, 1.0, 0.0).astype(BF)

def pick4(table, i):
    i1, i0 = i // 2, lax.rem(i, 2)
    c0, c1, c2, c3 = table
    return c0 + (c1 - c0) * i0 + (c2 - c0) * i1 + (c3 - c2 - c1 + c0) * i1 * i0


VMEM1 = 46
VMEM2 = 16
SEND = ((2, 0, 3, 1), (1, 0, 3, 2), (2, 3, 0, 1), (1, 3, 0, 2))
COLLECT = ((3, 2, 1), (1, 2, 3), (1, 2, 3), (3, 2, 1))
WORK = ((0, 3, 1, 2), (1, 3, 0, 2), (2, 0, 3, 1), (3, 0, 2, 1))


def quad_in(order, z, i):
    return pick4([pick4(row, i) for row in order], z)


def xor2(a, b):
    a1, a0, b1, b0 = a // 2, lax.rem(a, 2), b // 2, lax.rem(b, 2)
    return 2 * (a1 + b1 - 2 * a1 * b1) + (a0 + b0 - 2 * a0 * b0)


def packed_rows(shape, axis, blk, cap):
    r = lanes(shape, axis)
    block = fdiv(r, blk)
    part = fdiv(r - block * blk, cap)
    return block, part, r - block * blk - part * cap


def permutation(grp, blk, cap):
    a0, b0, p0 = packed_rows((grp, grp), 0, blk, cap)
    return ones(lanes((grp, grp), 1) == b0 * blk + a0 * cap + p0)


def step_kernel(
    n, cap, og, ids_hbm, wt_hbm, gp_hbm, up_hbm, wg_hbm, wu_hbm, wd_hbm,
    zlo, zlp, acc_out, wlast, wgrad,
    ids_ref, wt_ref, gp_ref, up_ref, wgu, wd, tok, sel, snd, rxo, rxp, pout, pin, snd2, zo, zp, zol, zpl,
    vbuf, wk, acc, gbuf, scs, sci, sco, scr, perm_ref,
    l_in, l_tok, s_tok, r_tok, l_w, s_d, r_d, s_f, r_f, s_p, r_p, s_s, r_s, s_b, r_b, s_c, r_c,
    s_g, r_g, l_o, l_a,
):
    me = lax.axis_index("expert")
    s = lax.axis_index("seq")
    o = 1 - s
    own, width = og.shape
    half = width // 2
    slots = n * cap
    blk = PARTS * cap
    grp = PARTS * blk
    rows = PARTS * cap
    qw = half // PARTS
    pw = half // PIECES
    hidden = wd_hbm.shape[0]
    quads = n // PARTS
    zat = me // PARTS
    tokens = 2 * own
    jat = lax.rem(me, PARTS)
    peers = [xor2(jat, r) for r in range(PARTS)]

    inputs = [
        pltpu.make_async_copy(ids_hbm, ids_ref, l_in.at[0]),
        pltpu.make_async_copy(wt_hbm, wt_ref, l_in.at[1]),
        pltpu.make_async_copy(gp_hbm, gp_ref, l_in.at[2]),
        pltpu.make_async_copy(up_hbm, up_ref, l_in.at[3]),
    ]
    inputs[0].start()
    barrier = pltpu.get_barrier_semaphore()
    pl.semaphore_signal(barrier, inc=1, device_id=(me, o), device_id_type=MESH)

    def greet(i, c):
        pl.semaphore_signal(
            barrier, inc=1, device_id=(lax.rem(me + i, n), s), device_id_type=MESH
        )
        return c

    lax.fori_loop(1, n, greet, 0)

    base = pl.multiple_of(s * half, 128)
    obase = pl.multiple_of(o * half, 128)
    mine = pl.multiple_of(s * own, 128)

    def remote(src, dst, ss, rs, dev):
        return pltpu.make_async_remote_copy(
            src_ref=src, dst_ref=dst, send_sem=ss, recv_sem=rs, device_id=dev, device_id_type=MESH
        )

    def tok_at(q):
        return tok.at[pl.ds(pl.multiple_of(q * tokens + mine, 16), own), :]

    def tok_local(q):
        cols = pl.ds(pl.multiple_of(base + q * qw, 128), qw)
        return pltpu.make_async_copy(og.at[:, cols], tok_at(q), l_tok)

    def tok_copy(q):
        cols = pl.ds(pl.multiple_of(obase + q * qw, 128), qw)
        return remote(og.at[:, cols], tok_at(q), s_tok, r_tok, (me, o))

    all_own = og.at[:, pl.ds(0, half)]
    all_tok = tok.at[pl.ds(0, PARTS * own), :]
    tok_all = remote(all_own, all_tok, s_tok, r_tok, (me, o))

    for q in range(PARTS):
        tok_local(q).start()
    for load in inputs[1:]:
        load.start()

    pl.semaphore_wait(barrier, n)
    for q in range(PARTS):
        tok_copy(q).start()

    inputs[0].wait()
    ids = jnp.transpose(ids_ref[...])
    e_lane = lax.broadcasted_iota(jnp.int32, (tokens, n), 1)
    hit = jnp.zeros((tokens, n), F32)
    for k in range(ids_ref.shape[0]):
        hit = jnp.where(ids[:, k : k + 1] == e_lane, 1.0, hit)
    tri = ones(lanes((tokens, tokens), 1) < lanes((tokens, tokens), 0))
    pos = dot(tri, hit.astype(BF), NN)
    v = jnp.where((hit > 0.5) & (pos < cap - 0.5), pos, 255.0)
    vbuf[...] = v
    vb = v.astype(BF)

    perm_ref[...] = permutation(grp, blk, cap)
    r_block, r_part, r_place = packed_rows((grp, tokens), 0, blk, cap)
    pick_block = packed_rows((grp, n), 0, blk, cap)[0]

    def build(quad, carry):
        pick = ones(pick_block + (quad * PARTS).astype(F32) == lanes((grp, n), 1))
        found = dot(pick, vb, NT) == r_place
        at = pl.ds(pl.multiple_of(quad * grp, 16), grp)
        for q in range(PARTS):
            sel[at, q * tokens : (q + 1) * tokens] = ones(found & (r_part == float(q)))
        return carry

    lax.fori_loop(0, quads, build, 0)

    def d_copy(dest):
        at = pl.multiple_of(dest * blk, 16)
        to = pl.multiple_of(me * blk, 16)
        return remote(
            snd.at[pl.ds(at, blk), :], rxo.at[pl.ds(to, blk), :], s_d, r_d.at[me], (dest, s)
        )

    def d_wait(src):
        at = pl.multiple_of(src * blk, 16)
        return remote(
            snd.at[pl.ds(at, blk), :], rxo.at[pl.ds(at, blk), :], s_d, r_d.at[src], (src, s)
        )

    def f_copy(src):
        at = pl.multiple_of(src * blk, 16)
        return remote(
            rxo.at[pl.ds(at, blk), :], rxp.at[pl.ds(at, blk), :], s_f, r_f.at[src // PARTS], (me, o)
        )

    def f_all(quad):
        at = pl.ds(pl.multiple_of(quad * grp, 16), grp)
        return remote(rxo.at[at, :], rxp.at[at, :], s_f, r_f.at[quad], (me, o))

    def own_copy():
        at = pl.multiple_of(me * blk, 16)
        return remote(
            snd.at[pl.ds(at, blk), :], rxp.at[pl.ds(at, blk), :], s_f, r_f.at[zat], (me, o)
        )

    pltpu.make_async_copy(all_own, all_tok, l_tok).wait()
    tok_all.wait_recv()

    def dispatch(i, carry):
        quad = quad_in(SEND, zat, i)
        at = pl.ds(pl.multiple_of(quad * grp, 16), grp)
        snd[at, :] = dot(sel[at, :], tok[...], NN).astype(BF)
        for j in peers:
            dest = quad * PARTS + j

            @pl.when(dest != me)
            def _():
                d_copy(dest).start()

            @pl.when(dest == me)
            def _():
                here = pl.ds(pl.multiple_of(me * blk, 16), blk)
                rxo[here, :] = snd[here, :]
                own_copy().start()

        return carry

    lax.fori_loop(0, quads, dispatch, 0)
    loads = [
        pltpu.make_async_copy(wd_hbm, wd, l_w.at[0]),
        pltpu.make_async_copy(wg_hbm, wgu.at[:, :hidden], l_w.at[1]),
        pltpu.make_async_copy(wu_hbm, wgu.at[:, hidden:], l_w.at[2]),
    ]
    for load in loads:
        load.start()

    for load in inputs[1:]:
        load.wait()
    my_ids = jnp.transpose(ids_ref[:, pl.ds(mine, own)].astype(F32))
    my_wts = jnp.transpose(wt_ref[:, pl.ds(mine, own)])
    my_v = vbuf[pl.ds(mine, own), :].astype(BF)
    my_lane = lanes((own, n), 1)
    wte = jnp.zeros((own, n), F32)
    for k in range(ids_ref.shape[0]):
        wte = jnp.where(my_ids[:, k : k + 1] == my_lane, my_wts[:, k : k + 1], wte)
    hi = wte.astype(BF)
    lo = (wte - hi.astype(F32)).astype(BF)

    others = [xor2(zat, pick4([row[i] for row in COLLECT], zat)) for i in range(quads - 1)]
    order = [zat] + others
    place = packed_rows((own, 2 * rows), 1, rows, cap)[2]
    upper = lanes((own, 2 * rows), 1) < rows - 0.5
    e_half, e_block, _ = packed_rows((n, 2 * rows), 1, rows, cap)
    for i, quad in enumerate(order):
        expert = e_block + (quad * PARTS).astype(F32)
        expand = ones(expert == lanes((n, 2 * rows), 0))
        taken = dot(my_v, expand, NN) == place
        both = jnp.where(upper, dot(hi, expand, NN), dot(lo, expand, NN))
        wk[i] = jnp.where(taken, both, 0.0).astype(BF)
    w_out = pltpu.make_async_copy(wk.at[quads - 1], wlast, l_o.at[0])
    w_out.start()

    def p_copy(i, h):
        return remote(
            pout.at[i, h], pin.at[i, h], s_p, r_p.at[i * PIECES + h], (me, o)
        )

    def sc_copy(i):
        return remote(scs.at[i], sci.at[i], s_s, r_s.at[i], (me, o))

    def back_at(quad, j):
        return pl.multiple_of((xor2(zat, quad) - 1) * grp + j * blk, 16)

    def far_copy(quad, j):
        dest = quad * PARTS + j
        at = pl.multiple_of(dest * blk, 16)
        return remote(
            snd2.at[pl.ds(at, blk), :], zol.at[pl.ds(back_at(quad, jat), blk), :],
            s_b, r_b.at[me], (dest, s),
        )

    def last_copy(quad, j):
        dest = quad * PARTS + j
        at = pl.multiple_of(dest * blk, 16)
        to = pl.multiple_of(jat * blk, 16)
        return remote(
            snd2.at[pl.ds(at, blk), :], zlo.at[pl.ds(to, blk), :], s_b, r_b.at[me], (dest, s)
        )

    def last_wait(quad, j):
        src = quad * PARTS + j
        at = pl.multiple_of(src * blk, 16)
        to = pl.multiple_of(j * blk, 16)
        return remote(
            snd2.at[pl.ds(at, blk), :], zlo.at[pl.ds(to, blk), :], s_b, r_b.at[src], (src, s)
        )

    def last_share(quad, j):
        src = quad * PARTS + j
        at = pl.multiple_of(j * blk, 16)
        return remote(
            zlo.at[pl.ds(at, blk), :], zlp.at[pl.ds(at, blk), :], s_g, r_g.at[src // PARTS], (me, o)
        )

    def far_wait(quad, j):
        src = quad * PARTS + j
        at = pl.multiple_of(src * blk, 16)
        return remote(
            snd2.at[pl.ds(at, blk), :], zol.at[pl.ds(back_at(quad, j), blk), :],
            s_b, r_b.at[src], (src, s),
        )

    def h_copy(quad, j):
        src = quad * PARTS + j
        at = back_at(quad, j)
        return remote(
            zol.at[pl.ds(at, blk), :], zpl.at[pl.ds(at, blk), :], s_g, r_g.at[src // PARTS], (me, o)
        )

    def b_copy(dest):
        at = pl.multiple_of(dest * blk, 16)
        to = pl.multiple_of(jat * blk, 16)
        return remote(
            snd2.at[pl.ds(at, blk), :], zo.at[pl.ds(to, blk), :], s_b, r_b.at[me], (dest, s)
        )

    def b_wait(j):
        src = zat * PARTS + j
        at = pl.multiple_of(src * blk, 16)
        to = pl.multiple_of(j * blk, 16)
        return remote(
            snd2.at[pl.ds(at, blk), :], zo.at[pl.ds(to, blk), :], s_b, r_b.at[src], (src, s)
        )

    def g_copy(j):
        src = zat * PARTS + j
        at = pl.multiple_of(j * blk, 16)
        return remote(
            zo.at[pl.ds(at, blk), :], zp.at[pl.ds(at, blk), :], s_g, r_g.at[src // PARTS], (me, o)
        )

    def own_back():
        at = pl.multiple_of(me * blk, 16)
        to = pl.multiple_of(jat * blk, 16)
        return remote(
            snd2.at[pl.ds(at, blk), :], zp.at[pl.ds(to, blk), :], s_g, r_g.at[zat], (me, o)
        )

    def c_copy(dest):
        return remote(sco.at[dest], scr.at[me], s_c, r_c, (dest, s))

    c_rows = pl.ds(0, n - 1)
    c_all = remote(sco.at[c_rows], scr.at[c_rows], s_c, r_c, (me, o))

    def work(i, carry):
        quad = quad_in(WORK, zat, i)
        packed = pl.ds(pl.multiple_of(quad * grp, 16), grp)
        slot_at = pl.ds(pl.multiple_of(quad * rows, 16), rows)
        for j in peers:
            src = quad * PARTS + j

            @pl.when(src != me)
            def _():
                d_wait(src).wait_recv()
                f_copy(src).start()

        @pl.when(i == 0)
        def _():
            loads[0].wait()

        perm = perm_ref[...]

        def contract(got, start):
            total = jnp.zeros((rows, hidden), F32)
            for q in range(0, PARTS, 2):
                x = jnp.concatenate([got[p * rows : (p + 1) * rows] for p in (q, q + 1)], axis=1)
                cols = pl.ds(pl.multiple_of(start + q * qw, 128), 2 * qw)
                total = total + dot(x, wd[:, cols], NT)
            return total

        grad = contract(dot(perm, rxo[packed, :], NN).astype(BF), base)
        f_all(quad).wait_recv()
        grad = grad + contract(dot(perm, rxp[packed, :], NN).astype(BF), obase)
        active, slope = silu_parts(gp_ref[slot_at, :].astype(F32))
        up = up_ref[slot_at, :].astype(F32)
        ud_v = grad * active
        diffs = jnp.concatenate([(grad * up * slope).astype(BF), ud_v.astype(BF)], axis=1)
        score = jnp.sum(ud_v * up, axis=1, keepdims=True)
        scs[i] = jnp.broadcast_to(score, (rows, 128)).astype(BF)
        sc_copy(i).start()

        @pl.when(i == 0)
        def _():
            loads[1].wait()
            loads[2].wait()

        def part(start):
            at = pl.ds(pl.multiple_of(start, 128), pw)
            return dot(diffs, wgu[at, :], NT).astype(BF)

        for h in range(PIECES):
            pout[i, h] = part(obase + h * pw)
            p_copy(i, h).start()
        kept = []
        for h in range(PIECES):
            value = part(base + h * pw).astype(F32)
            p_copy(i, h).wait_recv()
            value = (value + pin[i, h].astype(F32)).astype(BF)
            kept += [value[:, at : at + qw] for at in range(0, pw, qw)]
        snd2[packed, :] = dot(perm, jnp.concatenate(kept, axis=0), NN).astype(BF)
        sc_copy(i).wait_recv()
        total = (scs[i].astype(F32) + sci[i].astype(F32)).astype(BF)
        spot = packed_rows((rows, 128), 0, rows, cap)[2]
        spread = jnp.where(spot == lanes((rows, 128), 1), total.astype(F32), 0.0).astype(BF)
        block = packed_rows((8, rows), 1, rows, cap)[1]
        table = dot(ones(block == lanes((8, rows), 0)), spread, NN)
        for j in range(PARTS):
            sco[quad * PARTS + j] = table[j : j + 1]
        for j in peers:
            dest = quad * PARTS + j

            @pl.when(dest != me)
            def _():
                c_copy(dest).start()

        for j in peers:
            dest = quad * PARTS + j

            @pl.when(dest != me)
            def _():
                @pl.when(quad == zat)
                def _():
                    b_copy(dest).start()

                to_last = xor2(zat, quad) == pick4([row[-1] for row in COLLECT], quad)

                @pl.when((quad != zat) & to_last)
                def _():
                    last_copy(quad, j).start()

                @pl.when((quad != zat) & jnp.logical_not(to_last))
                def _():
                    far_copy(quad, j).start()

            @pl.when(dest == me)
            def _():
                here = pl.ds(pl.multiple_of(me * blk, 16), blk)
                zo[pl.ds(pl.multiple_of(jat * blk, 16), blk), :] = snd2[here, :]
                own_back().start()
                scr[me] = sco[me]

        return carry

    lax.fori_loop(0, quads, work, 0)

    def add(i, h, z, at):
        got = dot(perm_ref[...], z[at, :], NN).astype(BF)
        for q in range(PARTS):
            part = got[q * rows : (q + 1) * rows]
            value = dot(wk[i], jnp.concatenate([part, part], axis=0), NN)
            cols = slice(q * qw, (q + 1) * qw)
            acc[h, :, cols] = value if i == 0 else acc[h, :, cols] + value

    whole = pl.ds(0, grp)
    for j in peers[1:]:
        b_wait(j).wait_recv()
        g_copy(j).start()
    add(0, 0, zo, whole)
    remote(zo, zp, s_g, r_g.at[zat], (me, o)).wait_recv()
    add(0, 1, zp, whole)
    for i, quad in enumerate(others[:-1]):
        at = pl.ds(back_at(quad, 0), grp)
        for j in peers:
            far_wait(quad, j).wait_recv()
            h_copy(quad, j).start()
        add(i + 1, 0, zol, at)
        remote(zol.at[at, :], zpl.at[at, :], s_g, r_g.at[quad], (me, o)).wait_recv()
        add(i + 1, 1, zpl, at)
    a_out = pltpu.make_async_copy(acc, acc_out, l_a)
    a_out.start()

    most = pl.ds(0, (n - 1) * blk)
    remote(snd.at[most, :], rxo.at[most, :], s_d, r_d.at[me], (me, o)).wait_send()
    remote(rxo, rxp, s_f, r_f.at[zat], (me, o)).wait_send()
    tok_all.wait_send()
    remote(scs, sci, s_s, r_s.at[0], (me, o)).wait_send()
    remote(pout, pin, s_p, r_p.at[0], (me, o)).wait_send()
    w_out.wait()

    for j in peers:
        last_wait(others[-1], j).wait_recv()
        last_share(others[-1], j).start()
    c_all.wait_recv()
    scores = scr[...].reshape(n, 128).astype(BF)
    slot_of = vbuf[pl.ds(mine, own), :]
    found = jnp.zeros((own, 128), F32)
    for k in range(ids_ref.shape[0]):
        mask = my_ids[:, k : k + 1] == my_lane
        at = jnp.sum(jnp.where(mask, slot_of, 0.0), axis=1, keepdims=True)
        picked = jnp.where(lanes((own, 128), 1) == at, dot(ones(mask), scores, NN), 0.0)
        found = jnp.where(lanes((own, 128), 1) == k, jnp.sum(picked, axis=1, keepdims=True), found)
    gbuf[...] = jnp.transpose(found)[: gbuf.shape[0]]
    g_out = pltpu.make_async_copy(gbuf, wgrad, l_o.at[1])
    g_out.start()

    remote(snd2.at[most, :], rxo.at[most, :], s_b, r_b.at[me], (me, o)).wait_send()
    c_all.wait_send()
    a_out.wait()
    g_out.wait()
    remote(zlo, zlp, s_g, r_g.at[others[-1]], (me, o)).wait_recv()
    remote(rxo, rxp, s_g, r_g.at[zat], (me, o)).wait_send()


def finish_kernel(cap, zlo, zlp, acc, w_ref, g_ref, out, gout, ob, gb, s_out, s_g):
    s = lax.axis_index("seq")
    own = out.shape[0]
    half = out.shape[1] // 2
    qw = half // PARTS
    blk = PARTS * cap
    grp = PARTS * blk
    rows = PARTS * cap
    gb[...] = g_ref[...].astype(BF)
    g_copy = pltpu.make_async_copy(gb, gout, s_g)
    g_copy.start()
    perm = permutation(grp, blk, cap)
    stores = []
    for h, far in enumerate((zlo, zlp)):
        start = s * half if h == 0 else (1 - s) * half
        got = dot(perm, far[...], NN).astype(BF)
        for q in range(PARTS):
            part = got[q * rows : (q + 1) * rows]
            value = dot(w_ref[...], jnp.concatenate([part, part], axis=0), NN)
            ob[h, q] = (acc[h, :, q * qw : (q + 1) * qw] + value).astype(BF)
            copy = pltpu.make_async_copy(
                ob.at[h, q], out.at[:, pl.ds(pl.multiple_of(start + q * qw, 128), qw)],
                s_out.at[h * PARTS + q],
            )
            copy.start()
            stores.append(copy)
    g_copy.wait()
    for copy in stores:
        copy.wait()


def scratch(n, cap, own, width, hidden, topk):
    half = width // 2
    slots = n * cap
    big = PARTS * slots
    qw = half // PARTS
    quads = n // PARTS
    rows = PARTS * cap
    grp = PARTS * rows
    vm, dma = pltpu.VMEM, pltpu.SemaphoreType.DMA
    pw = half // PIECES
    return [
        vm((topk, 2 * own), jnp.int32), vm((topk, 2 * own), F32), vm((slots, hidden), BF), vm((slots, hidden), BF),
        vm((width, 2 * hidden), BF), vm((hidden, width), BF),
        vm((PARTS * 2 * own, qw), BF), vm((big, PARTS * 2 * own), BF), vm((big, qw), BF),
        vm((big, qw), BF), vm((big, qw), BF),
        vm((quads, PIECES, rows, pw), BF), vm((quads, PIECES, rows, pw), BF), vm((big, qw), BF),
        vm((grp, qw), BF), vm((grp, qw), BF), vm(((quads - 1) * grp, qw), BF), vm(((quads - 1) * grp, qw), BF),
        vm((2 * own, n), F32), vm((quads, own, 2 * rows), BF), vm((2, own, half), F32), vm((topk, own), F32),
        vm((quads, rows, 128), BF), vm((quads, rows, 128), BF), vm((n, 1, 128), F32),
        vm((n, 1, 128), F32), vm((grp, grp), BF),
        dma((4,)), dma, dma, dma, dma((3,)),
        dma, dma((n,)), dma, dma((quads,)), dma, dma((quads * PIECES,)), dma, dma((quads,)),
        dma, dma((n,)), dma, dma, dma, dma((quads,)), dma((2,)), dma,
    ]


def kernel_fits(n, cap, own, width, hidden):
    half = width // 2
    slots = n * cap
    size = 2 * (3 * width * hidden + 10 * slots * half + 4 * own * half)
    aligned = (PARTS * cap) % 16 == 0 and half % (PARTS * 128) == 0 and half % 512 == 0
    return n == PARTS * 4 and cap <= 16 and aligned and own == 128 and size < 48 * 2**20


def on_device(out_grad, route_ids, route_weights, gate_pre, up_pre, w_gate, w_up, w_down):
    n = lax.axis_size("expert")
    own, width = out_grad.shape
    slots, hidden = gate_pre.shape[1:]
    cap = slots // n
    topk = route_ids.shape[1]
    args = (out_grad, route_ids, route_weights, gate_pre, up_pre, w_gate, w_up, w_down)
    if not kernel_fits(n, cap, own, width, hidden):
        return on_device_xla(*args)
    half = width // 2
    qw = half // PARTS
    rows = PARTS * cap
    grp = PARTS * rows
    quads = n // PARTS
    anywhere = pl.BlockSpec(memory_space=pl.ANY)
    hbm = pl.BlockSpec(memory_space=pltpu.HBM)
    vmem = pl.BlockSpec(memory_space=pltpu.VMEM)
    operands = [
        pltpu.with_memory_space_constraint(x, pltpu.HBM)
        for x in (
            out_grad, route_ids.T, route_weights.T, gate_pre[0], up_pre[0], w_gate[0], w_up[0], w_down[0]
        )
    ]
    zlo, zlp, acc, wlast, wgrad = pl.pallas_call(
        functools.partial(step_kernel, n, cap),
        out_shape=(
            jax.ShapeDtypeStruct((grp, qw), BF),
            jax.ShapeDtypeStruct((grp, qw), BF),
            jax.ShapeDtypeStruct((2, own, half), F32),
            jax.ShapeDtypeStruct((own, 2 * rows), BF),
            jax.ShapeDtypeStruct((topk, own), F32),
        ),
        in_specs=[hbm] * 8,
        out_specs=(anywhere,) * 5,
        scratch_shapes=scratch(n, cap, own, width, hidden, topk),
        compiler_params=pltpu.CompilerParams(
            collective_id=0, has_side_effects=True, vmem_limit_bytes=VMEM1 * 2**20
        ),
        name="expert_step",
    )(
        *operands
    )
    in_grad, weight_grad = pl.pallas_call(
        functools.partial(finish_kernel, cap),
        out_shape=(
            jax.ShapeDtypeStruct((own, width), BF),
            jax.ShapeDtypeStruct((topk, own), BF),
        ),
        in_specs=[vmem] * 5,
        out_specs=(anywhere, anywhere),
        scratch_shapes=[
            pltpu.VMEM((2, PARTS, own, qw), BF), pltpu.VMEM((topk, own), BF),
            pltpu.SemaphoreType.DMA((2 * PARTS,)), pltpu.SemaphoreType.DMA,
        ],
        compiler_params=pltpu.CompilerParams(vmem_limit_bytes=VMEM2 * 2**20),
        name="combine",
    )(zlo, zlp, acc, wlast, wgrad)
    return in_grad, weight_grad.T


def solution(mesh):
    in_specs = (
        P(("expert", "seq"), None),
        P("expert", None),
        P("expert", None),
        P("expert", None, "seq"),
        P("expert", None, "seq"),
        P("expert", None, "seq"),
        P("expert", None, "seq"),
        P("expert", "seq", None),
    )
    out_specs = (P(("expert", "seq"), None), P(("expert", "seq"), None))
    return jax.shard_map(
        on_device, mesh=mesh, in_specs=in_specs, out_specs=out_specs, check_vma=False
    )
```

```python
import functools

import jax
import jax.numpy as jnp
from jax import lax
from jax.experimental import pallas as pl
from jax.experimental.pallas import tpu as pltpu
from jax.sharding import PartitionSpec as P

BF = jnp.bfloat16
F32 = jnp.float32
NT = (((1,), (1,)), ((), ()))
NN = (((1,), (0,)), ((), ()))
TN = (((0,), (0,)), ((), ()))


def silu_parts(value):
    sigma = jax.nn.sigmoid(value)
    return (value * sigma, sigma * (1.0 + value * (1.0 - sigma)))


def dot(a, b, dims):
    return lax.dot_general(a, b, dims, preferred_element_type=F32)


def swap(value):
    return lax.ppermute(value, "seq", [(0, 1), (1, 0)])


def ordered(mine, theirs, seq_at, axis):
    low = jnp.where(seq_at == 0, mine, theirs)
    high = jnp.where(seq_at == 0, theirs, mine)
    return jnp.concatenate([low, high], axis=axis)


def routing(ids, weights, experts, capacity):
    tokens = ids.shape[0]
    same = ids[:, :, None] == jnp.arange(experts, dtype=jnp.int32)
    hit = jnp.any(same, axis=1)
    weight = jnp.sum(jnp.where(same, weights[:, :, None], 0.0), axis=1)
    row = jnp.arange(tokens, dtype=jnp.int32)
    earlier = (row[None, :] < row[:, None]).astype(BF)
    position = dot(earlier, hit.astype(BF), NN)
    slot = jnp.where(hit, position, float(capacity))
    return slot, weight


def on_device_xla(out_grad, route_ids, route_weights, gate_pre, up_pre, w_gate, w_up, w_down):
    n_expert = lax.axis_size("expert")
    seq_at = lax.axis_index("seq")
    own, width = out_grad.shape
    half = width // 2
    experts = n_expert
    slots = gate_pre.shape[1]
    capacity = slots // n_expert
    slot, weight = routing(route_ids, route_weights, experts, capacity)
    table = (slot[:, :, None] == jnp.arange(capacity, dtype=F32)).reshape(2 * own, slots)
    w_all = jnp.broadcast_to(weight[:, :, None], (2 * own, experts, capacity)).reshape(2 * own, slots)
    w_all = jnp.where(table, w_all, 0.0)
    w_hi = w_all.astype(BF)
    w_lo = (w_all - w_hi.astype(F32)).astype(BF)
    mine = lax.dynamic_slice_in_dim(out_grad, seq_at * half, half, 1)
    other = lax.dynamic_slice_in_dim(out_grad, (1 - seq_at) * half, half, 1)
    tokens = ordered(mine, swap(other), seq_at, 0)
    outgoing = dot(table.astype(BF), tokens, TN).astype(BF).reshape(experts, capacity, half)
    received = lax.all_to_all(outgoing, "expert", split_axis=0, concat_axis=0, tiled=True)
    received = received.reshape(slots, half)
    slot_grad = ordered(received, swap(received), seq_at, 1)
    hidden_grad = dot(slot_grad, w_down[0], NT)
    active, slope = silu_parts(gate_pre[0].astype(F32))
    up_part = up_pre[0].astype(F32)
    score = jnp.sum(hidden_grad * active * up_part, axis=1).astype(BF)
    gate_diff = (hidden_grad * up_part * slope).astype(BF)
    up_diff = (hidden_grad * active).astype(BF)
    part = (dot(gate_diff, w_gate[0], NT) + dot(up_diff, w_up[0], NT)).astype(BF)
    score = lax.optimization_barrier(score)
    part = lax.optimization_barrier(part)
    keep = lax.dynamic_slice_in_dim(part, seq_at * half, half, 1)
    give = lax.dynamic_slice_in_dim(part, (1 - seq_at) * half, half, 1)
    total = (keep.astype(F32) + swap(give).astype(F32)).astype(BF)
    total_score = (score.astype(F32) + swap(score).astype(F32)).astype(BF)
    back = lax.all_to_all(
        total.reshape(n_expert, capacity, half), "expert", split_axis=0, concat_axis=0, tiled=True
    ).reshape(slots, half)
    back_score = lax.all_to_all(
        total_score.reshape(n_expert, capacity), "expert", split_axis=0, concat_axis=0, tiled=True
    ).reshape(slots)
    rows = (dot(w_hi, back, NN) + dot(w_lo, back, NN)).astype(BF)
    keep = lax.dynamic_slice_in_dim(rows, seq_at * own, own, 0)
    give = lax.dynamic_slice_in_dim(rows, (1 - seq_at) * own, own, 0)
    in_grad = ordered(keep, swap(give), seq_at, 1)
    own_table = lax.dynamic_slice_in_dim(table, seq_at * own, own, 0)
    own_ids = lax.dynamic_slice_in_dim(route_ids, seq_at * own, own, 0)
    of_expert = jnp.sum(
        jnp.where(own_table, back_score.astype(F32)[None, :], 0.0).reshape(own, experts, capacity),
        axis=2,
    )
    same = own_ids[:, :, None] == jnp.arange(experts, dtype=jnp.int32)
    weight_grad = jnp.sum(jnp.where(same, of_expert[:, None, :], 0.0), axis=2)
    return in_grad, weight_grad.astype(BF)


MESH = pl.DeviceIdType.MESH
PARTS = 4
PIECES = 2


def lanes(shape, axis):
    return lax.broadcasted_iota(jnp.int32, shape, axis).astype(F32)


def fdiv(value, by):
    return jnp.floor((value + 0.5) * (1.0 / by))


def ones(mask):
    return jnp.where(mask, 1.0, 0.0).astype(BF)

def pick4(table, i):
    i1, i0 = i // 2, lax.rem(i, 2)
    c0, c1, c2, c3 = table
    return c0 + (c1 - c0) * i0 + (c2 - c0) * i1 + (c3 - c2 - c1 + c0) * i1 * i0


VMEM1 = 46
VMEM2 = 16
SEND = ((2, 0, 3, 1), (1, 0, 3, 2), (2, 3, 0, 1), (1, 3, 0, 2))
COLLECT = ((3, 2, 1), (1, 2, 3), (1, 2, 3), (3, 2, 1))
WORK = ((0, 3, 1, 2), (1, 3, 0, 2), (2, 0, 3, 1), (3, 0, 2, 1))


def quad_in(order, z, i):
    return pick4([pick4(row, i) for row in order], z)


def xor2(a, b):
    a1, a0, b1, b0 = a // 2, lax.rem(a, 2), b // 2, lax.rem(b, 2)
    return 2 * (a1 + b1 - 2 * a1 * b1) + (a0 + b0 - 2 * a0 * b0)


def packed_rows(shape, axis, blk, cap):
    r = lanes(shape, axis)
    block = fdiv(r, blk)
    part = fdiv(r - block * blk, cap)
    return block, part, r - block * blk - part * cap


def permutation(grp, blk, cap):
    a0, b0, p0 = packed_rows((grp, grp), 0, blk, cap)
    return ones(lanes((grp, grp), 1) == b0 * blk + a0 * cap + p0)


def step_kernel(
    n, cap, og, ids_hbm, wt_hbm, gp_hbm, up_hbm, wg_hbm, wu_hbm, wd_hbm,
    zlo, zlp, acc_out, wlast, wgrad,
    ids_ref, wt_ref, gp_ref, up_ref, wgu, wd, tok, sel, snd, rxo, rxp, pout, pin, snd2, zo, zp, zol, zpl,
    vbuf, wk, acc, gbuf, scs, sci, sco, scr, perm_ref,
    l_in, l_tok, s_tok, r_tok, l_w, s_d, r_d, s_f, r_f, s_p, r_p, s_s, r_s, s_b, r_b, s_c, r_c,
    s_g, r_g, l_o, l_a,
):
    me = lax.axis_index("expert")
    s = lax.axis_index("seq")
    o = 1 - s
    own, width = og.shape
    half = width // 2
    slots = n * cap
    blk = PARTS * cap
    grp = PARTS * blk
    rows = PARTS * cap
    qw = half // PARTS
    pw = half // PIECES
    hidden = wd_hbm.shape[0]
    quads = n // PARTS
    zat = me // PARTS
    tokens = 2 * own
    jat = lax.rem(me, PARTS)
    peers = [xor2(jat, r) for r in range(PARTS)]

    inputs = [
        pltpu.make_async_copy(ids_hbm, ids_ref, l_in.at[0]),
        pltpu.make_async_copy(wt_hbm, wt_ref, l_in.at[1]),
        pltpu.make_async_copy(gp_hbm, gp_ref, l_in.at[2]),
        pltpu.make_async_copy(up_hbm, up_ref, l_in.at[3]),
    ]
    inputs[0].start()
    barrier = pltpu.get_barrier_semaphore()
    pl.semaphore_signal(barrier, inc=1, device_id=(me, o), device_id_type=MESH)

    def greet(i, c):
        pl.semaphore_signal(
            barrier, inc=1, device_id=(lax.rem(me + i, n), s), device_id_type=MESH
        )
        return c

    lax.fori_loop(1, n, greet, 0)

    base = pl.multiple_of(s * half, 128)
    obase = pl.multiple_of(o * half, 128)
    mine = pl.multiple_of(s * own, 128)

    def remote(src, dst, ss, rs, dev):
        return pltpu.make_async_remote_copy(
            src_ref=src, dst_ref=dst, send_sem=ss, recv_sem=rs, device_id=dev, device_id_type=MESH
        )

    def tok_at(q):
        return tok.at[pl.ds(pl.multiple_of(q * tokens + mine, 16), own), :]

    def tok_local(q):
        cols = pl.ds(pl.multiple_of(base + q * qw, 128), qw)
        return pltpu.make_async_copy(og.at[:, cols], tok_at(q), l_tok)

    def tok_copy(q):
        cols = pl.ds(pl.multiple_of(obase + q * qw, 128), qw)
        return remote(og.at[:, cols], tok_at(q), s_tok, r_tok, (me, o))

    all_own = og.at[:, pl.ds(0, half)]
    all_tok = tok.at[pl.ds(0, PARTS * own), :]
    tok_all = remote(all_own, all_tok, s_tok, r_tok, (me, o))

    for q in range(PARTS):
        tok_local(q).start()
    for load in inputs[1:]:
        load.start()

    pl.semaphore_wait(barrier, n)
    for q in range(PARTS):
        tok_copy(q).start()

    inputs[0].wait()
    ids = jnp.transpose(ids_ref[...])
    e_lane = lax.broadcasted_iota(jnp.int32, (tokens, n), 1)
    hit = jnp.zeros((tokens, n), F32)
    for k in range(ids_ref.shape[0]):
        hit = jnp.where(ids[:, k : k + 1] == e_lane, 1.0, hit)
    tri = ones(lanes((tokens, tokens), 1) < lanes((tokens, tokens), 0))
    pos = dot(tri, hit.astype(BF), NN)
    v = jnp.where((hit > 0.5) & (pos < cap - 0.5), pos, 255.0)
    vbuf[...] = v
    vb = v.astype(BF)

    perm_ref[...] = permutation(grp, blk, cap)
    r_block, r_part, r_place = packed_rows((grp, tokens), 0, blk, cap)
    pick_block = packed_rows((grp, n), 0, blk, cap)[0]

    def build(quad, carry):
        pick = ones(pick_block + (quad * PARTS).astype(F32) == lanes((grp, n), 1))
        found = dot(pick, vb, NT) == r_place
        at = pl.ds(pl.multiple_of(quad * grp, 16), grp)
        for q in range(PARTS):
            sel[at, q * tokens : (q + 1) * tokens] = ones(found & (r_part == float(q)))
        return carry

    for i in range(2):
        build(quad_in(SEND, zat, i), 0)

    def d_copy(dest):
        at = pl.multiple_of(dest * blk, 16)
        to = pl.multiple_of(me * blk, 16)
        return remote(
            snd.at[pl.ds(at, blk), :], rxo.at[pl.ds(to, blk), :], s_d, r_d.at[me], (dest, s)
        )

    def d_wait(src):
        at = pl.multiple_of(src * blk, 16)
        return remote(
            snd.at[pl.ds(at, blk), :], rxo.at[pl.ds(at, blk), :], s_d, r_d.at[src], (src, s)
        )

    def f_copy(src):
        at = pl.multiple_of(src * blk, 16)
        return remote(
            rxo.at[pl.ds(at, blk), :], rxp.at[pl.ds(at, blk), :], s_f, r_f.at[src // PARTS], (me, o)
        )

    def f_all(quad):
        at = pl.ds(pl.multiple_of(quad * grp, 16), grp)
        return remote(rxo.at[at, :], rxp.at[at, :], s_f, r_f.at[quad], (me, o))

    def own_copy():
        at = pl.multiple_of(me * blk, 16)
        return remote(
            snd.at[pl.ds(at, blk), :], rxp.at[pl.ds(at, blk), :], s_f, r_f.at[zat], (me, o)
        )

    pltpu.make_async_copy(all_own, all_tok, l_tok).wait()
    tok_all.wait_recv()

    def dispatch(i, carry):
        quad = quad_in(SEND, zat, i)

        @pl.when(i >= 2)
        def _():
            build(quad, 0)

        at = pl.ds(pl.multiple_of(quad * grp, 16), grp)
        snd[at, :] = dot(sel[at, :], tok[...], NN).astype(BF)
        for j in peers:
            dest = quad * PARTS + j

            @pl.when(dest != me)
            def _():
                d_copy(dest).start()

            @pl.when(dest == me)
            def _():
                here = pl.ds(pl.multiple_of(me * blk, 16), blk)
                rxo[here, :] = snd[here, :]
                own_copy().start()

        return carry

    lax.fori_loop(0, quads, dispatch, 0)
    loads = [
        pltpu.make_async_copy(wd_hbm, wd, l_w.at[0]),
        pltpu.make_async_copy(wg_hbm, wgu.at[:, :hidden], l_w.at[1]),
        pltpu.make_async_copy(wu_hbm, wgu.at[:, hidden:], l_w.at[2]),
    ]
    for load in loads:
        load.start()

    for load in inputs[1:]:
        load.wait()
    my_ids = jnp.transpose(ids_ref[:, pl.ds(mine, own)].astype(F32))
    my_wts = jnp.transpose(wt_ref[:, pl.ds(mine, own)])
    my_v = vbuf[pl.ds(mine, own), :].astype(BF)
    my_lane = lanes((own, n), 1)
    wte = jnp.zeros((own, n), F32)
    for k in range(ids_ref.shape[0]):
        wte = jnp.where(my_ids[:, k : k + 1] == my_lane, my_wts[:, k : k + 1], wte)
    hi = wte.astype(BF)
    lo = (wte - hi.astype(F32)).astype(BF)

    others = [xor2(zat, pick4([row[i] for row in COLLECT], zat)) for i in range(quads - 1)]
    order = [zat] + others
    place = packed_rows((own, 2 * rows), 1, rows, cap)[2]
    upper = lanes((own, 2 * rows), 1) < rows - 0.5
    e_half, e_block, _ = packed_rows((n, 2 * rows), 1, rows, cap)
    for i, quad in enumerate(order):
        expert = e_block + (quad * PARTS).astype(F32)
        expand = ones(expert == lanes((n, 2 * rows), 0))
        taken = dot(my_v, expand, NN) == place
        both = jnp.where(upper, dot(hi, expand, NN), dot(lo, expand, NN))
        wk[i] = jnp.where(taken, both, 0.0).astype(BF)
    w_out = pltpu.make_async_copy(wk.at[quads - 1], wlast, l_o.at[0])
    w_out.start()

    def p_copy(i, h):
        return remote(
            pout.at[i, h], pin.at[i, h], s_p, r_p.at[i * PIECES + h], (me, o)
        )

    def sc_copy(i):
        return remote(scs.at[i], sci.at[i], s_s, r_s.at[i], (me, o))

    def back_at(quad, j):
        return pl.multiple_of((xor2(zat, quad) - 1) * grp + j * blk, 16)

    def far_copy(quad, j):
        dest = quad * PARTS + j
        at = pl.multiple_of(dest * blk, 16)
        return remote(
            snd2.at[pl.ds(at, blk), :], zol.at[pl.ds(back_at(quad, jat), blk), :],
            s_b, r_b.at[me], (dest, s),
        )

    def last_copy(quad, j):
        dest = quad * PARTS + j
        at = pl.multiple_of(dest * blk, 16)
        to = pl.multiple_of(jat * blk, 16)
        return remote(
            snd2.at[pl.ds(at, blk), :], zlo.at[pl.ds(to, blk), :], s_b, r_b.at[me], (dest, s)
        )

    def last_wait(quad, j):
        src = quad * PARTS + j
        at = pl.multiple_of(src * blk, 16)
        to = pl.multiple_of(j * blk, 16)
        return remote(
            snd2.at[pl.ds(at, blk), :], zlo.at[pl.ds(to, blk), :], s_b, r_b.at[src], (src, s)
        )

    def last_share(quad, j):
        src = quad * PARTS + j
        at = pl.multiple_of(j * blk, 16)
        return remote(
            zlo.at[pl.ds(at, blk), :], zlp.at[pl.ds(at, blk), :], s_g, r_g.at[src // PARTS], (me, o)
        )

    def far_wait(quad, j):
        src = quad * PARTS + j
        at = pl.multiple_of(src * blk, 16)
        return remote(
            snd2.at[pl.ds(at, blk), :], zol.at[pl.ds(back_at(quad, j), blk), :],
            s_b, r_b.at[src], (src, s),
        )

    def h_copy(quad, j):
        src = quad * PARTS + j
        at = back_at(quad, j)
        return remote(
            zol.at[pl.ds(at, blk), :], zpl.at[pl.ds(at, blk), :], s_g, r_g.at[src // PARTS], (me, o)
        )

    def b_copy(dest):
        at = pl.multiple_of(dest * blk, 16)
        to = pl.multiple_of(jat * blk, 16)
        return remote(
            snd2.at[pl.ds(at, blk), :], zo.at[pl.ds(to, blk), :], s_b, r_b.at[me], (dest, s)
        )

    def b_wait(j):
        src = zat * PARTS + j
        at = pl.multiple_of(src * blk, 16)
        to = pl.multiple_of(j * blk, 16)
        return remote(
            snd2.at[pl.ds(at, blk), :], zo.at[pl.ds(to, blk), :], s_b, r_b.at[src], (src, s)
        )

    def g_copy(j):
        src = zat * PARTS + j
        at = pl.multiple_of(j * blk, 16)
        return remote(
            zo.at[pl.ds(at, blk), :], zp.at[pl.ds(at, blk), :], s_g, r_g.at[src // PARTS], (me, o)
        )

    def own_back():
        at = pl.multiple_of(me * blk, 16)
        to = pl.multiple_of(jat * blk, 16)
        return remote(
            snd2.at[pl.ds(at, blk), :], zp.at[pl.ds(to, blk), :], s_g, r_g.at[zat], (me, o)
        )

    def c_copy(dest):
        return remote(sco.at[dest], scr.at[me], s_c, r_c, (dest, s))

    c_rows = pl.ds(0, n - 1)
    c_all = remote(sco.at[c_rows], scr.at[c_rows], s_c, r_c, (me, o))

    def work(i, carry):
        quad = quad_in(WORK, zat, i)
        packed = pl.ds(pl.multiple_of(quad * grp, 16), grp)
        slot_at = pl.ds(pl.multiple_of(quad * rows, 16), rows)
        for j in peers:
            src = quad * PARTS + j

            @pl.when(src != me)
            def _():
                d_wait(src).wait_recv()
                f_copy(src).start()

        @pl.when(i == 0)
        def _():
            loads[0].wait()

        perm = perm_ref[...]

        def contract(got, start):
            total = jnp.zeros((rows, hidden), F32)
            for q in range(0, PARTS, 2):
                x = jnp.concatenate([got[p * rows : (p + 1) * rows] for p in (q, q + 1)], axis=1)
                cols = pl.ds(pl.multiple_of(start + q * qw, 128), 2 * qw)
                total = total + dot(x, wd[:, cols], NT)
            return total

        grad = contract(dot(perm, rxo[packed, :], NN).astype(BF), base)
        f_all(quad).wait_recv()
        grad = grad + contract(dot(perm, rxp[packed, :], NN).astype(BF), obase)
        active, slope = silu_parts(gp_ref[slot_at, :].astype(F32))
        up = up_ref[slot_at, :].astype(F32)
        ud_v = grad * active
        diffs = jnp.concatenate([(grad * up * slope).astype(BF), ud_v.astype(BF)], axis=1)
        score = jnp.sum(ud_v * up, axis=1, keepdims=True)
        scs[i] = jnp.broadcast_to(score, (rows, 128)).astype(BF)
        sc_copy(i).start()

        @pl.when(i == 0)
        def _():
            loads[1].wait()
            loads[2].wait()

        def part(start):
            at = pl.ds(pl.multiple_of(start, 128), pw)
            return dot(diffs, wgu[at, :], NT).astype(BF)

        for h in range(PIECES):
            pout[i, h] = part(obase + h * pw)
            p_copy(i, h).start()
        kept = []
        for h in range(PIECES):
            value = part(base + h * pw).astype(F32)
            p_copy(i, h).wait_recv()
            value = (value + pin[i, h].astype(F32)).astype(BF)
            kept += [value[:, at : at + qw] for at in range(0, pw, qw)]
        snd2[packed, :] = dot(perm, jnp.concatenate(kept, axis=0), NN).astype(BF)
        sc_copy(i).wait_recv()
        total = (scs[i].astype(F32) + sci[i].astype(F32)).astype(BF)
        spot = packed_rows((rows, 128), 0, rows, cap)[2]
        spread = jnp.where(spot == lanes((rows, 128), 1), total.astype(F32), 0.0).astype(BF)
        block = packed_rows((8, rows), 1, rows, cap)[1]
        table = dot(ones(block == lanes((8, rows), 0)), spread, NN)
        for j in range(PARTS):
            sco[quad * PARTS + j] = table[j : j + 1]
        for j in peers:
            dest = quad * PARTS + j

            @pl.when(dest != me)
            def _():
                c_copy(dest).start()

        for j in peers:
            dest = quad * PARTS + j

            @pl.when(dest != me)
            def _():
                @pl.when(quad == zat)
                def _():
                    b_copy(dest).start()

                to_last = xor2(zat, quad) == pick4([row[-1] for row in COLLECT], quad)

                @pl.when((quad != zat) & to_last)
                def _():
                    last_copy(quad, j).start()

                @pl.when((quad != zat) & jnp.logical_not(to_last))
                def _():
                    far_copy(quad, j).start()

            @pl.when(dest == me)
            def _():
                here = pl.ds(pl.multiple_of(me * blk, 16), blk)
                zo[pl.ds(pl.multiple_of(jat * blk, 16), blk), :] = snd2[here, :]
                own_back().start()
                scr[me] = sco[me]

        return carry

    lax.fori_loop(0, quads, work, 0)

    def add(i, h, z, at):
        got = dot(perm_ref[...], z[at, :], NN).astype(BF)
        for q in range(PARTS):
            part = got[q * rows : (q + 1) * rows]
            value = dot(wk[i], jnp.concatenate([part, part], axis=0), NN)
            cols = slice(q * qw, (q + 1) * qw)
            acc[h, :, cols] = value if i == 0 else acc[h, :, cols] + value

    whole = pl.ds(0, grp)
    for j in peers[1:]:
        b_wait(j).wait_recv()
        g_copy(j).start()
    add(0, 0, zo, whole)
    remote(zo, zp, s_g, r_g.at[zat], (me, o)).wait_recv()
    add(0, 1, zp, whole)
    for i, quad in enumerate(others[:-1]):
        at = pl.ds(back_at(quad, 0), grp)
        for j in peers:
            far_wait(quad, j).wait_recv()
            h_copy(quad, j).start()
        add(i + 1, 0, zol, at)
        remote(zol.at[at, :], zpl.at[at, :], s_g, r_g.at[quad], (me, o)).wait_recv()
        add(i + 1, 1, zpl, at)
    a_out = pltpu.make_async_copy(acc, acc_out, l_a)
    a_out.start()

    most = pl.ds(0, (n - 1) * blk)
    remote(snd.at[most, :], rxo.at[most, :], s_d, r_d.at[me], (me, o)).wait_send()
    remote(rxo, rxp, s_f, r_f.at[zat], (me, o)).wait_send()
    tok_all.wait_send()
    remote(scs, sci, s_s, r_s.at[0], (me, o)).wait_send()
    remote(pout, pin, s_p, r_p.at[0], (me, o)).wait_send()
    w_out.wait()

    c_all.wait_recv()
    scores = scr[...].reshape(n, 128).astype(BF)
    slot_of = vbuf[pl.ds(mine, own), :]
    found = jnp.zeros((own, 128), F32)
    for k in range(ids_ref.shape[0]):
        mask = my_ids[:, k : k + 1] == my_lane
        at = jnp.sum(jnp.where(mask, slot_of, 0.0), axis=1, keepdims=True)
        picked = jnp.where(lanes((own, 128), 1) == at, dot(ones(mask), scores, NN), 0.0)
        found = jnp.where(lanes((own, 128), 1) == k, jnp.sum(picked, axis=1, keepdims=True), found)
    gbuf[...] = jnp.transpose(found)[: gbuf.shape[0]]
    g_out = pltpu.make_async_copy(gbuf, wgrad, l_o.at[1])
    g_out.start()

    for j in peers:
        last_wait(others[-1], j).wait_recv()
        last_share(others[-1], j).start()

    remote(snd2.at[most, :], rxo.at[most, :], s_b, r_b.at[me], (me, o)).wait_send()
    c_all.wait_send()
    a_out.wait()
    g_out.wait()
    remote(zlo, zlp, s_g, r_g.at[others[-1]], (me, o)).wait_recv()
    remote(rxo, rxp, s_g, r_g.at[zat], (me, o)).wait_send()


def finish_kernel(cap, zlo, zlp, acc, w_ref, g_ref, out, gout, ob, gb, s_out, s_g):
    s = lax.axis_index("seq")
    own = out.shape[0]
    half = out.shape[1] // 2
    qw = half // PARTS
    blk = PARTS * cap
    grp = PARTS * blk
    rows = PARTS * cap
    gb[...] = g_ref[...].astype(BF)
    g_copy = pltpu.make_async_copy(gb, gout, s_g)
    g_copy.start()
    perm = permutation(grp, blk, cap)
    stores = []
    for h, far in enumerate((zlo, zlp)):
        start = s * half if h == 0 else (1 - s) * half
        got = dot(perm, far[...], NN).astype(BF)
        for q in range(PARTS):
            part = got[q * rows : (q + 1) * rows]
            value = dot(w_ref[...], jnp.concatenate([part, part], axis=0), NN)
            ob[h, q] = (acc[h, :, q * qw : (q + 1) * qw] + value).astype(BF)
            copy = pltpu.make_async_copy(
                ob.at[h, q], out.at[:, pl.ds(pl.multiple_of(start + q * qw, 128), qw)],
                s_out.at[h * PARTS + q],
            )
            copy.start()
            stores.append(copy)
    g_copy.wait()
    for copy in stores:
        copy.wait()


def scratch(n, cap, own, width, hidden, topk):
    half = width // 2
    slots = n * cap
    big = PARTS * slots
    qw = half // PARTS
    quads = n // PARTS
    rows = PARTS * cap
    grp = PARTS * rows
    vm, dma = pltpu.VMEM, pltpu.SemaphoreType.DMA
    pw = half // PIECES
    return [
        vm((topk, 2 * own), jnp.int32), vm((topk, 2 * own), F32), vm((slots, hidden), BF), vm((slots, hidden), BF),
        vm((width, 2 * hidden), BF), vm((hidden, width), BF),
        vm((PARTS * 2 * own, qw), BF), vm((big, PARTS * 2 * own), BF), vm((big, qw), BF),
        vm((big, qw), BF), vm((big, qw), BF),
        vm((quads, PIECES, rows, pw), BF), vm((quads, PIECES, rows, pw), BF), vm((big, qw), BF),
        vm((grp, qw), BF), vm((grp, qw), BF), vm(((quads - 1) * grp, qw), BF), vm(((quads - 1) * grp, qw), BF),
        vm((2 * own, n), F32), vm((quads, own, 2 * rows), BF), vm((2, own, half), F32), vm((topk, own), F32),
        vm((quads, rows, 128), BF), vm((quads, rows, 128), BF), vm((n, 1, 128), F32),
        vm((n, 1, 128), F32), vm((grp, grp), BF),
        dma((4,)), dma, dma, dma, dma((3,)),
        dma, dma((n,)), dma, dma((quads,)), dma, dma((quads * PIECES,)), dma, dma((quads,)),
        dma, dma((n,)), dma, dma, dma, dma((quads,)), dma((2,)), dma,
    ]


def kernel_fits(n, cap, own, width, hidden):
    half = width // 2
    slots = n * cap
    size = 2 * (3 * width * hidden + 10 * slots * half + 4 * own * half)
    aligned = (PARTS * cap) % 16 == 0 and half % (PARTS * 128) == 0 and half % 512 == 0
    return n == PARTS * 4 and cap <= 16 and aligned and own == 128 and size < 48 * 2**20


def on_device(out_grad, route_ids, route_weights, gate_pre, up_pre, w_gate, w_up, w_down):
    n = lax.axis_size("expert")
    own, width = out_grad.shape
    slots, hidden = gate_pre.shape[1:]
    cap = slots // n
    topk = route_ids.shape[1]
    args = (out_grad, route_ids, route_weights, gate_pre, up_pre, w_gate, w_up, w_down)
    if not kernel_fits(n, cap, own, width, hidden):
        return on_device_xla(*args)
    half = width // 2
    qw = half // PARTS
    rows = PARTS * cap
    grp = PARTS * rows
    quads = n // PARTS
    anywhere = pl.BlockSpec(memory_space=pl.ANY)
    hbm = pl.BlockSpec(memory_space=pltpu.HBM)
    vmem = pl.BlockSpec(memory_space=pltpu.VMEM)
    operands = [
        pltpu.with_memory_space_constraint(x, pltpu.HBM)
        for x in (
            out_grad, route_ids.T, route_weights.T, gate_pre[0], up_pre[0], w_gate[0], w_up[0], w_down[0]
        )
    ]
    zlo, zlp, acc, wlast, wgrad = pl.pallas_call(
        functools.partial(step_kernel, n, cap),
        out_shape=(
            jax.ShapeDtypeStruct((grp, qw), BF),
            jax.ShapeDtypeStruct((grp, qw), BF),
            jax.ShapeDtypeStruct((2, own, half), F32),
            jax.ShapeDtypeStruct((own, 2 * rows), BF),
            jax.ShapeDtypeStruct((topk, own), F32),
        ),
        in_specs=[hbm] * 8,
        out_specs=(anywhere,) * 5,
        scratch_shapes=scratch(n, cap, own, width, hidden, topk),
        compiler_params=pltpu.CompilerParams(
            collective_id=0, has_side_effects=True, vmem_limit_bytes=VMEM1 * 2**20
        ),
        name="expert_step",
    )(
        *operands
    )
    in_grad, weight_grad = pl.pallas_call(
        functools.partial(finish_kernel, cap),
        out_shape=(
            jax.ShapeDtypeStruct((own, width), BF),
            jax.ShapeDtypeStruct((topk, own), BF),
        ),
        in_specs=[vmem] * 5,
        out_specs=(anywhere, anywhere),
        scratch_shapes=[
            pltpu.VMEM((2, PARTS, own, qw), BF), pltpu.VMEM((topk, own), BF),
            pltpu.SemaphoreType.DMA((2 * PARTS,)), pltpu.SemaphoreType.DMA,
        ],
        compiler_params=pltpu.CompilerParams(vmem_limit_bytes=VMEM2 * 2**20),
        name="combine",
    )(zlo, zlp, acc, wlast, wgrad)
    return in_grad, weight_grad.T


def solution(mesh):
    in_specs = (
        P(("expert", "seq"), None),
        P("expert", None),
        P("expert", None),
        P("expert", None, "seq"),
        P("expert", None, "seq"),
        P("expert", None, "seq"),
        P("expert", None, "seq"),
        P("expert", "seq", None),
    )
    out_specs = (P(("expert", "seq"), None), P(("expert", "seq"), None))
    return jax.shard_map(
        on_device, mesh=mesh, in_specs=in_specs, out_specs=out_specs, check_vma=False
    )
```
